256 devices in a mesh: tensor: 4 (over x), expert: 64 (over z, y, core).
Axes of the slice: x: 4, y: 4, z: 8, core: 2. Of those that a mesh axis runs over, the one named last changes fastest.
Arguments:
- attn_out: bfloat16 [8192, 2048], P('expert', 'tensor'), may hold values from -6 to 6
- out_proj: bfloat16 [2048, 2048], P('tensor'), may hold values from -0.125 to 0.125
- hidden_in: bfloat16 [8192, 2048], P('expert')
- norm_gain: bfloat16 [2048], replicated, may hold values from 0.099609375 to 1.8984375
- router: bfloat16 [2048, 64], replicated, may hold values from -0.0625 to 0.0625
- routes: int32 [8192, 8], P('expert'), may hold values from 0 to 63, all different within a row; in each aligned block of 128 rows (0 to 127, 128 to 255, ...) at most 32 rows name the same one
- w_gate: bfloat16 [64, 2048, 1024], P('expert', None, 'tensor'), may hold values from -0.25 to 0.25
- w_up: bfloat16 [64, 2048, 1024], P('expert', None, 'tensor'), may hold values from -0.25 to 0.25
- w_down: bfloat16 [64, 1024, 2048], P('expert', 'tensor'), may hold values from -0.375 to 0.375
- final_gain: bfloat16 [2048], P('tensor'), may hold values from 0.099609375 to 1.8984375
- source: int32 [8192], P('expert'), may hold values from 0 to 8191, as said below
Outputs:
- mixed: bfloat16 [8192, 2048], P('expert', 'tensor')
The draws below stay inside these ranges and needn't reach their ends.
Inputs may be any that keep to these rules, and one draw needn't show every extreme that they name: `routes`: each row names 8 different experts. In each aligned block of 128 rows no expert is named by more than 32 rows, a bound that some block reaches. source is a permutation. Each aligned block of 128 requests takes exactly 2 rows from each aligned block of 128 rows.
All inputs are finite; a program needn't handle non-finite values.
Results may differ from the reference program's by a relative error of at most 0.007.
Values may be sent and summed in bfloat16 or wider, within the bound.
A program may use at most 128 MiB of HBM per device.

```python
import math
import jax
import jax.numpy as jnp
import numpy as np
from jax import lax

D = 2048
FF = 1024
HEADS = 16
HEAD_DIM = 128
TOPK = 8
ROWS_DEV = 128
EXPERTS = 64
ROWS = 8192
CAP = 32
PEER_ROWS = 2


def draw_hidden_in(key, part):
    key_columns, key_rows, key_entries = jax.random.split(key, 3)
    feature = jnp.arange(D, dtype=jnp.float32) / D
    column = 0.3 * 10.0 ** (0.8 * feature + 0.3 * jax.random.uniform(key_columns, (D,), jnp.float32))
    row_scale = jnp.exp(jax.random.uniform(key_rows, (ROWS, 1), jnp.float32, math.log(0.3), math.log(3.0)))
    entries = jax.random.truncated_normal(key_entries, -4.0, 4.0, (ROWS, D), jnp.float32)
    return (entries * row_scale * column[None, :]).astype(jnp.bfloat16)


def draw_source(key, part):
    blocks = ROWS // ROWS_DEV
    key_send, key_land = jax.random.split(jax.random.fold_in(key, 7))
    send_perm = jax.vmap(lambda one_key: jax.random.permutation(one_key, ROWS_DEV))(jax.random.split(key_send, blocks)).astype(jnp.int32)
    land_perm = jax.vmap(lambda one_key: jax.random.permutation(one_key, ROWS_DEV))(jax.random.split(key_land, blocks)).astype(jnp.int32)
    target = send_perm // PEER_ROWS
    within = send_perm % PEER_ROWS
    anchor = jnp.arange(blocks, dtype=jnp.int32)[:, None]
    landing = land_perm[target, anchor * PEER_ROWS + within]
    forward = (target * ROWS_DEV + landing).reshape(ROWS).astype(jnp.int32)
    return jnp.zeros((ROWS,), jnp.int32).at[forward].set(jnp.arange(ROWS, dtype=jnp.int32))


def block_scale(own_key, shape, cuts, smallest, high):
    level, own = 1.0, jax.random.fold_in(own_key, 6)
    for axis_at, blocks in cuts:
        steps = jnp.exp(jax.random.uniform(jax.random.fold_in(own, axis_at), (blocks,), jnp.float32, smallest / len(cuts), high / len(cuts)))
        level = level * jnp.repeat(steps, shape[axis_at] // blocks).reshape([-1 if axis == axis_at else 1 for axis in range(len(shape))])
    return level


def assign_block(key, own, number, rows, amount, top, bound, slope):
    ranking = jax.random.permutation(key, amount)
    heavy_load, common = shares(amount, rows * top, bound, slope, True), shares(amount, rows * top, bound, slope, False)
    places = jnp.arange(amount)

    def named(lengths, offset_by):
        used = int((lengths > 0).sum())
        fixed = max(1, used // 4)
        moved = fixed + (places - fixed + offset_by * (used - fixed)) % max(1, amount - fixed)
        return jnp.zeros((amount,), jnp.int32).at[ranking[jnp.where(places < fixed, places, moved)]].set(jnp.asarray(lengths, jnp.int32))

    lengths = jnp.where(number % 4 == 0, named(heavy_load, number // 4), named(common, number - number // 4 - 1))
    mixed = jax.random.permutation(jax.random.fold_in(own, 3), amount)
    source_of, sink = mixed[0:amount // 2 * 2:2], mixed[1:amount // 2 * 2:2]
    slack = jnp.minimum(lengths[source_of] - 1, bound - lengths[sink]) // 2
    slack = jnp.where((source_of == ranking[0]) | (sink == ranking[0]) | (lengths[sink] == 0), 0, jnp.maximum(slack, 0))
    moved = jax.random.randint(jax.random.fold_in(own, 4), (amount // 2,), 0, 1 << 20) % (slack + 1)
    lengths = lengths.at[source_of].add(-moved).at[sink].add(moved)
    labels = jnp.searchsorted(jnp.cumsum(lengths), jnp.arange(rows * top), side="right").astype(jnp.int32)
    listing = labels.reshape(top, rows).T
    listing = listing[jax.random.permutation(jax.random.fold_in(own, 1), rows)]
    offset_by = jax.random.randint(jax.random.fold_in(own, 2), (rows, 1), 0, top)
    return jnp.take_along_axis(listing, (jnp.arange(top)[None, :] + offset_by) % top, axis=1)


def shares(number_of, total, most, lean, full):
    loads = [(1 << 20) // math.isqrt(grade ** lean) + 1 for grade in range(1, number_of + 1)]
    largest = most if full else min(most, max(-(-total // number_of), total * loads[0] // sum(loads)))
    least = 1 if total - largest >= number_of - 1 else 0
    holding, surplus = [largest] + [least] * (number_of - 1), total - largest - least * (number_of - 1)
    while surplus > 0:
        candidates = [i for i in range(1, number_of) if holding[i] < largest] or [i for i in range(1, number_of) if holding[i] < most]
        whole, remaining = sum([loads[i] for i in candidates]), surplus
        for i in candidates:
            more = min(most - holding[i], max(1, remaining * loads[i] // whole), surplus)
            holding[i] = holding[i] + more
            surplus = surplus - more
    return np.array(holding)


def bell_draw(key, shape, scale, bound, shards=(), held_as=jnp.bfloat16):
    values = jax.random.normal(key, shape, jnp.float32) * scale
    if len(shards) > 0:
        values = block_scale(key, shape, shards, -0.22, 0.18) * values
    return jnp.clip(values, min=-bound, max=bound).astype(held_as)


def setup_inputs(seed: int = 0) -> dict:
    seeds = jax.random.split(jax.random.key(seed), 12)
    attn_out = bell_draw(seeds[0], (ROWS, HEADS * HEAD_DIM), 1.0, 6.0, ((0, 64), (1, 4)))
    out_proj = bell_draw(seeds[1], (HEADS * HEAD_DIM, D), (HEADS * HEAD_DIM) ** -0.5, 0.125, ((0, 4),))
    hidden_in = draw_hidden_in(jax.random.fold_in(seeds[11], 71), 0)
    norm_gain = jnp.clip(1.0 + 0.18 * jax.random.normal(seeds[3], (D,), jnp.float32), 0.099609375, 1.8984375).astype(jnp.bfloat16)
    router = bell_draw(seeds[4], (D, EXPERTS), (5 * D) ** -0.5, 0.0625)
    routes_keys = jax.random.split(jax.random.fold_in(seeds[5], 1), ROWS // ROWS_DEV)
    routes_turns = jax.random.permutation(jax.random.fold_in(seeds[5], 3), ROWS // ROWS_DEV)
    routes = jax.vmap(lambda own, number: assign_block(jax.random.fold_in(seeds[5], 2), own, number, ROWS_DEV, EXPERTS, TOPK, CAP, 2))(routes_keys, routes_turns).reshape((ROWS, TOPK))
    w_gate = bell_draw(seeds[6], (EXPERTS, D, FF), (D // 4) ** -0.5, 0.25, ((0, 64), (2, 4)))
    w_up = bell_draw(seeds[7], (EXPERTS, D, FF), (D // 4) ** -0.5, 0.25, ((0, 64), (2, 4)))
    w_down = bell_draw(seeds[8], (EXPERTS, FF, D), (FF // 4) ** -0.5, 0.375, ((0, 64), (1, 4)))
    final_gain = jnp.clip(1.0 + 0.18 * jax.random.normal(seeds[9], (D,), jnp.float32), 0.099609375, 1.8984375).astype(jnp.bfloat16)
    source = draw_source(jax.random.fold_in(seeds[11], 71), 0)
    return dict(attn_out=attn_out, out_proj=out_proj, hidden_in=hidden_in, norm_gain=norm_gain, router=router, routes=routes, w_gate=w_gate, w_up=w_up, w_down=w_down, final_gain=final_gain, source=source)


epsilon = 1e-06

def rms_normalize(values, gain):
    floats = values.astype(jnp.float32)
    inverse_rms = lax.rsqrt(lax.optimization_barrier(jnp.mean(floats * floats, axis=-1, keepdims=True)) + epsilon)
    return floats * inverse_rms * gain.astype(jnp.float32)

def reference(attn_out, out_proj, hidden_in, norm_gain, router, routes, w_gate, w_up, w_down, final_gain, source):
    attention = jnp.dot(attn_out, out_proj, preferred_element_type=jnp.float32)
    residual = (hidden_in.astype(jnp.float32) + attention).astype(jnp.bfloat16)
    normed = rms_normalize(residual, norm_gain).astype(jnp.bfloat16)
    logits = jnp.dot(normed, router, preferred_element_type=jnp.float32)
    chosen = jnp.take_along_axis(logits, routes, axis=1)
    powers = jnp.exp(chosen)
    gate_weights = powers / lax.optimization_barrier(jnp.sum(powers, axis=1, keepdims=True))
    pair_count = ROWS * TOPK
    flat_expert = routes.reshape(pair_count).astype(jnp.int32)
    flat_row = (jnp.arange(pair_count, dtype=jnp.int32) // TOPK).astype(jnp.int32)
    flat_gate = gate_weights.reshape(pair_count)
    ordering = jnp.argsort(flat_expert, stable=True).astype(jnp.int32)
    sorted_rows = flat_row[ordering]
    sorted_gates = flat_gate[ordering]
    expert_ids = jnp.arange(EXPERTS, dtype=jnp.int32)
    per_expert = lax.optimization_barrier(jnp.sum((flat_expert[:, None] == expert_ids[None, :]).astype(jnp.int32), axis=0)).astype(jnp.int32)
    begins = (jnp.cumsum(per_expert) - per_expert).astype(jnp.int32)
    longest = ROWS // ROWS_DEV * CAP
    padded_rows = jnp.concatenate([sorted_rows, jnp.zeros((longest,), jnp.int32)])
    padded_gates = jnp.concatenate([sorted_gates, jnp.zeros((longest,), jnp.float32)])

    def one_expert(carry, expert_id):
        begin_at = begins[expert_id]
        row_index = lax.dynamic_slice(padded_rows, (begin_at,), (longest,)).astype(jnp.int32)
        weights = lax.dynamic_slice(padded_gates, (begin_at,), (longest,))
        live = jnp.arange(longest, dtype=jnp.int32) < per_expert[expert_id]
        row_block = normed[row_index]
        gate_part = jnp.dot(row_block, w_gate[expert_id], preferred_element_type=jnp.float32)
        up_part = jnp.dot(row_block, w_up[expert_id], preferred_element_type=jnp.float32)
        activated = (jax.nn.silu(gate_part) * up_part).astype(jnp.bfloat16)
        expert_rows = jnp.dot(activated, w_down[expert_id], preferred_element_type=jnp.float32)
        scaled = jnp.where(live, weights, jnp.zeros_like(weights))[:, None] * expert_rows
        return (carry.at[row_index].add(scaled), None)
    mixture, unused = lax.scan(one_expert, jnp.zeros((ROWS, D), jnp.float32), expert_ids)
    total = residual.astype(jnp.float32) + mixture
    normalized = rms_normalize(total, final_gain).astype(jnp.bfloat16)
    return normalized[source]
```

```python
import jax
import jax.numpy as jnp
from jax import lax
from jax.sharding import PartitionSpec as P

epsilon = 1e-06


def rms_normalize(values, gain):
    floats = values.astype(jnp.float32)
    inverse_rms = lax.rsqrt(jnp.mean(floats * floats, axis=-1, keepdims=True) + epsilon)
    return floats * inverse_rms * gain.astype(jnp.float32)


def on_device(
    attn_out,
    out_proj,
    hidden_in,
    norm_gain,
    router,
    routes,
    w_gate,
    w_up,
    w_down,
    final_gain,
    source,
):
    rows_dev, model_width = hidden_in.shape
    tensor_count = lax.axis_size("tensor")
    peer_count = lax.axis_size("expert")
    experts = peer_count
    top_count = routes.shape[1]
    capacity = min(rows_dev, 2 * rows_dev * top_count // experts)
    slots = capacity // tensor_count
    peer_rows = rows_dev // peer_count
    feature_share = model_width // tensor_count
    plane = lax.axis_index("tensor")
    feature_first = plane * feature_share
    needed_block = source // rows_dev
    needed_local = source % rows_dev

    same = needed_block[:, None] == needed_block[None, :]
    earlier = jnp.arange(rows_dev)[None, :] < jnp.arange(rows_dev)[:, None]
    turn = jnp.sum((same & earlier).astype(jnp.int32), axis=1)
    place = needed_block * peer_rows + turn
    places = place[:, None] == jnp.arange(rows_dev)[None, :]
    wanted = jnp.sum(jnp.where(places, needed_local[:, None], 0), axis=0).reshape(
        peer_count, peer_rows
    )
    asked = lax.all_to_all(wanted, "expert", split_axis=0, concat_axis=0, tiled=True)

    gate_all = lax.all_gather(w_gate[0], "tensor")
    up_all = lax.all_gather(w_up[0], "tensor")
    down_all = lax.all_gather(w_down[0], "tensor")

    head_term = jnp.dot(attn_out, out_proj, preferred_element_type=jnp.float32)
    attention = lax.psum(head_term, "tensor")
    residual = (hidden_in.astype(jnp.float32) + attention).astype(jnp.bfloat16)
    normed = rms_normalize(residual, norm_gain).astype(jnp.bfloat16)
    logits = jnp.dot(normed, router, preferred_element_type=jnp.float32)

    named = jnp.any(routes[:, :, None] == jnp.arange(experts)[None, None, :], axis=1)
    powers = jnp.where(named, jnp.exp(logits), 0.0)
    gate_weights = powers / jnp.sum(powers, axis=1, keepdims=True)
    before = (jnp.arange(rows_dev)[None, :] < jnp.arange(rows_dev)[:, None]).astype(jnp.bfloat16)
    rank = jnp.dot(before, named.astype(jnp.bfloat16), preferred_element_type=jnp.float32)
    rank = rank.astype(jnp.int32) - plane * slots
    taken = named[:, :, None] & (rank[:, :, None] == jnp.arange(slots)[None, None, :])
    taken = taken.reshape(rows_dev, experts * slots)
    outgoing = lax.dot_general(
        taken.astype(jnp.bfloat16),
        normed,
        (((0,), (0,)), ((), ())),
        preferred_element_type=jnp.float32,
    ).astype(jnp.bfloat16)
    outgoing = outgoing.reshape(peer_count, slots, model_width)
    incoming = lax.all_to_all(outgoing, "expert", split_axis=0, concat_axis=0, tiled=True)
    row_block = incoming.reshape(peer_count * slots, model_width)

    gate_part = jnp.einsum("sd,qdf->sqf", row_block, gate_all, preferred_element_type=jnp.float32)
    up_part = jnp.einsum("sd,qdf->sqf", row_block, up_all, preferred_element_type=jnp.float32)
    activated = (jax.nn.silu(gate_part) * up_part).astype(jnp.bfloat16)
    expert_rows = jnp.einsum(
        "sqf,qfd->sd", activated, down_all, preferred_element_type=jnp.float32
    ).astype(jnp.bfloat16)
    returned = lax.all_to_all(
        expert_rows.reshape(peer_count, slots, model_width),
        "expert",
        split_axis=0,
        concat_axis=0,
        tiled=True,
    ).reshape(peer_count * slots, model_width)

    spread = jnp.where(taken, jnp.repeat(gate_weights, slots, axis=1), 0.0)
    spread_high = spread.astype(jnp.bfloat16)
    spread_low = (spread - spread_high.astype(jnp.float32)).astype(jnp.bfloat16)
    mixture = jnp.dot(spread_high, returned, preferred_element_type=jnp.float32) + jnp.dot(
        spread_low, returned, preferred_element_type=jnp.float32
    )
    mixture = lax.psum_scatter(mixture, "tensor", scatter_dimension=1, tiled=True)
    residual_mine = lax.dynamic_slice_in_dim(residual, feature_first, feature_share, 1)
    total_mine = residual_mine.astype(jnp.float32) + mixture
    squares = lax.psum(jnp.sum(total_mine * total_mine, axis=-1), "tensor")
    inverse_rms = lax.rsqrt(squares / model_width + epsilon)[:, None]
    normalized = (total_mine * inverse_rms * final_gain.astype(jnp.float32)).astype(jnp.bfloat16)
    picks = (asked.reshape(rows_dev)[:, None] == jnp.arange(rows_dev)[None, :]).astype(jnp.bfloat16)
    packed = jnp.dot(picks, normalized, preferred_element_type=jnp.float32).astype(jnp.bfloat16)
    arrived = lax.all_to_all(
        packed.reshape(peer_count, peer_rows, feature_share),
        "expert",
        split_axis=0,
        concat_axis=0,
        tiled=True,
    ).reshape(rows_dev, feature_share)
    return jnp.dot(
        places.astype(jnp.bfloat16), arrived, preferred_element_type=jnp.float32
    ).astype(jnp.bfloat16)


def solution(mesh):
    placed = (
        P("expert", "tensor"),
        P("tensor", None),
        P("expert", None),
        P(),
        P(),
        P("expert", None),
        P("expert", None, "tensor"),
        P("expert", None, "tensor"),
        P("expert", "tensor", None),
        P("tensor"),
        P("expert"),
    )
    return jax.shard_map(
        on_device, mesh=mesh, in_specs=placed, out_specs=P("expert", "tensor"), check_vma=False
    )
```

```python
import functools

import jax
import jax.numpy as jnp
from jax import lax
from jax.experimental import pallas as pl
from jax.experimental.pallas import tpu as pltpu
from jax.sharding import PartitionSpec as P

epsilon = 1e-06
BF = jnp.bfloat16
F32 = jnp.float32
VMEM = pltpu.VMEM
DMA = pltpu.SemaphoreType.DMA


def dot(a, b):
    return jnp.dot(a, b, preferred_element_type=F32)


def iota(shape, dim):
    return lax.broadcasted_iota(jnp.int32, shape, dim)


def layer(
    planes,
    peers,
    attn_ref,
    proj_ref,
    hidden_ref,
    gain_ref,
    router_ref,
    routes_ref,
    gate_hbm,
    up_hbm,
    down_hbm,
    last_gain_ref,
    source_ref,
    out_ref,
    part,
    att_send,
    att_recv,
    res,
    normed,
    gates,
    ups,
    downs,
    ask_send,
    ask_recv,
    slot_send,
    slot_recv,
    rows_in,
    acts,
    back_send,
    back_recv,
    mix_send,
    mix_recv,
    mix_own,
    total,
    sq_send,
    sq_recv,
    pack_send,
    pack_recv,
    high,
    low,
    own_sem,
    att_s,
    att_r,
    res_s,
    res_r,
    ask_s,
    ask_r,
    slot_s,
    slot_r,
    w_s,
    w_r,
    d_s,
    d_r,
    back_s,
    back_r,
    mix_s,
    mix_r,
    sq_s,
    sq_r,
    pack_s,
    pack_r,
):
    x = lax.axis_index("tensor")
    me = lax.axis_index("expert")
    rows, share = attn_ref.shape
    width = planes * share
    slots = slot_send.shape[1]
    all_slots = peers * slots
    hidden_units = gate_hbm.shape[2]
    right = lax.rem(x + 1, planes)
    left = lax.rem(x + planes - 1, planes)

    def to_plane(src, dst, send, recv, plane):
        return pltpu.make_async_remote_copy(
            src_ref=src, dst_ref=dst, send_sem=send, recv_sem=recv, device_id={"tensor": plane}
        )

    def to_peer(src, dst, send, recv, peer):
        return pltpu.make_async_remote_copy(
            src_ref=src, dst_ref=dst, send_sem=send, recv_sem=recv, device_id={"expert": peer}
        )

    def peer_at(step):
        return lax.rem(me + step, peers)

    own = [
        pltpu.make_async_copy(gate_hbm.at[0], gates.at[0], own_sem.at[0]),
        pltpu.make_async_copy(up_hbm.at[0], ups.at[0], own_sem.at[1]),
    ]
    for j in range(planes):
        own.append(
            pltpu.make_async_copy(
                down_hbm.at[0, :, pl.ds(j * share, share)], downs.at[0, j], own_sem.at[2 + j]
            )
        )
    for copy in own:
        copy.start()

    barrier = pltpu.get_barrier_semaphore()
    for d in range(1, planes):
        pl.semaphore_signal(barrier, inc=1, device_id={"tensor": lax.rem(x + d, planes)})

    @pl.loop(1, peers)
    def _(step):
        pl.semaphore_signal(barrier, inc=1, device_id={"expert": peer_at(step)})

    ask_send[...] = jnp.broadcast_to(source_ref[...], ask_send.shape)
    for j in range(planes):
        part[j] = dot(attn_ref[...], proj_ref[:, j * share : (j + 1) * share])
    for d in range(1, planes):
        att_send[d - 1] = part[lax.rem(x + d, planes)].astype(BF)

    pl.semaphore_wait(barrier, planes - 1 + peers - 1)

    att = [
        to_plane(
            att_send.at[d - 1],
            att_recv.at[d - 1],
            att_s.at[d - 1],
            att_r.at[d - 1],
            lax.rem(x + d, planes),
        )
        for d in range(1, planes)
    ]
    for copy in att:
        copy.start()

    @pl.loop(1, peers)
    def _(step):
        to_peer(ask_send, ask_recv.at[me], ask_s, ask_r, peer_at(step)).start()

    for copy in att:
        copy.wait_recv()
    mine = pl.ds(pl.multiple_of(x * share, share), share)
    attention = part[x]
    for d in range(planes - 1):
        attention = attention + att_recv[d].astype(F32)
    res[x] = (hidden_ref[:, mine].astype(F32) + attention).astype(BF)
    spread_res = [
        to_plane(res.at[x], res.at[x], res_s.at[d - 1], res_r.at[d - 1], lax.rem(x + d, planes))
        for d in range(1, planes)
    ]
    for copy in spread_res:
        copy.start()

    gate_r = to_plane(gate_hbm.at[0], gates.at[1], w_s.at[0], w_r.at[0], right)
    up_r = to_plane(up_hbm.at[0], ups.at[1], w_s.at[1], w_r.at[1], right)
    up_l = to_plane(up_hbm.at[0], ups.at[2], w_s.at[2], w_r.at[2], left)
    gate_l = to_plane(gate_hbm.at[0], gates.at[2], w_s.at[3], w_r.at[3], left)
    gate_on = to_plane(gates.at[1], gates.at[3], w_s.at[4], w_r.at[4], right)
    up_on = to_plane(ups.at[2], ups.at[3], w_s.at[5], w_r.at[5], left)
    gate_r.start()
    up_l.start()
    up_r.start()
    gate_l.start()

    for copy in spread_res:
        copy.wait_recv()
    square = jnp.zeros((rows, 1), F32)
    for j in range(planes):
        floats = res[j].astype(F32)
        square = square + jnp.sum(floats * floats, axis=1, keepdims=True)
    inverse = lax.rsqrt(square / width + epsilon)
    experts = peers
    logits = jnp.zeros((rows, experts), F32)
    for j in range(planes):
        cols = slice(j * share, (j + 1) * share)
        scaled = (res[j].astype(F32) * inverse * gain_ref[:, cols].astype(F32)).astype(BF)
        normed[j] = scaled
        logits = logits + dot(scaled, router_ref[cols, :])
    named = jnp.zeros((rows, experts), jnp.bool_)
    which = iota((rows, experts), 1)
    for k in range(routes_ref.shape[1]):
        named = named | (routes_ref[:, k : k + 1] == which)
    named_f = jnp.where(named, 1.0, 0.0).astype(F32)
    powers = jnp.where(named, jnp.exp(logits), 0.0)
    weights = powers / jnp.sum(powers, axis=1, keepdims=True)
    before = jnp.where(iota((rows, rows), 1) < iota((rows, rows), 0), 1.0, 0.0).astype(BF)
    rank = dot(before, named_f.astype(BF))
    wide = jnp.where(
        iota((experts, all_slots), 1) // slots == iota((experts, all_slots), 0), 1.0, 0.0
    ).astype(BF)
    wide_rank = dot(rank.astype(BF), wide)
    wide_named = dot(named_f.astype(BF), wide)
    turn = (iota((rows, all_slots), 1) % slots + x * slots).astype(F32)
    taken = (wide_named > 0.5) & (wide_rank == turn)
    weights_high = weights.astype(BF)
    weights_low = (weights - weights_high.astype(F32)).astype(BF)
    high[...] = jnp.where(taken, dot(weights_high, wide), 0.0).astype(BF)
    low[...] = jnp.where(taken, dot(weights_low, wide), 0.0).astype(BF)
    pick = jnp.transpose(jnp.where(taken, 1.0, 0.0).astype(F32)).astype(BF)
    for j in range(planes):
        chosen = dot(pick, normed[j]).astype(BF)
        slot_send[:, :, j * share : (j + 1) * share] = chosen.reshape(peers, slots, share)

    @pl.loop(1, peers)
    def _(step):
        peer = peer_at(step)
        to_peer(slot_send.at[peer], slot_recv.at[me], slot_s, slot_r, peer).start()

    own_slot = pltpu.make_async_copy(slot_send.at[me], slot_recv.at[me], own_sem.at[2 + planes])
    own_slot.start()

    gate_r.wait_recv()
    gate_on.start()
    up_l.wait_recv()
    up_on.start()

    half = hidden_units // 2
    down_r, down_l, on_r, on_l = [], [], [], []
    for j in range(planes):
        cols = pl.ds(j * share, share)
        down_r.append(
            to_plane(down_hbm.at[0, :, cols], downs.at[1, j], d_s.at[0, j], d_r.at[0, j], right)
        )
        down_l.append(
            to_plane(down_hbm.at[0, :, cols], downs.at[2, j], d_s.at[1, j], d_r.at[1, j], left)
        )
        top, bottom = pl.ds(0, half), pl.ds(half, half)
        on_r.append(
            to_plane(
                downs.at[1, j, top], downs.at[3, j, top], d_s.at[2, j], d_r.at[2, j], right
            )
        )
        on_l.append(
            to_plane(
                downs.at[2, j, bottom], downs.at[3, j, bottom], d_s.at[3, j], d_r.at[3, j], left
            )
        )
    for j in range(2):
        down_r[j].start()
        down_l[j].start()

    everyone = pl.ds(0, peers - 1)
    to_peer(slot_send.at[everyone], slot_recv.at[everyone], slot_s, slot_r, me).wait_recv()
    own_slot.wait()
    tiles = 4
    tile_peers = peers // tiles
    tile_rows = tile_peers * slots
    for t in range(tiles):
        rows_in[t * tile_rows : (t + 1) * tile_rows] = slot_recv[
            t * tile_peers : (t + 1) * tile_peers
        ].reshape(tile_rows, width)

    def activate(q):
        gate_part = dot(rows_in[...], gates[q])
        up_part = dot(rows_in[...], ups[q])
        acts[q] = (gate_part / (1.0 + jnp.exp(-gate_part)) * up_part).astype(BF)

    own[0].wait()
    own[1].wait()
    activate(0)
    up_r.wait_recv()
    activate(1)
    gate_l.wait_recv()
    activate(2)

    for copy in own[2:]:
        copy.wait()
    down_r[0].wait_recv()
    on_r[0].start()
    down_l[0].wait_recv()
    on_l[0].start()
    for j in range(2, planes):
        down_r[j].start()
        down_l[j].start()

    gate_on.wait_recv()
    up_on.wait_recv()
    activate(3)

    def combine(j):
        to_peer(
            back_send.at[j, everyone], back_recv.at[j, everyone], back_s.at[j], back_r.at[j], me
        ).wait_recv()
        back = back_recv[j].reshape(all_slots, share)
        mixed = dot(high[...], back) + dot(low[...], back)
        mix_send[j] = mixed.astype(BF)

        @pl.when(x == j)
        def _():
            mix_own[...] = mixed

        @pl.when(x != j)
        def _():
            to_plane(mix_send.at[j], mix_recv.at[x], mix_s, mix_r, j).start()

    for j in range(planes):
        if j + 1 < planes:
            down_r[j + 1].wait_recv()
            on_r[j + 1].start()
            down_l[j + 1].wait_recv()
            on_l[j + 1].start()
        on_r[j].wait_recv()
        on_l[j].wait_recv()
        product = dot(acts[0], downs[0, j])
        for q in range(1, planes):
            product = product + dot(acts[q], downs[q, j])
        back_send[j] = product.astype(BF).reshape(peers, slots, share)
        back_recv[j, me] = back_send[j, me]

        @pl.loop(1, peers)
        def _(step):
            peer = peer_at(step)
            to_peer(
                back_send.at[j, peer], back_recv.at[j, me], back_s.at[j], back_r.at[j], peer
            ).start()

        if j >= 1:
            combine(j - 1)
    combine(planes - 1)

    three = pl.ds(0, planes - 1)
    to_plane(mix_send.at[three], mix_recv.at[three], mix_s, mix_r, x).wait_recv()
    whole = mix_own[...] + res[x].astype(F32)
    for j in range(planes):
        whole = whole + jnp.where(x == j, 0.0, mix_recv[j].astype(F32))
    total[...] = whole
    squares = jnp.zeros((rows, 128), F32)
    for c in range(share // 128):
        piece = whole[:, c * 128 : (c + 1) * 128]
        squares = squares + piece * piece
    row_sum = jnp.sum(jnp.transpose(squares), axis=0, keepdims=True)
    sq_send[...] = jnp.broadcast_to(row_sum, sq_send.shape)
    sq = [
        to_plane(sq_send, sq_recv.at[d - 1], sq_s.at[d - 1], sq_r.at[d - 1], lax.rem(x + d, planes))
        for d in range(1, planes)
    ]
    for copy in sq:
        copy.start()

    to_peer(ask_recv.at[everyone], ask_recv.at[everyone], ask_s, ask_r, me).wait_recv()
    ask_recv[me] = ask_send[...]
    asked = ask_recv[...].reshape(peers * 8, rows)
    lanes = iota((peers * 8, rows), 1)
    ours = asked // rows == me
    first = jnp.min(jnp.where(ours, lanes, rows), axis=1, keepdims=True)
    second = jnp.max(jnp.where(ours, lanes, -1), axis=1, keepdims=True)
    line = iota((peers * 8, 1), 0) % 8
    request = jnp.where(line < 4, first, second)
    local = jnp.sum(jnp.where(lanes == request, asked % rows, 0), axis=1, keepdims=True)
    wanted = lanes == local

    for copy in sq:
        copy.wait_recv()
    sums = sq_send[...]
    for d in range(planes - 1):
        sums = sums + sq_recv[d]
    column = jnp.transpose(jnp.broadcast_to(sums[0:1], (rows, rows)))[:, 0:1]
    scale = lax.rsqrt(column / width + epsilon)
    result = (total[...] * scale * last_gain_ref[...].astype(F32)).astype(BF)
    packed = jnp.zeros((peers * 8, 128), F32)
    for c in range(4):
        chooser = jnp.where(wanted & (line % 4 == c), 1.0, 0.0).astype(BF)
        packed = packed + dot(chooser, result[:, c * 128 : (c + 1) * 128])
    pack_send[...] = packed.astype(BF).reshape(peers, 8, 128)
    pack_recv[me] = pack_send[me]

    @pl.loop(1, peers)
    def _(step):
        peer = peer_at(step)
        to_peer(pack_send.at[peer], pack_recv.at[me], pack_s, pack_r, peer).start()

    asks = jnp.broadcast_to(source_ref[...], (rows, rows))
    asks_down = jnp.transpose(asks.astype(F32)).astype(jnp.int32)
    same = (asks // rows == asks_down // rows) & (iota((rows, rows), 1) < iota((rows, rows), 0))
    later = jnp.max(jnp.where(same, 1, 0), axis=1, keepdims=True)
    place = (asks_down[:, 0:1] // rows) * 8 + later * 4
    at = iota((rows, peers * 8), 1)
    to_peer(pack_send.at[everyone], pack_recv.at[everyone], pack_s, pack_r, me).wait_recv()
    landed = pack_recv[...].reshape(peers * 8, 128)
    for c in range(4):
        chooser = jnp.where(at == place + c, 1.0, 0.0).astype(BF)
        out_ref[:, c * 128 : (c + 1) * 128] = dot(chooser, landed).astype(BF)

    for copy in (
        att + spread_res + [gate_r, up_r, up_l, gate_l, gate_on, up_on]
        + down_r + down_l + on_r + on_l + sq
    ):
        copy.wait_send()

    @pl.loop(1, peers)
    def _(step):
        to_peer(ask_send, ask_recv.at[me], ask_s, ask_r, me).wait_send()

    to_peer(slot_send.at[everyone], slot_recv.at[everyone], slot_s, slot_r, me).wait_send()
    for j in range(planes):
        to_peer(
            back_send.at[j, everyone], back_recv.at[j, everyone], back_s.at[j], back_r.at[j], me
        ).wait_send()
    to_plane(mix_send.at[three], mix_recv.at[three], mix_s, mix_r, x).wait_send()
    to_peer(pack_send.at[everyone], pack_recv.at[everyone], pack_s, pack_r, me).wait_send()


def solution(mesh):
    planes, peers = mesh.shape["tensor"], mesh.shape["expert"]

    def on_device(
        attn_out,
        out_proj,
        hidden_in,
        norm_gain,
        router,
        routes,
        w_gate,
        w_up,
        w_down,
        final_gain,
        source,
    ):
        rows, width = hidden_in.shape
        share = width // planes
        top = routes.shape[1]
        slots = min(rows, 2 * rows * top // peers) // planes
        units = w_gate.shape[2]
        local = pl.BlockSpec(memory_space=pltpu.VMEM)
        remote = pl.BlockSpec(memory_space=pl.ANY)
        return pl.pallas_call(
            functools.partial(layer, planes, peers),
            out_shape=jax.ShapeDtypeStruct((rows, share), BF),
            in_specs=[local] * 6 + [remote] * 3 + [local] * 2,
            out_specs=local,
            scratch_shapes=[
                VMEM((planes, rows, share), F32),
                VMEM((planes - 1, rows, share), BF),
                VMEM((planes - 1, rows, share), BF),
                VMEM((planes, rows, share), BF),
                VMEM((planes, rows, share), BF),
                VMEM((planes, width, units), BF),
                VMEM((planes, width, units), BF),
                VMEM((planes, planes, units, share), BF),
                VMEM((8, rows), jnp.int32),
                VMEM((peers, 8, rows), jnp.int32),
                VMEM((peers, slots, width), BF),
                VMEM((peers, slots, width), BF),
                VMEM((peers * slots, width), BF),
                VMEM((planes, peers * slots, units), BF),
                VMEM((planes, peers, slots, share), BF),
                VMEM((planes, peers, slots, share), BF),
                VMEM((planes, rows, share), BF),
                VMEM((planes, rows, share), BF),
                VMEM((rows, share), F32),
                VMEM((rows, share), F32),
                VMEM((8, rows), F32),
                VMEM((planes - 1, 8, rows), F32),
                VMEM((peers, 8, 128), BF),
                VMEM((peers, 8, 128), BF),
                VMEM((rows, peers * slots), BF),
                VMEM((rows, peers * slots), BF),
                DMA((3 + planes,)),
                DMA((planes - 1,)),
                DMA((planes - 1,)),
                DMA((planes - 1,)),
                DMA((planes - 1,)),
                DMA,
                DMA,
                DMA,
                DMA,
                DMA((6,)),
                DMA((6,)),
                DMA((4, planes)),
                DMA((4, planes)),
                DMA((planes,)),
                DMA((planes,)),
                DMA,
                DMA,
                DMA((planes - 1,)),
                DMA((planes - 1,)),
                DMA,
                DMA,
            ],
            compiler_params=pltpu.CompilerParams(
                collective_id=0, has_side_effects=True, vmem_limit_bytes=56 * 1024 * 1024
            ),
        )(
            attn_out,
            out_proj,
            hidden_in,
            norm_gain.reshape(1, width),
            router,
            routes,
            w_gate,
            w_up,
            w_down,
            final_gain.reshape(1, share),
            source.reshape(1, rows),
        )

    placed = (
        P("expert", "tensor"),
        P("tensor", None),
        P("expert", None),
        P(),
        P(),
        P("expert", None),
        P("expert", None, "tensor"),
        P("expert", None, "tensor"),
        P("expert", "tensor", None),
        P("tensor"),
        P("expert"),
    )
    return jax.shard_map(
        on_device, mesh=mesh, in_specs=placed, out_specs=P("expert", "tensor"), check_vma=False
    )
```

```python
import functools

import jax
import jax.numpy as jnp
from jax import lax
from jax.experimental import pallas as pl
from jax.experimental.pallas import tpu as pltpu
from jax.sharding import PartitionSpec as P

epsilon = 1e-06
BF = jnp.bfloat16
F32 = jnp.float32
VMEM = pltpu.VMEM
DMA = pltpu.SemaphoreType.DMA


def dot(a, b):
    return jnp.dot(a, b, preferred_element_type=F32)


def iota(shape, dim):
    return lax.broadcasted_iota(jnp.int32, shape, dim)


def layer(
    planes,
    peers,
    attn_hbm,
    proj_hbm,
    hidden_hbm,
    gain_ref,
    router_hbm,
    routes_hbm,
    gate_hbm,
    up_hbm,
    down_hbm,
    last_gain_ref,
    source_ref,
    out_ref,
    attn_ref,
    proj_ref,
    hidden_ref,
    router_ref,
    routes_ref,
    part,
    far_send,
    far_recv,
    near_send,
    near_recv,
    res,
    normed,
    gates,
    ups,
    downs,
    ask_send,
    ask_recv,
    slot_send,
    slot_recv,
    rows_in,
    acts,
    back_send,
    back_recv,
    mix_send,
    mix_recv,
    mix_own,
    total,
    sq_send,
    sq_recv,
    pack_send,
    pack_recv,
    high,
    low,
    in_sem,
    own_sem,
    att_s,
    att_r,
    res_s,
    res_r,
    ask_s,
    ask_r,
    slot_s,
    slot_r,
    w_s,
    w_r,
    d_s,
    d_r,
    back_s,
    back_r,
    mix_s,
    mix_r,
    sq_s,
    sq_r,
    pack_s,
    pack_r,
):
    x = lax.axis_index("tensor")
    me = lax.axis_index("expert")
    rows, share = attn_hbm.shape
    width = planes * share
    slots = slot_send.shape[1]
    all_slots = peers * slots
    hidden_units = gate_hbm.shape[2]
    right = lax.rem(x + 1, planes)
    left = lax.rem(x + planes - 1, planes)

    def to_plane(src, dst, send, recv, plane):
        return pltpu.make_async_remote_copy(
            src_ref=src, dst_ref=dst, send_sem=send, recv_sem=recv, device_id={"tensor": plane}
        )

    def to_peer(src, dst, send, recv, peer):
        return pltpu.make_async_remote_copy(
            src_ref=src, dst_ref=dst, send_sem=send, recv_sem=recv, device_id={"expert": peer}
        )

    def peer_at(step):
        return lax.rem(me + step, peers)

    barrier = pltpu.get_barrier_semaphore()
    for d in range(1, planes):
        pl.semaphore_signal(barrier, inc=1, device_id={"tensor": lax.rem(x + d, planes)})

    @pl.loop(1, peers)
    def _(step):
        pl.semaphore_signal(barrier, inc=1, device_id={"expert": peer_at(step)})

    inputs = [
        pltpu.make_async_copy(src, dst, in_sem.at[i])
        for i, (src, dst) in enumerate(
            [
                (attn_hbm, attn_ref),
                (proj_hbm, proj_ref),
                (hidden_hbm, hidden_ref),
                (router_hbm, router_ref),
                (routes_hbm, routes_ref),
            ]
        )
    ]
    for copy in inputs:
        copy.start()

    piece = share // planes
    own = [
        pltpu.make_async_copy(gate_hbm.at[0], gates.at[0], own_sem.at[0]),
        pltpu.make_async_copy(up_hbm.at[0], ups.at[0], own_sem.at[1]),
    ]
    for j in range(planes):
        for p in range(planes):
            own.append(
                pltpu.make_async_copy(
                    down_hbm.at[0, :, pl.ds(p * share + j * piece, piece)],
                    downs.at[0, j, :, pl.ds(p * piece, piece)],
                    own_sem.at[2 + j * planes + p],
                )
            )
    for copy in own:
        copy.start()

    ask_send[...] = jnp.broadcast_to(source_ref[...], ask_send.shape)
    inputs[0].wait()
    inputs[1].wait()
    for j in range(planes):
        part[j] = dot(attn_ref[...], proj_ref[:, j * share : (j + 1) * share])
    top, bottom = pl.ds(0, rows // 2), pl.ds(rows // 2, rows // 2)
    far_send[...] = part[lax.rem(x + 2, planes)].astype(BF)

    pl.semaphore_wait(barrier, planes - 1 + peers - 1)

    far = [
        to_plane(far_send.at[top], far_recv.at[0], att_s.at[0], att_r.at[0], right),
        to_plane(far_send.at[bottom], far_recv.at[1], att_s.at[1], att_r.at[1], left),
    ]
    for copy in far:
        copy.start()

    fill = width // 8

    def weights_to(hbm, buffer, slot, at, plane):
        pieces = [
            to_plane(
                hbm.at[0, pl.ds(first, count)],
                buffer.at[slot, pl.ds(first, count)],
                w_s.at[at],
                w_r.at[at],
                plane,
            )
            for first, count in ((0, fill), (fill, fill), (2 * fill, fill), (3 * fill, width - 3 * fill))
        ]
        return pieces, to_plane(hbm.at[0], buffer.at[slot], w_s.at[at], w_r.at[at], plane)

    gate_r_pieces, gate_r = weights_to(gate_hbm, gates, 1, 0, right)
    up_r_pieces, up_r = weights_to(up_hbm, ups, 1, 1, right)
    up_l_pieces, up_l = weights_to(up_hbm, ups, 2, 2, left)
    gate_l_pieces, gate_l = weights_to(gate_hbm, gates, 2, 3, left)
    gate_on = to_plane(gates.at[1], gates.at[3], w_s.at[4], w_r.at[4], right)
    up_on = to_plane(ups.at[2], ups.at[3], w_s.at[5], w_r.at[5], left)
    gate_r_pieces[0].start()
    up_l_pieces[0].start()

    @pl.loop(1, peers)
    def _(step):
        to_peer(ask_send, ask_recv.at[me], ask_s, ask_r, peer_at(step)).start()

    for copy in far:
        copy.wait_recv()
    near_send[0] = part[right].astype(BF)
    near_send[1] = part[left].astype(BF)
    near_send[0, top] = (part[right, top] + far_recv[0].astype(F32)).astype(BF)
    near_send[1, bottom] = (part[left, bottom] + far_recv[1].astype(F32)).astype(BF)
    near = [
        to_plane(near_send.at[0], near_recv.at[0], att_s.at[2], att_r.at[2], right),
        to_plane(near_send.at[1], near_recv.at[1], att_s.at[3], att_r.at[3], left),
    ]
    for copy in near:
        copy.start()
    gate_r_pieces[1].start()
    up_l_pieces[1].start()
    inputs[2].wait()
    inputs[3].wait()
    inputs[4].wait()
    for copy in near:
        copy.wait_recv()
    mine = pl.ds(pl.multiple_of(x * share, share), share)
    attention = part[x] + near_recv[0].astype(F32) + near_recv[1].astype(F32)
    res[x] = (hidden_ref[:, mine].astype(F32) + attention).astype(BF)
    spread_res = [
        to_plane(res.at[x], res.at[x], res_s.at[0], res_r.at[0], right),
        to_plane(res.at[x], res.at[x], res_s.at[1], res_r.at[1], left),
    ]
    for copy in spread_res:
        copy.start()
    gate_r_pieces[2].start()
    up_l_pieces[2].start()
    res_on = [
        to_plane(res.at[left, top], res.at[left, top], res_s.at[2], res_r.at[2], right),
        to_plane(res.at[right, bottom], res.at[right, bottom], res_s.at[3], res_r.at[3], left),
    ]
    for copy, onward in zip(spread_res, res_on):
        copy.wait_recv()
        onward.start()
    gate_r_pieces[3].start()
    up_l_pieces[3].start()
    for copy in up_r_pieces + gate_l_pieces:
        copy.start()

    for copy in res_on:
        copy.wait_recv()
    square = jnp.zeros((rows, 1), F32)
    for j in range(planes):
        floats = res[j].astype(F32)
        square = square + jnp.sum(floats * floats, axis=1, keepdims=True)
    inverse = lax.rsqrt(square / width + epsilon)
    experts = peers
    logits = jnp.zeros((rows, experts), F32)
    for j in range(planes):
        cols = slice(j * share, (j + 1) * share)
        scaled = (res[j].astype(F32) * inverse * gain_ref[cols].astype(F32).reshape(1, share)).astype(BF)
        normed[j] = scaled
        logits = logits + lax.dot_general(
            scaled, router_ref[:, cols], (((1,), (1,)), ((), ())), preferred_element_type=F32
        )
    named = jnp.zeros((rows, experts), jnp.bool_)
    which = iota((rows, experts), 1)
    routed = jnp.transpose(routes_ref[...].astype(F32)).astype(jnp.int32)
    for k in range(routed.shape[1]):
        named = named | (routed[:, k : k + 1] == which)
    named_f = jnp.where(named, 1.0, 0.0).astype(F32)
    powers = jnp.where(named, jnp.exp(logits), 0.0)
    weights = powers / jnp.sum(powers, axis=1, keepdims=True)
    before = jnp.where(iota((rows, rows), 1) < iota((rows, rows), 0), 1.0, 0.0).astype(BF)
    rank = dot(before, named_f.astype(BF))
    wide = jnp.where(
        iota((experts, all_slots), 1) // slots == iota((experts, all_slots), 0), 1.0, 0.0
    ).astype(BF)
    wide_rank = dot(rank.astype(BF), wide)
    wide_named = dot(named_f.astype(BF), wide)
    turn = (iota((rows, all_slots), 1) % slots + x * slots).astype(F32)
    taken = (wide_named > 0.5) & (wide_rank == turn)
    weights_high = weights.astype(BF)
    weights_low = (weights - weights_high.astype(F32)).astype(BF)
    high[...] = jnp.where(taken, dot(weights_high, wide), 0.0).astype(BF)
    low[...] = jnp.where(taken, dot(weights_low, wide), 0.0).astype(BF)
    pick = jnp.transpose(jnp.where(taken, 1.0, 0.0).astype(F32)).astype(BF)
    for j in range(planes):
        chosen = dot(pick, normed[j]).astype(BF)
        slot_send[:, :, j * share : (j + 1) * share] = chosen.reshape(peers, slots, share)

    @pl.loop(1, peers)
    def _(step):
        peer = peer_at(step)
        to_peer(slot_send.at[peer], slot_recv.at[me], slot_s, slot_r, peer).start()

    own_slot = pltpu.make_async_copy(slot_send.at[me], slot_recv.at[me], own_sem.at[2 + planes * planes])
    own_slot.start()

    gate_r.wait_recv()
    gate_on.start()
    up_l.wait_recv()
    up_on.start()

    half = hidden_units // 2
    down_r, down_l, on_r, on_l = [], [], [], []
    for j in range(planes):
        down_r.append(to_plane(downs.at[0, j], downs.at[1, j], d_s.at[0, j], d_r.at[0, j], right))
        down_l.append(to_plane(downs.at[0, j], downs.at[2, j], d_s.at[1, j], d_r.at[1, j], left))
        upper, lower = pl.ds(0, half), pl.ds(half, half)
        on_r.append(
            to_plane(
                downs.at[1, j, upper], downs.at[3, j, upper], d_s.at[2, j], d_r.at[2, j], right
            )
        )
        on_l.append(
            to_plane(
                downs.at[2, j, lower], downs.at[3, j, lower], d_s.at[3, j], d_r.at[3, j], left
            )
        )
    for copy in own[2:]:
        copy.wait()
    for j in range(2):
        down_r[j].start()
        down_l[j].start()

    def pass_down(j):
        down_r[j].wait_recv()
        on_r[j].start()
        down_l[j].wait_recv()
        on_l[j].start()
        if j + 2 < planes:
            down_r[j + 2].start()
            down_l[j + 2].start()

    everyone = pl.ds(0, peers - 1)
    to_peer(slot_send.at[everyone], slot_recv.at[everyone], slot_s, slot_r, me).wait_recv()
    own_slot.wait()
    tiles = 4
    tile_peers = peers // tiles
    tile_rows = tile_peers * slots
    for t in range(tiles):
        rows_in[t * tile_rows : (t + 1) * tile_rows] = slot_recv[
            t * tile_peers : (t + 1) * tile_peers
        ].reshape(tile_rows, width)

    def activate(q):
        gate_part = dot(rows_in[...], gates[q])
        up_part = dot(rows_in[...], ups[q])
        acts[q] = (gate_part / (1.0 + jnp.exp(-gate_part)) * up_part).astype(BF)

    own[0].wait()
    own[1].wait()
    activate(0)
    up_r.wait_recv()
    activate(1)
    gate_l.wait_recv()
    activate(2)

    pass_down(0)
    gate_on.wait_recv()
    up_on.wait_recv()
    activate(3)

    def combine(j):
        to_peer(
            back_send.at[j, everyone], back_recv.at[j, everyone], back_s.at[j], back_r.at[j], me
        ).wait_recv()
        back = back_recv[j].reshape(all_slots, share)
        mixed = dot(high[...], back) + dot(low[...], back)
        for p in range(planes):
            mix_send[j, p] = mixed[:, p * piece : (p + 1) * piece].astype(BF)
            mix_own[p] = mixed[:, p * piece : (p + 1) * piece]
        total[:, j * piece : (j + 1) * piece] = mix_own[x]
        for d in range(1, planes):
            plane = lax.rem(x + d, planes)
            to_plane(mix_send.at[j, plane], mix_recv.at[d - 1, j], mix_s, mix_r, plane).start()

    def produce(j):
        on_r[j].wait_recv()
        on_l[j].wait_recv()
        product = dot(acts[0], downs[0, j])
        for q in range(1, planes):
            product = product + dot(acts[q], downs[q, j])
        back_send[j] = product.astype(BF).reshape(peers, slots, share)
        back_recv[j, me] = back_send[j, me]

        @pl.loop(1, peers)
        def _(step):
            peer = peer_at(step)
            to_peer(
                back_send.at[j, peer], back_recv.at[j, me], back_s.at[j], back_r.at[j], peer
            ).start()

    pass_down(1)
    produce(0)
    pass_down(2)
    produce(1)
    pass_down(3)
    produce(2)
    combine(0)
    produce(3)
    combine(1)
    combine(2)
    combine(3)

    three = pl.ds(0, planes - 1)
    to_plane(mix_recv.at[three], mix_recv.at[three], mix_s, mix_r, x).wait_recv()
    mixture = [total[:, j * piece : (j + 1) * piece] for j in range(planes)]
    for j in range(planes):
        for d in range(planes - 1):
            mixture[j] = mixture[j] + mix_recv[d, j].astype(F32)
    whole = jnp.concatenate(mixture, axis=1) + res[x].astype(F32)
    total[...] = whole
    squares = jnp.zeros((rows, 128), F32)
    for c in range(share // 128):
        part_of = whole[:, c * 128 : (c + 1) * 128]
        squares = squares + part_of * part_of
    row_sum = jnp.sum(jnp.transpose(squares), axis=0, keepdims=True)
    sq_send[...] = jnp.broadcast_to(row_sum, sq_send.shape)
    sq = [
        to_plane(sq_send, sq_recv.at[d - 1], sq_s.at[d - 1], sq_r.at[d - 1], lax.rem(x + d, planes))
        for d in range(1, planes)
    ]
    for copy in sq:
        copy.start()

    to_peer(ask_recv.at[everyone], ask_recv.at[everyone], ask_s, ask_r, me).wait_recv()
    ask_recv[me] = ask_send[...]
    asked = ask_recv[...].reshape(peers * 8, rows)
    lanes = iota((peers * 8, rows), 1)
    ours = asked // rows == me
    first = jnp.min(jnp.where(ours, lanes, rows), axis=1, keepdims=True)
    second = jnp.max(jnp.where(ours, lanes, -1), axis=1, keepdims=True)
    line = iota((peers * 8, 1), 0) % 8
    request = jnp.where(line < 4, first, second)
    local = jnp.sum(jnp.where(lanes == request, asked % rows, 0), axis=1, keepdims=True)
    wanted = lanes == local

    for copy in sq:
        copy.wait_recv()
    sums = sq_send[...]
    for d in range(planes - 1):
        sums = sums + sq_recv[d]
    column = jnp.transpose(jnp.broadcast_to(sums[0:1], (rows, rows)))[:, 0:1]
    scale = lax.rsqrt(column / width + epsilon)
    result = (total[...] * scale * last_gain_ref[...].astype(F32).reshape(1, share)).astype(BF)
    packed = jnp.zeros((peers * 8, 128), F32)
    for c in range(4):
        chooser = jnp.where(wanted & (line % 4 == c), 1.0, 0.0).astype(BF)
        packed = packed + dot(chooser, result[:, c * 128 : (c + 1) * 128])
    pack_send[...] = packed.astype(BF).reshape(peers, 8, 128)
    pack_recv[me] = pack_send[me]

    @pl.loop(1, peers)
    def _(step):
        peer = peer_at(step)
        to_peer(pack_send.at[peer], pack_recv.at[me], pack_s, pack_r, peer).start()

    asks = jnp.broadcast_to(source_ref[...], (rows, rows))
    asks_down = jnp.transpose(asks.astype(F32)).astype(jnp.int32)
    same = (asks // rows == asks_down // rows) & (iota((rows, rows), 1) < iota((rows, rows), 0))
    later = jnp.max(jnp.where(same, 1, 0), axis=1, keepdims=True)
    place = (asks_down[:, 0:1] // rows) * 8 + later * 4
    at = iota((rows, peers * 8), 1)
    to_peer(pack_send.at[everyone], pack_recv.at[everyone], pack_s, pack_r, me).wait_recv()
    landed = pack_recv[...].reshape(peers * 8, 128)
    for c in range(4):
        chooser = jnp.where(at == place + c, 1.0, 0.0).astype(BF)
        out_ref[:, c * 128 : (c + 1) * 128] = dot(chooser, landed).astype(BF)

    for copy in (
        far + near + spread_res + res_on + [gate_r, up_r, up_l, gate_l, gate_on, up_on]
        + down_r + down_l + on_r + on_l + sq
    ):
        copy.wait_send()

    @pl.loop(1, peers)
    def _(step):
        to_peer(ask_send, ask_recv.at[me], ask_s, ask_r, me).wait_send()

    to_peer(slot_send.at[everyone], slot_recv.at[everyone], slot_s, slot_r, me).wait_send()
    for j in range(planes):
        to_peer(
            back_send.at[j, everyone], back_recv.at[j, everyone], back_s.at[j], back_r.at[j], me
        ).wait_send()
    to_plane(mix_send.at[:, three], mix_recv.at[three], mix_s, mix_r, x).wait_send()
    to_peer(pack_send.at[everyone], pack_recv.at[everyone], pack_s, pack_r, me).wait_send()


def solution(mesh):
    planes, peers = mesh.shape["tensor"], mesh.shape["expert"]

    def on_device(
        attn_out,
        out_proj,
        hidden_in,
        norm_gain,
        router,
        routes,
        w_gate,
        w_up,
        w_down,
        final_gain,
        source,
    ):
        rows, width = hidden_in.shape
        share = width // planes
        top = routes.shape[1]
        slots = min(rows, 2 * rows * top // peers) // planes
        units = w_gate.shape[2]
        local = pl.BlockSpec(memory_space=pltpu.VMEM)
        remote = pl.BlockSpec(memory_space=pl.ANY)
        return pl.pallas_call(
            functools.partial(layer, planes, peers),
            out_shape=jax.ShapeDtypeStruct((rows, share), BF),
            in_specs=[remote] * 3 + [local] + [remote] * 5 + [local] * 2,
            out_specs=local,
            scratch_shapes=[
                VMEM((rows, share), BF),
                VMEM((share, width), BF),
                VMEM((rows, width), BF),
                VMEM((peers, width), BF),
                VMEM((top, rows), jnp.int32),
                VMEM((planes, rows, share), F32),
                VMEM((rows, share), BF),
                VMEM((2, rows // 2, share), BF),
                VMEM((2, rows, share), BF),
                VMEM((2, rows, share), BF),
                VMEM((planes, rows, share), BF),
                VMEM((planes, rows, share), BF),
                VMEM((planes, width, units), BF),
                VMEM((planes, width, units), BF),
                VMEM((planes, planes, units, share), BF),
                VMEM((8, rows), jnp.int32),
                VMEM((peers, 8, rows), jnp.int32),
                VMEM((peers, slots, width), BF),
                VMEM((peers, slots, width), BF),
                VMEM((peers * slots, width), BF),
                VMEM((planes, peers * slots, units), BF),
                VMEM((planes, peers, slots, share), BF),
                VMEM((planes, peers, slots, share), BF),
                VMEM((planes, planes, rows, share // planes), BF),
                VMEM((planes - 1, planes, rows, share // planes), BF),
                VMEM((planes, rows, share // planes), F32),
                VMEM((rows, share), F32),
                VMEM((8, rows), F32),
                VMEM((planes - 1, 8, rows), F32),
                VMEM((peers, 8, 128), BF),
                VMEM((peers, 8, 128), BF),
                VMEM((rows, peers * slots), BF),
                VMEM((rows, peers * slots), BF),
                DMA((5,)),
                DMA((3 + planes * planes,)),
                DMA((4,)),
                DMA((4,)),
                DMA((4,)),
                DMA((4,)),
                DMA,
                DMA,
                DMA,
                DMA,
                DMA((6,)),
                DMA((6,)),
                DMA((4, planes)),
                DMA((4, planes)),
                DMA((planes,)),
                DMA((planes,)),
                DMA,
                DMA,
                DMA((planes - 1,)),
                DMA((planes - 1,)),
                DMA,
                DMA,
            ],
            compiler_params=pltpu.CompilerParams(
                collective_id=0, has_side_effects=True, vmem_limit_bytes=56 * 1024 * 1024
            ),
        )(
            attn_out,
            out_proj,
            hidden_in,
            norm_gain,
            router.T,
            routes.T,
            w_gate,
            w_up,
            w_down,
            final_gain,
            source.reshape(1, rows),
        )

    placed = (
        P("expert", "tensor"),
        P("tensor", None),
        P("expert", None),
        P(),
        P(),
        P("expert", None),
        P("expert", None, "tensor"),
        P("expert", None, "tensor"),
        P("expert", "tensor", None),
        P("tensor"),
        P("expert"),
    )
    return jax.shard_map(
        on_device, mesh=mesh, in_specs=placed, out_specs=P("expert", "tensor"), check_vma=False
    )
```

```python
import functools

import jax
import jax.numpy as jnp
from jax import lax
from jax.experimental import pallas as pl
from jax.experimental.pallas import tpu as pltpu
from jax.sharding import PartitionSpec as P

epsilon = 1e-06
BF = jnp.bfloat16
F32 = jnp.float32
VMEM = pltpu.VMEM
DMA = pltpu.SemaphoreType.DMA


def dot(a, b):
    return jnp.dot(a, b, preferred_element_type=F32)


def iota(shape, dim):
    return lax.broadcasted_iota(jnp.int32, shape, dim)


def layer(
    planes,
    peers,
    attn_hbm,
    proj_hbm,
    hidden_hbm,
    gain_hbm,
    router_hbm,
    routes_hbm,
    gate_hbm,
    up_hbm,
    down_hbm,
    last_gain_hbm,
    source_hbm,
    out_ref,
    attn_ref,
    proj_ref,
    hidden_ref,
    router_ref,
    routes_ref,
    gain_ref,
    last_gain_ref,
    source_ref,
    part,
    far_send,
    far_recv,
    near_send,
    near_recv,
    res,
    normed,
    gates,
    ups,
    downs,
    ask_send,
    ask_recv,
    slot_send,
    slot_recv,
    rows_in,
    acts,
    back_send,
    back_recv,
    mix_send,
    mix_recv,
    total,
    sq_send,
    sq_recv,
    pack_send,
    pack_recv,
    high,
    low,
    in_sem,
    own_sem,
    att_s,
    att_r,
    res_s,
    res_r,
    ask_s,
    ask_r,
    slot_s,
    slot_r,
    w_s,
    w_r,
    d_s,
    d_r,
    back_s,
    back_r,
    mix_s,
    mix_r,
    sq_s,
    sq_r,
    pack_s,
    pack_r,
):
    x = lax.axis_index("tensor")
    me = lax.axis_index("expert")
    rows, share = attn_hbm.shape
    width = planes * share
    slots = slot_send.shape[1]
    all_slots = peers * slots
    hidden_units = gate_hbm.shape[2]
    right = lax.rem(x + 1, planes)
    left = lax.rem(x + planes - 1, planes)

    def to_plane(src, dst, send, recv, plane):
        return pltpu.make_async_remote_copy(
            src_ref=src, dst_ref=dst, send_sem=send, recv_sem=recv, device_id={"tensor": plane}
        )

    def to_peer(src, dst, send, recv, peer):
        return pltpu.make_async_remote_copy(
            src_ref=src, dst_ref=dst, send_sem=send, recv_sem=recv, device_id={"expert": peer}
        )

    def peer_at(step):
        return lax.rem(me + step, peers)

    barrier = pltpu.get_barrier_semaphore()
    for d in range(1, planes):
        pl.semaphore_signal(barrier, inc=1, device_id={"tensor": lax.rem(x + d, planes)})

    @pl.loop(1, peers)
    def _(step):
        pl.semaphore_signal(barrier, inc=1, device_id={"expert": peer_at(step)})

    inputs = [
        pltpu.make_async_copy(src, dst, in_sem.at[i])
        for i, (src, dst) in enumerate(
            [
                (attn_hbm, attn_ref),
                (proj_hbm, proj_ref),
                (hidden_hbm, hidden_ref),
                (router_hbm, router_ref),
                (routes_hbm, routes_ref),
                (gain_hbm, gain_ref),
                (last_gain_hbm, last_gain_ref),
                (source_hbm, source_ref),
            ]
        )
    ]
    for copy in inputs:
        copy.start()

    piece = share // planes
    chunks = 2 * planes
    own = [
        pltpu.make_async_copy(gate_hbm.at[0], gates.at[0], own_sem.at[0]),
        pltpu.make_async_copy(up_hbm.at[0], ups.at[0], own_sem.at[1]),
    ]
    for c in range(chunks):
        for i in range(2):
            first = (c % 2 * 2 + i) * share + c // 2 * piece
            own.append(
                pltpu.make_async_copy(
                    down_hbm.at[0, :, pl.ds(first, piece)],
                    downs.at[0, c, :, pl.ds(i * piece, piece)],
                    own_sem.at[2 + 2 * c + i],
                )
            )
    for copy in own:
        copy.start()

    inputs[7].wait()
    ask_send[...] = jnp.broadcast_to(source_ref[...], ask_send.shape)
    inputs[0].wait()
    inputs[1].wait()
    for j in range(planes):
        part[j] = dot(attn_ref[...], proj_ref[:, j * share : (j + 1) * share])
    top, bottom = pl.ds(0, rows // 2), pl.ds(rows // 2, rows // 2)
    far_send[...] = part[lax.rem(x + 2, planes)].astype(BF)

    pl.semaphore_wait(barrier, planes - 1 + peers - 1)

    far = [
        to_plane(far_send.at[top], far_recv.at[0], att_s.at[0], att_r.at[0], right),
        to_plane(far_send.at[bottom], far_recv.at[1], att_s.at[1], att_r.at[1], left),
    ]
    for copy in far:
        copy.start()

    fill = width // 8

    def weights_to(hbm, buffer, slot, at, plane):
        pieces = [
            to_plane(
                hbm.at[0, pl.ds(first, count)],
                buffer.at[slot, pl.ds(first, count)],
                w_s.at[at],
                w_r.at[at],
                plane,
            )
            for first, count in ((0, fill), (fill, fill), (2 * fill, fill), (3 * fill, width - 3 * fill))
        ]
        return pieces, to_plane(hbm.at[0], buffer.at[slot], w_s.at[at], w_r.at[at], plane)

    gate_r_pieces, gate_r = weights_to(gate_hbm, gates, 1, 0, right)
    up_r_pieces, up_r = weights_to(up_hbm, ups, 1, 1, right)
    up_l_pieces, up_l = weights_to(up_hbm, ups, 2, 2, left)
    gate_l_pieces, gate_l = weights_to(gate_hbm, gates, 2, 3, left)
    gate_on = to_plane(gates.at[1], gates.at[3], w_s.at[4], w_r.at[4], right)
    up_on = to_plane(ups.at[2], ups.at[3], w_s.at[5], w_r.at[5], left)
    gate_r_pieces[0].start()
    up_l_pieces[0].start()

    @pl.loop(1, peers)
    def _(step):
        to_peer(ask_send, ask_recv.at[me], ask_s, ask_r, peer_at(step)).start()

    for copy in far:
        copy.wait_recv()
    near_send[0] = part[right].astype(BF)
    near_send[1] = part[left].astype(BF)
    near_send[0, top] = (part[right, top] + far_recv[0].astype(F32)).astype(BF)
    near_send[1, bottom] = (part[left, bottom] + far_recv[1].astype(F32)).astype(BF)
    near = [
        to_plane(near_send.at[0], near_recv.at[0], att_s.at[2], att_r.at[2], right),
        to_plane(near_send.at[1], near_recv.at[1], att_s.at[3], att_r.at[3], left),
    ]
    for copy in near:
        copy.start()
    gate_r_pieces[1].start()
    up_l_pieces[1].start()
    for copy in inputs[2:7]:
        copy.wait()
    for copy in near:
        copy.wait_recv()
    mine = pl.ds(pl.multiple_of(x * share, share), share)
    attention = part[x] + near_recv[0].astype(F32) + near_recv[1].astype(F32)
    res[x] = (hidden_ref[:, mine].astype(F32) + attention).astype(BF)
    spread_res = [
        to_plane(res.at[x], res.at[x], res_s.at[0], res_r.at[0], right),
        to_plane(res.at[x], res.at[x], res_s.at[1], res_r.at[1], left),
    ]
    for copy in spread_res:
        copy.start()
    gate_r_pieces[2].start()
    up_l_pieces[2].start()
    res_on = [
        to_plane(res.at[left, top], res.at[left, top], res_s.at[2], res_r.at[2], right),
        to_plane(res.at[right, bottom], res.at[right, bottom], res_s.at[3], res_r.at[3], left),
    ]
    for copy, onward in zip(spread_res, res_on):
        copy.wait_recv()
        onward.start()
    gate_r_pieces[3].start()
    up_l_pieces[3].start()
    for copy in up_r_pieces + gate_l_pieces:
        copy.start()

    for copy in res_on:
        copy.wait_recv()
    square = jnp.zeros((rows, 1), F32)
    for j in range(planes):
        floats = res[j].astype(F32)
        square = square + jnp.sum(floats * floats, axis=1, keepdims=True)
    inverse = lax.rsqrt(square / width + epsilon)
    experts = peers
    logits = jnp.zeros((rows, experts), F32)
    for j in range(planes):
        cols = slice(j * share, (j + 1) * share)
        gain = gain_ref[cols].astype(F32).reshape(1, share)
        scaled = (res[j].astype(F32) * inverse * gain).astype(BF)
        normed[j] = scaled
        logits = logits + lax.dot_general(
            scaled, router_ref[:, cols], (((1,), (1,)), ((), ())), preferred_element_type=F32
        )
    named = jnp.zeros((rows, experts), jnp.bool_)
    which = iota((rows, experts), 1)
    routed = jnp.transpose(routes_ref[...].astype(F32)).astype(jnp.int32)
    for k in range(routed.shape[1]):
        named = named | (routed[:, k : k + 1] == which)
    named_f = jnp.where(named, 1.0, 0.0).astype(F32)
    powers = jnp.where(named, jnp.exp(logits), 0.0)
    weights = powers / jnp.sum(powers, axis=1, keepdims=True)
    before = jnp.where(iota((rows, rows), 1) < iota((rows, rows), 0), 1.0, 0.0).astype(BF)
    rank = dot(before, named_f.astype(BF))
    wide = jnp.where(
        iota((experts, all_slots), 1) // slots == iota((experts, all_slots), 0), 1.0, 0.0
    ).astype(BF)
    wide_rank = dot(rank.astype(BF), wide)
    wide_named = dot(named_f.astype(BF), wide)
    turn = (iota((rows, all_slots), 1) % slots + x * slots).astype(F32)
    taken = (wide_named > 0.5) & (wide_rank == turn)
    weights_high = weights.astype(BF)
    weights_low = (weights - weights_high.astype(F32)).astype(BF)
    high[...] = jnp.where(taken, dot(weights_high, wide), 0.0).astype(BF)
    low[...] = jnp.where(taken, dot(weights_low, wide), 0.0).astype(BF)
    pick = jnp.transpose(jnp.where(taken, 1.0, 0.0).astype(F32)).astype(BF)
    for j in range(planes):
        chosen = dot(pick, normed[j]).astype(BF)
        slot_send[:, :, j * share : (j + 1) * share] = chosen.reshape(peers, slots, share)

    @pl.loop(1, peers)
    def _(step):
        peer = peer_at(step)
        to_peer(slot_send.at[peer], slot_recv.at[me], slot_s, slot_r, peer).start()

    own_slot = pltpu.make_async_copy(slot_send.at[me], slot_recv.at[me], own_sem.at[2 + 2 * chunks])
    own_slot.start()

    half = hidden_units // 2
    upper, lower = pl.ds(0, half), pl.ds(half, half)
    down_r, down_l, on_r, on_l = [], [], [], []
    for c in range(chunks):
        down_r.append(to_plane(downs.at[0, c], downs.at[1, c], d_s.at[0, c], d_r.at[0, c], right))
        down_l.append(to_plane(downs.at[0, c], downs.at[2, c], d_s.at[1, c], d_r.at[1, c], left))
        on_r.append(
            to_plane(
                downs.at[1, c, upper], downs.at[3, c, upper], d_s.at[2, c], d_r.at[2, c], right
            )
        )
        on_l.append(
            to_plane(
                downs.at[2, c, lower], downs.at[3, c, lower], d_s.at[3, c], d_r.at[3, c], left
            )
        )

    def send_down(c):
        down_r[c].start()
        down_l[c].start()

    def pass_down(c):
        down_r[c].wait_recv()
        on_r[c].start()
        down_l[c].wait_recv()
        on_l[c].start()

    for copy in own[2:]:
        copy.wait()
    send_down(0)
    gate_r.wait_recv()
    gate_on.start()
    up_l.wait_recv()
    up_on.start()
    pass_down(0)
    send_down(1)
    send_down(2)

    everyone = pl.ds(0, peers - 1)
    to_peer(slot_send.at[everyone], slot_recv.at[everyone], slot_s, slot_r, me).wait_recv()
    own_slot.wait()
    tiles = 4
    tile_peers = peers // tiles
    tile_rows = tile_peers * slots
    for t in range(tiles):
        rows_in[t * tile_rows : (t + 1) * tile_rows] = slot_recv[
            t * tile_peers : (t + 1) * tile_peers
        ].reshape(tile_rows, width)

    def activate(q):
        gate_part = dot(rows_in[...], gates[q])
        up_part = dot(rows_in[...], ups[q])
        acts[q] = (gate_part / (1.0 + jnp.exp(-gate_part)) * up_part).astype(BF)

    own[0].wait()
    own[1].wait()
    activate(0)
    up_r.wait_recv()
    activate(1)
    gate_l.wait_recv()
    activate(2)

    gate_on.wait_recv()
    up_on.wait_recv()
    activate(3)

    def combine(j):
        to_peer(
            back_send.at[j, everyone], back_recv.at[j, everyone], back_s.at[j], back_r.at[j], me
        ).wait_recv()
        back = back_recv[j].reshape(all_slots, 2 * piece)
        mixed = dot(high[...], back) + dot(low[...], back)
        at = j // 2
        for i in range(2):
            plane = j % 2 * 2 + i
            part_of = mixed[:, i * piece : (i + 1) * piece]
            mix_send[at, plane] = part_of.astype(BF)

            @pl.when(x == plane)
            def _():
                total[:, at * piece : (at + 1) * piece] = part_of

            @pl.when(x != plane)
            def _():
                slot = lax.rem(x - plane + planes, planes) - 1
                to_plane(
                    mix_send.at[at, plane], mix_recv.at[slot, at], mix_s, mix_r, plane
                ).start()

    def produce(j):
        on_r[j].wait_recv()
        on_l[j].wait_recv()
        product = dot(acts[0], downs[0, j])
        for q in range(1, planes):
            product = product + dot(acts[q], downs[q, j])
        back_send[j] = product.astype(BF).reshape(peers, slots, 2 * piece)
        back_recv[j, me] = back_send[j, me]

        @pl.loop(1, peers)
        def _(step):
            peer = peer_at(step)
            to_peer(
                back_send.at[j, peer], back_recv.at[j, me], back_s.at[j], back_r.at[j], peer
            ).start()

    produce(0)
    for c in range(1, chunks):
        pass_down(c)
        if c + 2 < chunks:
            send_down(c + 2)
        if c >= 2:
            produce(c - 1)
        if c == 5:
            combine(0)
    produce(chunks - 1)
    for c in range(1, chunks):
        combine(c)

    three = pl.ds(0, planes - 1)
    to_plane(mix_recv.at[three], mix_recv.at[three], mix_s, mix_r, x).wait_recv()
    mixture = [total[:, j * piece : (j + 1) * piece] for j in range(planes)]
    for j in range(planes):
        for d in range(planes - 1):
            mixture[j] = mixture[j] + mix_recv[d, j].astype(F32)
    whole = jnp.concatenate(mixture, axis=1) + res[x].astype(F32)
    total[...] = whole
    squares = jnp.zeros((rows, 128), F32)
    for c in range(share // 128):
        part_of = whole[:, c * 128 : (c + 1) * 128]
        squares = squares + part_of * part_of
    row_sum = jnp.sum(jnp.transpose(squares), axis=0, keepdims=True)
    sq_send[...] = jnp.broadcast_to(row_sum, sq_send.shape)
    sq = [
        to_plane(sq_send, sq_recv.at[d - 1], sq_s.at[d - 1], sq_r.at[d - 1], lax.rem(x + d, planes))
        for d in range(1, planes)
    ]
    for copy in sq:
        copy.start()

    to_peer(ask_recv.at[everyone], ask_recv.at[everyone], ask_s, ask_r, me).wait_recv()
    ask_recv[me] = ask_send[...]
    asked = ask_recv[...].reshape(peers * 8, rows)
    lanes = iota((peers * 8, rows), 1)
    ours = asked // rows == me
    first = jnp.min(jnp.where(ours, lanes, rows), axis=1, keepdims=True)
    second = jnp.max(jnp.where(ours, lanes, -1), axis=1, keepdims=True)
    line = iota((peers * 8, 1), 0) % 8
    request = jnp.where(line < 4, first, second)
    local = jnp.sum(jnp.where(lanes == request, asked % rows, 0), axis=1, keepdims=True)
    wanted = lanes == local

    for copy in sq:
        copy.wait_recv()
    sums = sq_send[...]
    for d in range(planes - 1):
        sums = sums + sq_recv[d]
    column = jnp.transpose(jnp.broadcast_to(sums[0:1], (rows, rows)))[:, 0:1]
    scale = lax.rsqrt(column / width + epsilon)
    last_gain = last_gain_ref[...].astype(F32).reshape(1, share)
    result = (total[...] * scale * last_gain).astype(BF)
    packed = jnp.zeros((peers * 8, 128), F32)
    for c in range(4):
        chooser = jnp.where(wanted & (line % 4 == c), 1.0, 0.0).astype(BF)
        packed = packed + dot(chooser, result[:, c * 128 : (c + 1) * 128])
    pack_send[...] = packed.astype(BF).reshape(peers, 8, 128)
    pack_recv[me] = pack_send[me]

    @pl.loop(1, peers)
    def _(step):
        peer = peer_at(step)
        to_peer(pack_send.at[peer], pack_recv.at[me], pack_s, pack_r, peer).start()

    asks = jnp.broadcast_to(source_ref[...], (rows, rows))
    asks_down = jnp.transpose(asks.astype(F32)).astype(jnp.int32)
    same = (asks // rows == asks_down // rows) & (iota((rows, rows), 1) < iota((rows, rows), 0))
    later = jnp.max(jnp.where(same, 1, 0), axis=1, keepdims=True)
    place = (asks_down[:, 0:1] // rows) * 8 + later * 4
    at = iota((rows, peers * 8), 1)
    for copy in (
        far + near + spread_res + res_on + [gate_r, up_r, up_l, gate_l, gate_on, up_on]
        + down_r + down_l + on_r + on_l + sq
    ):
        copy.wait_send()

    @pl.loop(1, peers)
    def _(step):
        to_peer(ask_send, ask_recv.at[me], ask_s, ask_r, me).wait_send()

    to_peer(slot_send.at[everyone], slot_recv.at[everyone], slot_s, slot_r, me).wait_send()
    for j in range(chunks):
        to_peer(
            back_send.at[j, everyone], back_recv.at[j, everyone], back_s.at[j], back_r.at[j], me
        ).wait_send()
    to_plane(mix_send.at[:, three], mix_recv.at[three], mix_s, mix_r, x).wait_send()
    to_peer(pack_send.at[everyone], pack_recv.at[everyone], pack_s, pack_r, me).wait_recv()
    landed = pack_recv[...].reshape(peers * 8, 128)
    for c in range(4):
        chooser = jnp.where(at == place + c, 1.0, 0.0).astype(BF)
        out_ref[:, c * 128 : (c + 1) * 128] = dot(chooser, landed).astype(BF)

    to_peer(pack_send.at[everyone], pack_recv.at[everyone], pack_s, pack_r, me).wait_send()


def solution(mesh):
    planes, peers = mesh.shape["tensor"], mesh.shape["expert"]

    def on_device(
        attn_out,
        out_proj,
        hidden_in,
        norm_gain,
        router,
        routes,
        w_gate,
        w_up,
        w_down,
        final_gain,
        source,
    ):
        rows, width = hidden_in.shape
        share = width // planes
        top = routes.shape[1]
        slots = min(rows, 2 * rows * top // peers) // planes
        units = w_gate.shape[2]
        local = pl.BlockSpec(memory_space=pltpu.VMEM)
        remote = pl.BlockSpec(memory_space=pl.ANY)
        return pl.pallas_call(
            functools.partial(layer, planes, peers),
            out_shape=jax.ShapeDtypeStruct((rows, share), BF),
            in_specs=[remote] * 11,
            out_specs=local,
            scratch_shapes=[
                VMEM((rows, share), BF),
                VMEM((share, width), BF),
                VMEM((rows, width), BF),
                VMEM((peers, width), BF),
                VMEM((top, rows), jnp.int32),
                VMEM((width,), BF),
                VMEM((share,), BF),
                VMEM((1, rows), jnp.int32),
                VMEM((planes, rows, share), F32),
                VMEM((rows, share), BF),
                VMEM((2, rows // 2, share), BF),
                VMEM((2, rows, share), BF),
                VMEM((2, rows, share), BF),
                VMEM((planes, rows, share), BF),
                VMEM((planes, rows, share), BF),
                VMEM((planes, width, units), BF),
                VMEM((planes, width, units), BF),
                VMEM((planes, 2 * planes, units, share // 2), BF),
                VMEM((8, rows), jnp.int32),
                VMEM((peers, 8, rows), jnp.int32),
                VMEM((peers, slots, width), BF),
                VMEM((peers, slots, width), BF),
                VMEM((peers * slots, width), BF),
                VMEM((planes, peers * slots, units), BF),
                VMEM((2 * planes, peers, slots, share // 2), BF),
                VMEM((2 * planes, peers, slots, share // 2), BF),
                VMEM((planes, planes, rows, share // planes), BF),
                VMEM((planes - 1, planes, rows, share // planes), BF),
                VMEM((rows, share), F32),
                VMEM((8, rows), F32),
                VMEM((planes - 1, 8, rows), F32),
                VMEM((peers, 8, 128), BF),
                VMEM((peers, 8, 128), BF),
                VMEM((rows, peers * slots), BF),
                VMEM((rows, peers * slots), BF),
                DMA((8,)),
                DMA((3 + 4 * planes,)),
                DMA((4,)),
                DMA((4,)),
                DMA((4,)),
                DMA((4,)),
                DMA,
                DMA,
                DMA,
                DMA,
                DMA((6,)),
                DMA((6,)),
                DMA((4, 2 * planes)),
                DMA((4, 2 * planes)),
                DMA((2 * planes,)),
                DMA((2 * planes,)),
                DMA,
                DMA,
                DMA((planes - 1,)),
                DMA((planes - 1,)),
                DMA,
                DMA,
            ],
            compiler_params=pltpu.CompilerParams(
                collective_id=0, has_side_effects=True, vmem_limit_bytes=56 * 1024 * 1024
            ),
        )(
            attn_out,
            out_proj,
            hidden_in,
            norm_gain,
            router.T,
            routes.T,
            w_gate,
            w_up,
            w_down,
            final_gain,
            source.reshape(1, rows),
        )

    placed = (
        P("expert", "tensor"),
        P("tensor", None),
        P("expert", None),
        P(),
        P(),
        P("expert", None),
        P("expert", None, "tensor"),
        P("expert", None, "tensor"),
        P("expert", "tensor", None),
        P("tensor"),
        P("expert"),
    )
    return jax.shard_map(
        on_device, mesh=mesh, in_specs=placed, out_specs=P("expert", "tensor"), check_vma=False
    )
```

```python
import functools

import jax
import jax.numpy as jnp
from jax import lax
from jax.experimental import pallas as pl
from jax.experimental.pallas import tpu as pltpu
from jax.sharding import PartitionSpec as P

epsilon = 1e-06
BF = jnp.bfloat16
F32 = jnp.float32
VMEM = pltpu.VMEM
DMA = pltpu.SemaphoreType.DMA


def dot(a, b):
    return jnp.dot(a, b, preferred_element_type=F32)


def iota(shape, dim):
    return lax.broadcasted_iota(jnp.int32, shape, dim)


def layer(
    planes,
    peers,
    attn_hbm,
    proj_hbm,
    hidden_hbm,
    gain_hbm,
    router_hbm,
    routes_hbm,
    gate_hbm,
    up_hbm,
    down_hbm,
    last_gain_hbm,
    source_hbm,
    out_ref,
    attn_ref,
    proj_ref,
    hidden_ref,
    router_ref,
    routes_ref,
    gain_ref,
    last_gain_ref,
    source_ref,
    part,
    far_send,
    far_recv,
    near_send,
    near_recv,
    res,
    normed,
    gates,
    ups,
    downs,
    stage,
    ask_send,
    ask_recv,
    slot_send,
    slot_recv,
    rows_in,
    acts,
    back_send,
    back_recv,
    mix_send,
    mix_recv,
    total,
    sq_send,
    sq_recv,
    pack_send,
    pack_recv,
    high,
    low,
    in_sem,
    own_sem,
    att_s,
    att_r,
    res_s,
    res_r,
    ask_s,
    ask_r,
    slot_s,
    slot_r,
    w_s,
    w_r,
    d_s,
    d_r,
    back_s,
    back_r,
    mix_s,
    mix_r,
    sq_s,
    sq_r,
    pack_s,
    pack_r,
):
    x = lax.axis_index("tensor")
    me = lax.axis_index("expert")
    rows, share = attn_hbm.shape
    width = planes * share
    slots = slot_send.shape[1]
    all_slots = peers * slots
    hidden_units = gate_hbm.shape[2]
    right = lax.rem(x + 1, planes)
    left = lax.rem(x + planes - 1, planes)
    active = x // 2
    host = lax.rem(me, 2) == active
    guest = jnp.logical_not(host)
    partner = x + 1 - 2 * lax.rem(x, 2)
    outer = planes - 1 - x
    sibling = me + 1 - 2 * lax.rem(me, 2)

    def to_plane(src, dst, send, recv, plane):
        return pltpu.make_async_remote_copy(
            src_ref=src, dst_ref=dst, send_sem=send, recv_sem=recv, device_id={"tensor": plane}
        )

    def to_device(src, dst, send, recv, plane, peer):
        return pltpu.make_async_remote_copy(
            src_ref=src,
            dst_ref=dst,
            send_sem=send,
            recv_sem=recv,
            device_id={"tensor": plane, "expert": peer},
        )

    def to_peer(src, dst, send, recv, peer):
        return pltpu.make_async_remote_copy(
            src_ref=src, dst_ref=dst, send_sem=send, recv_sem=recv, device_id={"expert": peer}
        )

    def peer_at(step):
        return lax.rem(me + step, peers)

    barrier = pltpu.get_barrier_semaphore()
    for d in range(1, planes):
        pl.semaphore_signal(barrier, inc=1, device_id={"tensor": lax.rem(x + d, planes)})
    pl.semaphore_signal(barrier, inc=1, device_id={"tensor": outer, "expert": sibling})

    @pl.loop(1, peers)
    def _(step):
        pl.semaphore_signal(barrier, inc=1, device_id={"expert": peer_at(step)})

    inputs = [
        pltpu.make_async_copy(src, dst, in_sem.at[i])
        for i, (src, dst) in enumerate(
            [
                (attn_hbm, attn_ref),
                (proj_hbm, proj_ref),
                (hidden_hbm, hidden_ref),
                (router_hbm, router_ref),
                (routes_hbm, routes_ref),
                (gain_hbm, gain_ref),
                (last_gain_hbm, last_gain_ref),
                (source_hbm, source_ref),
            ]
        )
    ]
    for copy in inputs:
        copy.start()

    piece = share // planes
    chunks = 2 * planes
    own = [
        pltpu.make_async_copy(gate_hbm.at[0], gates.at[0], own_sem.at[0]),
        pltpu.make_async_copy(up_hbm.at[0], ups.at[0], own_sem.at[1]),
    ]

    def own_down(c, buffer):
        copies = []
        for i in range(2):
            first = (c % 2 * 2 + i) * share + c // 2 * piece
            copies.append(
                pltpu.make_async_copy(
                    down_hbm.at[0, :, pl.ds(first, piece)],
                    buffer.at[c, :, pl.ds(i * piece, piece)],
                    own_sem.at[2 + 2 * c + i],
                )
            )
        return copies

    @pl.when(host)
    def _():
        for copy in own:
            copy.start()
        for c in range(chunks):
            for copy in own_down(c, downs.at[0]):
                copy.start()

    @pl.when(guest)
    def _():
        for c in range(chunks):
            for copy in own_down(c, stage):
                copy.start()

    inputs[7].wait()
    ask_send[...] = jnp.broadcast_to(source_ref[...], ask_send.shape)
    inputs[0].wait()
    inputs[1].wait()
    for j in range(planes):
        part[j] = dot(attn_ref[...], proj_ref[:, j * share : (j + 1) * share])
    top, bottom = pl.ds(0, rows // 2), pl.ds(rows // 2, rows // 2)
    far_send[...] = part[lax.rem(x + 2, planes)].astype(BF)

    pl.semaphore_wait(barrier, planes - 1 + 1 + peers - 1)

    far = [
        to_plane(far_send.at[top], far_recv.at[0], att_s.at[0], att_r.at[0], right),
        to_plane(far_send.at[bottom], far_recv.at[1], att_s.at[1], att_r.at[1], left),
    ]
    for copy in far:
        copy.start()

    fill = width // 16
    middle = width // 2
    units_of = [(gates, gate_hbm, 0), (gates, gate_hbm, middle), (ups, up_hbm, 0), (ups, up_hbm, middle)]

    def unit_view(slot, u):
        buffer, _, first = units_of[u]
        return buffer.at[slot, pl.ds(first, middle)]

    def own_unit(u, slot, kind, plane, peer, first=0, count=middle):
        buffer, hbm, base = units_of[u]
        return to_device(
            hbm.at[0, pl.ds(base + first, count)],
            buffer.at[slot, pl.ds(base + first, count)],
            w_s.at[kind, u],
            w_r.at[slot, u],
            plane,
            peer,
        )

    def onward_unit(u, slot, there, kind, plane, peer):
        return to_device(
            unit_view(slot, u), unit_view(there, u), w_s.at[kind, u], w_r.at[there, u], plane, peer
        )

    def unit_arrived(slot, u):
        own_unit(u, slot, 0, x, me).wait_recv()

    def send_units(first, count, later):
        @pl.when(host)
        def _():
            own_unit(0, 1, 0, partner, me, first, count).start()
            for u in range(1, 4 if later else 1):
                own_unit(u, 1, 0, partner, me).start()

        @pl.when(guest)
        def _():
            own_unit(0, 2, 0, outer, sibling, first, count).start()
            for u in range(1, 4 if later else 1):
                own_unit(u, 2, 0, outer, sibling).start()

    send_units(0, fill, False)

    @pl.loop(1, peers)
    def _(step):
        to_peer(ask_send, ask_recv.at[me], ask_s, ask_r, peer_at(step)).start()

    for copy in far:
        copy.wait_recv()
    near_send[0] = part[right].astype(BF)
    near_send[1] = part[left].astype(BF)
    near_send[0, top] = (part[right, top] + far_recv[0].astype(F32)).astype(BF)
    near_send[1, bottom] = (part[left, bottom] + far_recv[1].astype(F32)).astype(BF)
    near = [
        to_plane(near_send.at[0], near_recv.at[0], att_s.at[2], att_r.at[2], right),
        to_plane(near_send.at[1], near_recv.at[1], att_s.at[3], att_r.at[3], left),
    ]
    for copy in near:
        copy.start()
    send_units(fill, fill, False)
    for copy in inputs[2:7]:
        copy.wait()
    for copy in near:
        copy.wait_recv()
    mine = pl.ds(pl.multiple_of(x * share, share), share)
    attention = part[x] + near_recv[0].astype(F32) + near_recv[1].astype(F32)
    res[x] = (hidden_ref[:, mine].astype(F32) + attention).astype(BF)
    spread_res = [
        to_plane(res.at[x], res.at[x], res_s.at[0], res_r.at[0], right),
        to_plane(res.at[x], res.at[x], res_s.at[1], res_r.at[1], left),
    ]
    for copy in spread_res:
        copy.start()
    send_units(2 * fill, fill, False)
    res_on = [
        to_plane(res.at[left, top], res.at[left, top], res_s.at[2], res_r.at[2], right),
        to_plane(res.at[right, bottom], res.at[right, bottom], res_s.at[3], res_r.at[3], left),
    ]
    for copy, onward in zip(spread_res, res_on):
        copy.wait_recv()
        onward.start()
    send_units(3 * fill, middle - 3 * fill, True)

    @pl.when(host)
    def _():
        for u in range(4):
            own_unit(u, 0, 1, x, sibling).start()


    for copy in res_on:
        copy.wait_recv()
    square = jnp.zeros((rows, 1), F32)
    for j in range(planes):
        floats = res[j].astype(F32)
        square = square + jnp.sum(floats * floats, axis=1, keepdims=True)
    inverse = lax.rsqrt(square / width + epsilon)
    experts = peers
    logits = jnp.zeros((rows, experts), F32)
    for j in range(planes):
        cols = slice(j * share, (j + 1) * share)
        gain = gain_ref[cols].astype(F32).reshape(1, share)
        scaled = (res[j].astype(F32) * inverse * gain).astype(BF)
        normed[j] = scaled
        logits = logits + lax.dot_general(
            scaled, router_ref[:, cols], (((1,), (1,)), ((), ())), preferred_element_type=F32
        )
    named = jnp.zeros((rows, experts), jnp.bool_)
    which = iota((rows, experts), 1)
    routed = jnp.transpose(routes_ref[...].astype(F32)).astype(jnp.int32)
    for k in range(routed.shape[1]):
        named = named | (routed[:, k : k + 1] == which)
    named_f = jnp.where(named, 1.0, 0.0).astype(F32)
    powers = jnp.where(named, jnp.exp(logits), 0.0)
    weights = powers / jnp.sum(powers, axis=1, keepdims=True)
    before = jnp.where(iota((rows, rows), 1) < iota((rows, rows), 0), 1.0, 0.0).astype(BF)
    rank = dot(before, named_f.astype(BF))
    wide = jnp.where(
        iota((experts, all_slots), 1) // (2 * slots) * 2 + active == iota((experts, all_slots), 0),
        1.0,
        0.0,
    ).astype(BF)
    wide_rank = dot(rank.astype(BF), wide)
    wide_named = dot(named_f.astype(BF), wide)
    turn = (iota((rows, all_slots), 1) % (2 * slots) + lax.rem(x, 2) * 2 * slots).astype(F32)
    taken = (wide_named > 0.5) & (wide_rank == turn)
    weights_high = weights.astype(BF)
    weights_low = (weights - weights_high.astype(F32)).astype(BF)
    high[...] = jnp.where(taken, dot(weights_high, wide), 0.0).astype(BF)
    low[...] = jnp.where(taken, dot(weights_low, wide), 0.0).astype(BF)
    pick = jnp.transpose(jnp.where(taken, 1.0, 0.0).astype(F32)).astype(BF)
    for j in range(planes):
        chosen = dot(pick, normed[j]).astype(BF)
        slot_send[:, :, j * share : (j + 1) * share] = chosen.reshape(peers, slots, share)

    @pl.loop(1, peers)
    def _(step):
        peer = peer_at(step)
        to_peer(slot_send.at[peer], slot_recv.at[me], slot_s, slot_r, peer).start()

    own_slot = pltpu.make_async_copy(slot_send.at[me], slot_recv.at[me], own_sem.at[2 + 2 * chunks])
    own_slot.start()

    def chunk_copy(c, source, slot, kind, plane, peer):
        return to_device(
            source.at[c], downs.at[slot, c], d_s.at[kind, c], d_r.at[slot, c], plane, peer
        )

    def chunk_arrived(slot, c):
        chunk_copy(c, stage, slot, 0, x, me).wait_recv()

    @pl.when(host)
    def _():
        for c in range(chunks):
            for copy in own_down(c, downs.at[0]):
                copy.wait()
            chunk_copy(c, downs.at[0], 0, 1, x, sibling).start()
        for u in range(4):
            unit_arrived(1, u)
            onward_unit(u, 1, 1, 2, x, sibling).start()
        for c in range(2):
            chunk_copy(c, downs.at[0], 1, 0, partner, me).start()

    @pl.when(guest)
    def _():
        for c in range(chunks):
            for copy in own_down(c, stage):
                copy.wait()
            chunk_copy(c, stage, 2, 0, outer, sibling).start()
        for u in range(4):
            unit_arrived(2, u)
            onward_unit(u, 2, 3, 1, partner, me).start()
            onward_unit(u, 2, 2, 2, x, sibling).start()
        for c in range(chunks):
            chunk_arrived(2, c)
            chunk_copy(c, downs.at[2], 3, 1, partner, me).start()
            chunk_copy(c, downs.at[2], 2, 2, x, sibling).start()
        for u in range(4):
            unit_arrived(3, u)
            onward_unit(u, 3, 3, 3, x, sibling).start()

    def pass_down(c):
        @pl.when(host)
        def _():
            chunk_arrived(1, c)
            chunk_copy(c, downs.at[1], 1, 2, x, sibling).start()

        @pl.when(guest)
        def _():
            chunk_arrived(3, c)
            chunk_copy(c, downs.at[3], 3, 3, x, sibling).start()

    everyone = pl.ds(0, peers - 1)
    to_peer(slot_send.at[everyone], slot_recv.at[everyone], slot_s, slot_r, me).wait_recv()
    @pl.when(host)
    def _():
        for c in range(2, chunks):
            chunk_copy(c, downs.at[0], 1, 0, partner, me).start()

    own_slot.wait()
    tiles = 4
    tile_peers = peers // tiles
    tile_rows = tile_peers * slots
    for t in range(tiles):
        rows_in[t * tile_rows : (t + 1) * tile_rows] = slot_recv[
            t * tile_peers : (t + 1) * tile_peers
        ].reshape(tile_rows, width)

    def activate(q):
        gate_part = dot(rows_in[...], gates[q])
        up_part = dot(rows_in[...], ups[q])
        acts[q] = (gate_part / (1.0 + jnp.exp(-gate_part)) * up_part).astype(BF)

    @pl.when(host)
    def _():
        for copy in own:
            copy.wait()
        for u in range(4):
            unit_arrived(2, u)
            unit_arrived(3, u)

    @pl.when(guest)
    def _():
        for u in range(4):
            unit_arrived(0, u)
            unit_arrived(1, u)

    for q in range(planes):
        activate(q)

    def combine(j):
        to_peer(
            back_send.at[j, everyone], back_recv.at[j, everyone], back_s.at[j], back_r.at[j], me
        ).wait_recv()
        back = back_recv[j].reshape(all_slots, 2 * piece)
        mixed = dot(high[...], back) + dot(low[...], back)
        at = j // 2
        for i in range(2):
            plane = j % 2 * 2 + i
            part_of = mixed[:, i * piece : (i + 1) * piece]
            mix_send[at, plane] = part_of.astype(BF)

            @pl.when(x == plane)
            def _():
                total[:, at * piece : (at + 1) * piece] = part_of

            @pl.when(x != plane)
            def _():
                slot = lax.rem(x - plane + planes, planes) - 1
                to_plane(
                    mix_send.at[at, plane], mix_recv.at[slot, at], mix_s, mix_r, plane
                ).start()

    def produce(j):
        @pl.when(host)
        def _():
            chunk_arrived(2, j)
            chunk_arrived(3, j)

        @pl.when(guest)
        def _():
            chunk_arrived(0, j)
            chunk_arrived(1, j)

        product = dot(acts[0], downs[0, j])
        for q in range(1, planes):
            product = product + dot(acts[q], downs[q, j])
        back_send[j] = product.astype(BF).reshape(peers, slots, 2 * piece)
        back_recv[j, me] = back_send[j, me]

        @pl.loop(1, peers)
        def _(step):
            peer = peer_at(step)
            to_peer(
                back_send.at[j, peer], back_recv.at[j, me], back_s.at[j], back_r.at[j], peer
            ).start()

    pass_down(0)
    for c in range(chunks):
        if c + 1 < chunks:
            pass_down(c + 1)
        produce(c)
        if c >= 4:
            combine(c - 4)
    for c in range(chunks - 4, chunks):
        combine(c)

    three = pl.ds(0, planes - 1)
    to_plane(mix_recv.at[three], mix_recv.at[three], mix_s, mix_r, x).wait_recv()
    mixture = [total[:, j * piece : (j + 1) * piece] for j in range(planes)]
    for j in range(planes):
        for d in range(planes - 1):
            mixture[j] = mixture[j] + mix_recv[d, j].astype(F32)
    whole = jnp.concatenate(mixture, axis=1) + res[x].astype(F32)
    total[...] = whole
    squares = jnp.zeros((rows, 128), F32)
    for c in range(share // 128):
        part_of = whole[:, c * 128 : (c + 1) * 128]
        squares = squares + part_of * part_of
    row_sum = jnp.sum(jnp.transpose(squares), axis=0, keepdims=True)
    sq_send[...] = jnp.broadcast_to(row_sum, sq_send.shape)
    sq = [
        to_plane(sq_send, sq_recv.at[d - 1], sq_s.at[d - 1], sq_r.at[d - 1], lax.rem(x + d, planes))
        for d in range(1, planes)
    ]
    for copy in sq:
        copy.start()

    to_peer(ask_recv.at[everyone], ask_recv.at[everyone], ask_s, ask_r, me).wait_recv()
    ask_recv[me] = ask_send[...]
    asked = ask_recv[...].reshape(peers * 8, rows)
    lanes = iota((peers * 8, rows), 1)
    ours = asked // rows == me
    first = jnp.min(jnp.where(ours, lanes, rows), axis=1, keepdims=True)
    second = jnp.max(jnp.where(ours, lanes, -1), axis=1, keepdims=True)
    line = iota((peers * 8, 1), 0) % 8
    request = jnp.where(line < 4, first, second)
    local = jnp.sum(jnp.where(lanes == request, asked % rows, 0), axis=1, keepdims=True)
    wanted = lanes == local

    for copy in sq:
        copy.wait_recv()
    sums = sq_send[...]
    for d in range(planes - 1):
        sums = sums + sq_recv[d]
    column = jnp.transpose(jnp.broadcast_to(sums[0:1], (rows, rows)))[:, 0:1]
    scale = lax.rsqrt(column / width + epsilon)
    last_gain = last_gain_ref[...].astype(F32).reshape(1, share)
    result = (total[...] * scale * last_gain).astype(BF)
    packed = jnp.zeros((peers * 8, 128), F32)
    for c in range(4):
        chooser = jnp.where(wanted & (line % 4 == c), 1.0, 0.0).astype(BF)
        packed = packed + dot(chooser, result[:, c * 128 : (c + 1) * 128])
    pack_send[...] = packed.astype(BF).reshape(peers, 8, 128)
    pack_recv[me] = pack_send[me]

    @pl.loop(1, peers)
    def _(step):
        peer = peer_at(step)
        to_peer(pack_send.at[peer], pack_recv.at[me], pack_s, pack_r, peer).start()

    asks = jnp.broadcast_to(source_ref[...], (rows, rows))
    asks_down = jnp.transpose(asks.astype(F32)).astype(jnp.int32)
    same = (asks // rows == asks_down // rows) & (iota((rows, rows), 1) < iota((rows, rows), 0))
    later = jnp.max(jnp.where(same, 1, 0), axis=1, keepdims=True)
    place = (asks_down[:, 0:1] // rows) * 8 + later * 4
    at = iota((rows, peers * 8), 1)
    for copy in far + near + spread_res + res_on + sq:
        copy.wait_send()

    @pl.when(host)
    def _():
        for kind in range(3):
            for u in range(4):
                own_unit(u, 0, kind, x, me).wait_send()
            for c in range(chunks):
                chunk_copy(c, stage, 0, kind, x, me).wait_send()

    @pl.when(guest)
    def _():
        for kind in range(4):
            for u in range(4):
                own_unit(u, 0, kind, x, me).wait_send()
            for c in range(chunks):
                chunk_copy(c, stage, 0, kind, x, me).wait_send()

    @pl.loop(1, peers)
    def _(step):
        to_peer(ask_send, ask_recv.at[me], ask_s, ask_r, me).wait_send()

    to_peer(slot_send.at[everyone], slot_recv.at[everyone], slot_s, slot_r, me).wait_send()
    for j in range(chunks):
        to_peer(
            back_send.at[j, everyone], back_recv.at[j, everyone], back_s.at[j], back_r.at[j], me
        ).wait_send()
    to_plane(mix_send.at[:, three], mix_recv.at[three], mix_s, mix_r, x).wait_send()
    to_peer(pack_send.at[everyone], pack_recv.at[everyone], pack_s, pack_r, me).wait_recv()
    landed = pack_recv[...].reshape(peers * 8, 128)
    for c in range(4):
        chooser = jnp.where(at == place + c, 1.0, 0.0).astype(BF)
        out_ref[:, c * 128 : (c + 1) * 128] = dot(chooser, landed).astype(BF)

    to_peer(pack_send.at[everyone], pack_recv.at[everyone], pack_s, pack_r, me).wait_send()


def solution(mesh):
    planes, peers = mesh.shape["tensor"], mesh.shape["expert"]

    def on_device(
        attn_out,
        out_proj,
        hidden_in,
        norm_gain,
        router,
        routes,
        w_gate,
        w_up,
        w_down,
        final_gain,
        source,
    ):
        rows, width = hidden_in.shape
        share = width // planes
        top = routes.shape[1]
        slots = min(rows, 2 * rows * top // peers) // planes
        units = w_gate.shape[2]
        local = pl.BlockSpec(memory_space=pltpu.VMEM)
        remote = pl.BlockSpec(memory_space=pl.ANY)
        return pl.pallas_call(
            functools.partial(layer, planes, peers),
            out_shape=jax.ShapeDtypeStruct((rows, share), BF),
            in_specs=[remote] * 11,
            out_specs=local,
            scratch_shapes=[
                VMEM((rows, share), BF),
                VMEM((share, width), BF),
                VMEM((rows, width), BF),
                VMEM((peers, width), BF),
                VMEM((top, rows), jnp.int32),
                VMEM((width,), BF),
                VMEM((share,), BF),
                VMEM((1, rows), jnp.int32),
                VMEM((planes, rows, share), F32),
                VMEM((rows, share), BF),
                VMEM((2, rows // 2, share), BF),
                VMEM((2, rows, share), BF),
                VMEM((2, rows, share), BF),
                VMEM((planes, rows, share), BF),
                VMEM((planes, rows, share), BF),
                VMEM((planes, width, units), BF),
                VMEM((planes, width, units), BF),
                VMEM((planes, 2 * planes, units, share // 2), BF),
                VMEM((2 * planes, units, share // 2), BF),
                VMEM((8, rows), jnp.int32),
                VMEM((peers, 8, rows), jnp.int32),
                VMEM((peers, slots, width), BF),
                VMEM((peers, slots, width), BF),
                VMEM((peers * slots, width), BF),
                VMEM((planes, peers * slots, units), BF),
                VMEM((2 * planes, peers, slots, share // 2), BF),
                VMEM((2 * planes, peers, slots, share // 2), BF),
                VMEM((planes, planes, rows, share // planes), BF),
                VMEM((planes - 1, planes, rows, share // planes), BF),
                VMEM((rows, share), F32),
                VMEM((8, rows), F32),
                VMEM((planes - 1, 8, rows), F32),
                VMEM((peers, 8, 128), BF),
                VMEM((peers, 8, 128), BF),
                VMEM((rows, peers * slots), BF),
                VMEM((rows, peers * slots), BF),
                DMA((8,)),
                DMA((3 + 4 * planes,)),
                DMA((4,)),
                DMA((4,)),
                DMA((4,)),
                DMA((4,)),
                DMA,
                DMA,
                DMA,
                DMA,
                DMA((4, 4)),
                DMA((4, 4)),
                DMA((4, 2 * planes)),
                DMA((4, 2 * planes)),
                DMA((2 * planes,)),
                DMA((2 * planes,)),
                DMA,
                DMA,
                DMA((planes - 1,)),
                DMA((planes - 1,)),
                DMA,
                DMA,
            ],
            compiler_params=pltpu.CompilerParams(
                collective_id=0, has_side_effects=True, vmem_limit_bytes=56 * 1024 * 1024
            ),
        )(
            attn_out,
            out_proj,
            hidden_in,
            norm_gain,
            router.T,
            routes.T,
            w_gate,
            w_up,
            w_down,
            final_gain,
            source.reshape(1, rows),
        )

    placed = (
        P("expert", "tensor"),
        P("tensor", None),
        P("expert", None),
        P(),
        P(),
        P("expert", None),
        P("expert", None, "tensor"),
        P("expert", None, "tensor"),
        P("expert", "tensor", None),
        P("tensor"),
        P("expert"),
    )
    return jax.shard_map(
        on_device, mesh=mesh, in_specs=placed, out_specs=P("expert", "tensor"), check_vma=False
    )
```

```python
import functools

import jax
import jax.numpy as jnp
from jax import lax
from jax.experimental import pallas as pl
from jax.experimental.pallas import tpu as pltpu
from jax.sharding import PartitionSpec as P

epsilon = 1e-06
BF = jnp.bfloat16
F32 = jnp.float32
VMEM = pltpu.VMEM
DMA = pltpu.SemaphoreType.DMA


def dot(a, b):
    return jnp.dot(a, b, preferred_element_type=F32)


def iota(shape, dim):
    return lax.broadcasted_iota(jnp.int32, shape, dim)


def layer(
    planes,
    peers,
    attn_hbm,
    proj_hbm,
    hidden_hbm,
    gain_hbm,
    router_hbm,
    routes_hbm,
    gate_hbm,
    up_hbm,
    down_hbm,
    last_gain_hbm,
    source_hbm,
    out_ref,
    attn_ref,
    proj_ref,
    hidden_ref,
    router_ref,
    routes_ref,
    gain_ref,
    last_gain_ref,
    source_ref,
    part,
    far_send,
    far_recv,
    near_send,
    near_recv,
    res,
    normed,
    gates,
    ups,
    downs,
    stage,
    ask_send,
    ask_recv,
    slot_send,
    slot_recv,
    rows_in,
    acts,
    back_send,
    back_recv,
    mix_send,
    mix_recv,
    total,
    sq_send,
    sq_recv,
    pack_send,
    pack_recv,
    high,
    low,
    in_sem,
    own_sem,
    att_s,
    att_r,
    res_s,
    res_r,
    ask_s,
    ask_r,
    slot_s,
    slot_r,
    w_s,
    w_r,
    d_s,
    d_r,
    back_s,
    back_r,
    mix_s,
    mix_r,
    sq_s,
    sq_r,
    pack_s,
    pack_r,
):
    x = lax.axis_index("tensor")
    me = lax.axis_index("expert")
    rows, share = attn_hbm.shape
    width = planes * share
    slots = slot_send.shape[1]
    all_slots = peers * slots
    hidden_units = gate_hbm.shape[2]
    right = lax.rem(x + 1, planes)
    left = lax.rem(x + planes - 1, planes)
    active = x // 2
    host = lax.rem(me, 2) == active
    guest = jnp.logical_not(host)
    partner = x + 1 - 2 * lax.rem(x, 2)
    outer = planes - 1 - x
    sibling = me + 1 - 2 * lax.rem(me, 2)

    def to_plane(src, dst, send, recv, plane):
        return pltpu.make_async_remote_copy(
            src_ref=src, dst_ref=dst, send_sem=send, recv_sem=recv, device_id={"tensor": plane}
        )

    def to_device(src, dst, send, recv, plane, peer):
        return pltpu.make_async_remote_copy(
            src_ref=src,
            dst_ref=dst,
            send_sem=send,
            recv_sem=recv,
            device_id={"tensor": plane, "expert": peer},
        )

    def to_peer(src, dst, send, recv, peer):
        return pltpu.make_async_remote_copy(
            src_ref=src, dst_ref=dst, send_sem=send, recv_sem=recv, device_id={"expert": peer}
        )

    def peer_at(step):
        return lax.rem(me + step, peers)

    barrier = pltpu.get_barrier_semaphore()
    for d in range(1, planes):
        pl.semaphore_signal(barrier, inc=1, device_id={"tensor": lax.rem(x + d, planes)})
    pl.semaphore_signal(barrier, inc=1, device_id={"tensor": outer, "expert": sibling})

    @pl.loop(1, peers)
    def _(step):
        pl.semaphore_signal(barrier, inc=1, device_id={"expert": peer_at(step)})

    inputs = [
        pltpu.make_async_copy(src, dst, in_sem.at[i])
        for i, (src, dst) in enumerate(
            [
                (attn_hbm, attn_ref),
                (proj_hbm, proj_ref),
                (hidden_hbm, hidden_ref),
                (router_hbm, router_ref),
                (routes_hbm, routes_ref),
                (gain_hbm, gain_ref),
                (last_gain_hbm, last_gain_ref),
                (source_hbm, source_ref),
            ]
        )
    ]
    for copy in inputs:
        copy.start()

    piece = share // planes
    chunks = 2 * planes
    own = [
        pltpu.make_async_copy(gate_hbm.at[0], gates.at[0], own_sem.at[0]),
        pltpu.make_async_copy(up_hbm.at[0], ups.at[0], own_sem.at[1]),
    ]

    def own_down(c, buffer):
        copies = []
        for i in range(2):
            first = (c % 2 * 2 + i) * share + c // 2 * piece
            copies.append(
                pltpu.make_async_copy(
                    down_hbm.at[0, :, pl.ds(first, piece)],
                    buffer.at[c, :, pl.ds(i * piece, piece)],
                    own_sem.at[2 + 2 * c + i],
                )
            )
        return copies

    @pl.when(host)
    def _():
        for copy in own:
            copy.start()
        for c in range(chunks):
            for copy in own_down(c, downs.at[0]):
                copy.start()

    @pl.when(guest)
    def _():
        for c in range(chunks):
            for copy in own_down(c, stage):
                copy.start()

    inputs[7].wait()
    ask_send[...] = jnp.broadcast_to(source_ref[...], ask_send.shape)
    inputs[0].wait()
    inputs[1].wait()
    for j in range(planes):
        part[j] = dot(attn_ref[...], proj_ref[:, j * share : (j + 1) * share])
    top, bottom = pl.ds(0, rows // 2), pl.ds(rows // 2, rows // 2)
    wing = share // 2
    wings = [pl.ds(0, wing), pl.ds(wing, wing)]
    for h in range(2):
        far_send[h] = part[lax.rem(x + 2, planes), :, wings[h]].astype(BF)

    pl.semaphore_wait(barrier, planes - 1 + 1 + peers - 1)

    far = [
        [
            to_plane(far_send.at[h, top], far_recv.at[h, 0], att_s.at[h, 0], att_r.at[h, 0], right),
            to_plane(
                far_send.at[h, bottom], far_recv.at[h, 1], att_s.at[h, 1], att_r.at[h, 1], left
            ),
        ]
        for h in range(2)
    ]
    for copy in far[0] + far[1]:
        copy.start()

    middle = width // 4
    units_of = [(gates, gate_hbm, first) for first in range(0, width, middle)]
    units_of += [(ups, up_hbm, first) for first in range(0, width, middle)]
    unit_count = len(units_of)

    def unit_view(slot, u):
        buffer, _, first = units_of[u]
        return buffer.at[slot, pl.ds(first, middle)]

    def own_unit(u, slot, kind, plane, peer, first=0, count=middle):
        buffer, hbm, base = units_of[u]
        return to_device(
            hbm.at[0, pl.ds(base + first, count)],
            buffer.at[slot, pl.ds(base + first, count)],
            w_s.at[kind, u],
            w_r.at[slot, u],
            plane,
            peer,
        )

    def onward_unit(u, slot, there, kind, plane, peer):
        return to_device(
            unit_view(slot, u), unit_view(there, u), w_s.at[kind, u], w_r.at[there, u], plane, peer
        )

    def unit_arrived(slot, u):
        own_unit(u, slot, 0, x, me).wait_recv()

    def send_rows(phase):
        def spans(marks):
            marks = (0,) + marks + (unit_count * middle,)
            first, last = marks[phase], marks[phase + 1]
            while first < last:
                count = min(last, first // middle * middle + middle) - first
                yield first // middle, first % middle, count
                first += count

        @pl.when(host)
        def _():
            for u, first, count in spans((128, 256, 384)):
                own_unit(u, 1, 0, partner, me, first, count).start()

        @pl.when(guest)
        def _():
            for u, first, count in spans((128, 256, 384)):
                own_unit(u, 2, 0, outer, sibling, first, count).start()

    send_rows(0)

    near = []
    for h in range(2):
        for copy in far[h]:
            copy.wait_recv()
        wing_at = wings[h]
        near_send[h, 0] = part[right, :, wing_at].astype(BF)
        near_send[h, 1] = part[left, :, wing_at].astype(BF)
        near_send[h, 0, top] = (part[right, top, wing_at] + far_recv[h, 0].astype(F32)).astype(BF)
        near_send[h, 1, bottom] = (part[left, bottom, wing_at] + far_recv[h, 1].astype(F32)).astype(BF)
        near.append(
            [
                to_plane(
                    near_send.at[h, 0], near_recv.at[h, 0], att_s.at[h, 2], att_r.at[h, 2], right
                ),
                to_plane(
                    near_send.at[h, 1], near_recv.at[h, 1], att_s.at[h, 3], att_r.at[h, 3], left
                ),
            ]
        )
        for copy in near[h]:
            copy.start()
    send_rows(1)

    @pl.loop(1, peers)
    def _(step):
        to_peer(ask_send, ask_recv.at[me], ask_s, ask_r, peer_at(step)).start()

    for copy in inputs[2:7]:
        copy.wait()
    spread_res, res_on = [], []
    for h in range(2):
        for copy in near[h]:
            copy.wait_recv()
        mine = pl.ds(pl.multiple_of(x * share + h * wing, wing), wing)
        attention = part[x, :, wings[h]] + near_recv[h, 0].astype(F32) + near_recv[h, 1].astype(F32)
        res[x, :, wings[h]] = (hidden_ref[:, mine].astype(F32) + attention).astype(BF)
        ours = res.at[x, :, wings[h]]
        spread_res.append(
            [
                to_plane(ours, ours, res_s.at[h, 0], res_r.at[h, 0], right),
                to_plane(ours, ours, res_s.at[h, 1], res_r.at[h, 1], left),
            ]
        )
        for copy in spread_res[h]:
            copy.start()
    send_rows(2)
    for h in range(2):
        from_left, from_right = res.at[left, top, wings[h]], res.at[right, bottom, wings[h]]
        res_on.append(
            [
                to_plane(from_left, from_left, res_s.at[h, 2], res_r.at[h, 2], right),
                to_plane(from_right, from_right, res_s.at[h, 3], res_r.at[h, 3], left),
            ]
        )
        for copy, onward in zip(spread_res[h], res_on[h]):
            copy.wait_recv()
            onward.start()
    send_rows(3)

    @pl.when(host)
    def _():
        for u in range(unit_count):
            own_unit(u, 0, 1, x, sibling).start()


    for copy in res_on[0] + res_on[1]:
        copy.wait_recv()
    square = jnp.zeros((rows, 1), F32)
    for j in range(planes):
        floats = res[j].astype(F32)
        square = square + jnp.sum(floats * floats, axis=1, keepdims=True)
    inverse = lax.rsqrt(square / width + epsilon)
    experts = peers
    logits = jnp.zeros((rows, experts), F32)
    for j in range(planes):
        cols = slice(j * share, (j + 1) * share)
        gain = gain_ref[cols].astype(F32).reshape(1, share)
        scaled = (res[j].astype(F32) * inverse * gain).astype(BF)
        normed[j] = scaled
        logits = logits + lax.dot_general(
            scaled, router_ref[:, cols], (((1,), (1,)), ((), ())), preferred_element_type=F32
        )
    named = jnp.zeros((rows, experts), jnp.bool_)
    which = iota((rows, experts), 1)
    routed = jnp.transpose(routes_ref[...].astype(F32)).astype(jnp.int32)
    for k in range(routed.shape[1]):
        named = named | (routed[:, k : k + 1] == which)
    named_f = jnp.where(named, 1.0, 0.0).astype(F32)
    powers = jnp.where(named, jnp.exp(logits), 0.0)
    weights = powers / jnp.sum(powers, axis=1, keepdims=True)
    before = jnp.where(iota((rows, rows), 1) < iota((rows, rows), 0), 1.0, 0.0).astype(BF)
    rank = dot(before, named_f.astype(BF))
    wide = jnp.where(
        iota((experts, all_slots), 1) // (2 * slots) * 2 + active == iota((experts, all_slots), 0),
        1.0,
        0.0,
    ).astype(BF)
    wide_rank = dot(rank.astype(BF), wide)
    wide_named = dot(named_f.astype(BF), wide)
    turn = (iota((rows, all_slots), 1) % (2 * slots) + lax.rem(x, 2) * 2 * slots).astype(F32)
    taken = (wide_named > 0.5) & (wide_rank == turn)
    weights_high = weights.astype(BF)
    weights_low = (weights - weights_high.astype(F32)).astype(BF)
    high[...] = jnp.where(taken, dot(weights_high, wide), 0.0).astype(BF)
    low[...] = jnp.where(taken, dot(weights_low, wide), 0.0).astype(BF)
    pick = jnp.transpose(jnp.where(taken, 1.0, 0.0).astype(F32)).astype(BF)
    for j in range(planes):
        chosen = dot(pick, normed[j]).astype(BF)
        slot_send[:, :, j * share : (j + 1) * share] = chosen.reshape(peers, slots, share)

    side = peers // 2
    for h in range(2):

        @pl.loop(1 - h, side)
        def _(k):
            peer = peer_at(2 * k + h)
            to_peer(
                slot_send.at[peer], slot_recv.at[k + h * side], slot_s, slot_r.at[h], peer
            ).start()

    own_slot = pltpu.make_async_copy(slot_send.at[me], slot_recv.at[0], own_sem.at[2 + 2 * chunks])
    own_slot.start()

    def chunk_copy(c, source, slot, kind, plane, peer):
        return to_device(
            source.at[c], downs.at[slot, c], d_s.at[kind, c], d_r.at[slot, c], plane, peer
        )

    def chunk_arrived(slot, c):
        chunk_copy(c, stage, slot, 0, x, me).wait_recv()

    @pl.when(host)
    def _():
        for c in range(chunks):
            for copy in own_down(c, downs.at[0]):
                copy.wait()
            chunk_copy(c, downs.at[0], 0, 1, x, sibling).start()
        for u in range(unit_count):
            unit_arrived(1, u)
            onward_unit(u, 1, 1, 2, x, sibling).start()
        for c in range(1):
            chunk_copy(c, downs.at[0], 1, 0, partner, me).start()

    @pl.when(guest)
    def _():
        for c in range(chunks):
            for copy in own_down(c, stage):
                copy.wait()
            chunk_copy(c, stage, 2, 0, outer, sibling).start()
        for u in range(unit_count):
            unit_arrived(2, u)
            onward_unit(u, 2, 3, 1, partner, me).start()
            onward_unit(u, 2, 2, 2, x, sibling).start()
        for c in range(chunks):
            chunk_arrived(2, c)
            chunk_copy(c, downs.at[2], 3, 1, partner, me).start()
            chunk_copy(c, downs.at[2], 2, 2, x, sibling).start()
    def pass_down(c):
        @pl.when(host)
        def _():
            chunk_arrived(1, c)
            chunk_copy(c, downs.at[1], 1, 2, x, sibling).start()

        @pl.when(guest)
        def _():
            chunk_arrived(3, c)
            chunk_copy(c, downs.at[3], 3, 3, x, sibling).start()

    everyone = pl.ds(0, peers - 1)
    side_rows = side * slots

    def take_rows(h):
        count = pl.ds(0, side - 1 if h == 0 else side)
        to_peer(slot_send.at[count], slot_recv.at[count], slot_s, slot_r.at[h], me).wait_recv()
        half_side = side // 2
        for t in range(2):
            first = h * side + t * half_side
            rows_in[first * slots : (first + half_side) * slots] = slot_recv[
                first : first + half_side
            ].reshape(half_side * slots, width)

    def activate(q, h):
        there = slice(h * side_rows, (h + 1) * side_rows)
        gate_part = dot(rows_in[there], gates[q])
        up_part = dot(rows_in[there], ups[q])
        acts[q, there] = (gate_part / (1.0 + jnp.exp(-gate_part)) * up_part).astype(BF)

    own_slot.wait()
    take_rows(0)

    @pl.when(host)
    def _():
        for copy in own:
            copy.wait()

    @pl.when(guest)
    def _():
        for u in range(unit_count):
            unit_arrived(0, u)

    activate(0, 0)

    @pl.when(host)
    def _():
        for u in range(unit_count):
            unit_arrived(2, u)

    activate(2, 0)

    @pl.when(guest)
    def _():
        for u in range(unit_count):
            unit_arrived(1, u)

    activate(1, 0)

    @pl.when(host)
    def _():
        for u in range(unit_count):
            unit_arrived(3, u)
        for c in range(1, chunks):
            chunk_copy(c, downs.at[0], 1, 0, partner, me).start()

    @pl.when(guest)
    def _():
        for u in range(unit_count):
            unit_arrived(3, u)
            onward_unit(u, 3, 3, 3, x, sibling).start()

    activate(3, 0)

    def combine(j):
        to_peer(
            back_send.at[j, everyone], back_recv.at[j, everyone], back_s.at[j], back_r.at[j], me
        ).wait_recv()
        back = back_recv[j].reshape(all_slots, 2 * piece)
        mixed = dot(high[...], back) + dot(low[...], back)
        at = j // 2
        for i in range(2):
            plane = j % 2 * 2 + i
            part_of = mixed[:, i * piece : (i + 1) * piece]
            mix_send[at, plane] = part_of.astype(BF)

            @pl.when(x == plane)
            def _():
                total[:, at * piece : (at + 1) * piece] = part_of

            @pl.when(x != plane)
            def _():
                slot = lax.rem(x - plane + planes, planes) - 1
                to_plane(
                    mix_send.at[at, plane], mix_recv.at[slot, at], mix_s, mix_r, plane
                ).start()

    def chunk_ready(c):
        @pl.when(host)
        def _():
            chunk_arrived(2, c)
            chunk_arrived(3, c)

        @pl.when(guest)
        def _():
            chunk_arrived(0, c)
            chunk_arrived(1, c)

    def produce(j, h):
        there = slice(h * side_rows, (h + 1) * side_rows)
        product = dot(acts[0, there], downs[0, j])
        for q in range(1, planes):
            product = product + dot(acts[q, there], downs[q, j])
        back_send[j, h * side : (h + 1) * side] = product.astype(BF).reshape(side, slots, 2 * piece)
        if h == 0:
            back_recv[j, me] = back_send[j, 0]

        @pl.loop(1 - h, side)
        def _(k):
            to_peer(
                back_send.at[j, k + h * side],
                back_recv.at[j, me],
                back_s.at[j],
                back_r.at[j],
                peer_at(peers - 2 * k - h),
            ).start()

    pass_down(0)
    chunk_ready(0)
    produce(0, 0)
    take_rows(1)
    for q in range(planes):
        activate(q, 1)
    produce(0, 1)
    pass_down(1)
    for c in range(1, chunks):
        if c + 1 < chunks:
            pass_down(c + 1)
        chunk_ready(c)
        produce(c, 0)
        produce(c, 1)
        if c >= 4:
            combine(c - 4)
    for c in range(chunks - 4, chunks):
        combine(c)

    three = pl.ds(0, planes - 1)
    to_plane(mix_recv.at[three], mix_recv.at[three], mix_s, mix_r, x).wait_recv()
    mixture = [total[:, j * piece : (j + 1) * piece] for j in range(planes)]
    for j in range(planes):
        for d in range(planes - 1):
            mixture[j] = mixture[j] + mix_recv[d, j].astype(F32)
    whole = jnp.concatenate(mixture, axis=1) + res[x].astype(F32)
    total[...] = whole
    squares = jnp.zeros((rows, 128), F32)
    for c in range(share // 128):
        part_of = whole[:, c * 128 : (c + 1) * 128]
        squares = squares + part_of * part_of
    row_sum = jnp.sum(jnp.transpose(squares), axis=0, keepdims=True)
    sq_send[...] = jnp.broadcast_to(row_sum, sq_send.shape)
    sq = [
        to_plane(sq_send, sq_recv.at[d - 1], sq_s.at[d - 1], sq_r.at[d - 1], lax.rem(x + d, planes))
        for d in range(1, planes)
    ]
    for copy in sq:
        copy.start()

    to_peer(ask_recv.at[everyone], ask_recv.at[everyone], ask_s, ask_r, me).wait_recv()
    ask_recv[me] = ask_send[...]
    asked = ask_recv[...].reshape(peers * 8, rows)
    lanes = iota((peers * 8, rows), 1)
    ours = asked // rows == me
    first = jnp.min(jnp.where(ours, lanes, rows), axis=1, keepdims=True)
    second = jnp.max(jnp.where(ours, lanes, -1), axis=1, keepdims=True)
    line = iota((peers * 8, 1), 0) % 8
    request = jnp.where(line < 4, first, second)
    local = jnp.sum(jnp.where(lanes == request, asked % rows, 0), axis=1, keepdims=True)
    wanted = lanes == local

    for copy in sq:
        copy.wait_recv()
    sums = sq_send[...]
    for d in range(planes - 1):
        sums = sums + sq_recv[d]
    column = jnp.transpose(jnp.broadcast_to(sums[0:1], (rows, rows)))[:, 0:1]
    scale = lax.rsqrt(column / width + epsilon)
    last_gain = last_gain_ref[...].astype(F32).reshape(1, share)
    result = (total[...] * scale * last_gain).astype(BF)
    packed = jnp.zeros((peers * 8, 128), F32)
    for c in range(4):
        chooser = jnp.where(wanted & (line % 4 == c), 1.0, 0.0).astype(BF)
        packed = packed + dot(chooser, result[:, c * 128 : (c + 1) * 128])
    pack_send[...] = packed.astype(BF).reshape(peers, 8, 128)
    pack_recv[me] = pack_send[me]

    @pl.loop(1, peers)
    def _(step):
        peer = peer_at(step)
        to_peer(pack_send.at[peer], pack_recv.at[me], pack_s, pack_r, peer).start()

    asks = jnp.broadcast_to(source_ref[...], (rows, rows))
    asks_down = jnp.transpose(asks.astype(F32)).astype(jnp.int32)
    same = (asks // rows == asks_down // rows) & (iota((rows, rows), 1) < iota((rows, rows), 0))
    later = jnp.max(jnp.where(same, 1, 0), axis=1, keepdims=True)
    place = (asks_down[:, 0:1] // rows) * 8 + later * 4
    at = iota((rows, peers * 8), 1)
    att = far + near + spread_res + res_on
    for copy in sum(att, []) + sq:
        copy.wait_send()

    @pl.when(host)
    def _():
        for kind in range(3):
            for u in range(unit_count):
                own_unit(u, 0, kind, x, me).wait_send()
            for c in range(chunks):
                chunk_copy(c, stage, 0, kind, x, me).wait_send()

    @pl.when(guest)
    def _():
        for kind in range(4):
            for u in range(unit_count):
                own_unit(u, 0, kind, x, me).wait_send()
            for c in range(chunks):
                chunk_copy(c, stage, 0, kind, x, me).wait_send()

    @pl.loop(1, peers)
    def _(step):
        to_peer(ask_send, ask_recv.at[me], ask_s, ask_r, me).wait_send()

    to_peer(slot_send.at[everyone], slot_recv.at[everyone], slot_s, slot_r, me).wait_send()
    for j in range(chunks):
        to_peer(
            back_send.at[j, everyone], back_recv.at[j, everyone], back_s.at[j], back_r.at[j], me
        ).wait_send()
    to_plane(mix_send.at[:, three], mix_recv.at[three], mix_s, mix_r, x).wait_send()
    to_peer(pack_send.at[everyone], pack_recv.at[everyone], pack_s, pack_r, me).wait_recv()
    landed = pack_recv[...].reshape(peers * 8, 128)
    for c in range(4):
        chooser = jnp.where(at == place + c, 1.0, 0.0).astype(BF)
        out_ref[:, c * 128 : (c + 1) * 128] = dot(chooser, landed).astype(BF)

    to_peer(pack_send.at[everyone], pack_recv.at[everyone], pack_s, pack_r, me).wait_send()


def solution(mesh):
    planes, peers = mesh.shape["tensor"], mesh.shape["expert"]

    def on_device(
        attn_out,
        out_proj,
        hidden_in,
        norm_gain,
        router,
        routes,
        w_gate,
        w_up,
        w_down,
        final_gain,
        source,
    ):
        rows, width = hidden_in.shape
        share = width // planes
        top = routes.shape[1]
        slots = min(rows, 2 * rows * top // peers) // planes
        units = w_gate.shape[2]
        local = pl.BlockSpec(memory_space=pltpu.VMEM)
        remote = pl.BlockSpec(memory_space=pl.ANY)
        return pl.pallas_call(
            functools.partial(layer, planes, peers),
            out_shape=jax.ShapeDtypeStruct((rows, share), BF),
            in_specs=[remote] * 11,
            out_specs=local,
            scratch_shapes=[
                VMEM((rows, share), BF),
                VMEM((share, width), BF),
                VMEM((rows, width), BF),
                VMEM((peers, width), BF),
                VMEM((top, rows), jnp.int32),
                VMEM((width,), BF),
                VMEM((share,), BF),
                VMEM((1, rows), jnp.int32),
                VMEM((planes, rows, share), F32),
                VMEM((2, rows, share // 2), BF),
                VMEM((2, 2, rows // 2, share // 2), BF),
                VMEM((2, 2, rows, share // 2), BF),
                VMEM((2, 2, rows, share // 2), BF),
                VMEM((planes, rows, share), BF),
                VMEM((planes, rows, share), BF),
                VMEM((planes, width, units), BF),
                VMEM((planes, width, units), BF),
                VMEM((planes, 2 * planes, units, share // 2), BF),
                VMEM((2 * planes, units, share // 2), BF),
                VMEM((8, rows), jnp.int32),
                VMEM((peers, 8, rows), jnp.int32),
                VMEM((peers, slots, width), BF),
                VMEM((peers, slots, width), BF),
                VMEM((peers * slots, width), BF),
                VMEM((planes, peers * slots, units), BF),
                VMEM((2 * planes, peers, slots, share // 2), BF),
                VMEM((2 * planes, peers, slots, share // 2), BF),
                VMEM((planes, planes, rows, share // planes), BF),
                VMEM((planes - 1, planes, rows, share // planes), BF),
                VMEM((rows, share), F32),
                VMEM((8, rows), F32),
                VMEM((planes - 1, 8, rows), F32),
                VMEM((peers, 8, 128), BF),
                VMEM((peers, 8, 128), BF),
                VMEM((rows, peers * slots), BF),
                VMEM((rows, peers * slots), BF),
                DMA((8,)),
                DMA((3 + 4 * planes,)),
                DMA((2, 4)),
                DMA((2, 4)),
                DMA((2, 4)),
                DMA((2, 4)),
                DMA,
                DMA,
                DMA,
                DMA((2,)),
                DMA((4, 8)),
                DMA((4, 8)),
                DMA((4, 2 * planes)),
                DMA((4, 2 * planes)),
                DMA((2 * planes,)),
                DMA((2 * planes,)),
                DMA,
                DMA,
                DMA((planes - 1,)),
                DMA((planes - 1,)),
                DMA,
                DMA,
            ],
            compiler_params=pltpu.CompilerParams(
                collective_id=0, has_side_effects=True, vmem_limit_bytes=56 * 1024 * 1024
            ),
        )(
            attn_out,
            out_proj,
            hidden_in,
            norm_gain,
            router.T,
            routes.T,
            w_gate,
            w_up,
            w_down,
            final_gain,
            source.reshape(1, rows),
        )

    placed = (
        P("expert", "tensor"),
        P("tensor", None),
        P("expert", None),
        P(),
        P(),
        P("expert", None),
        P("expert", None, "tensor"),
        P("expert", None, "tensor"),
        P("expert", "tensor", None),
        P("tensor"),
        P("expert"),
    )
    return jax.shard_map(
        on_device, mesh=mesh, in_specs=placed, out_specs=P("expert", "tensor"), check_vma=False
    )
```

```python
import functools

import jax
import jax.numpy as jnp
from jax import lax
from jax.experimental import pallas as pl
from jax.experimental.pallas import tpu as pltpu
from jax.sharding import PartitionSpec as P

epsilon = 1e-06
BF = jnp.bfloat16
F32 = jnp.float32
VMEM = pltpu.VMEM
DMA = pltpu.SemaphoreType.DMA


def dot(a, b):
    return jnp.dot(a, b, preferred_element_type=F32)


def iota(shape, dim):
    return lax.broadcasted_iota(jnp.int32, shape, dim)


def layer(
    planes,
    peers,
    attn_hbm,
    proj_hbm,
    hidden_hbm,
    gain_hbm,
    router_hbm,
    routes_hbm,
    gate_hbm,
    up_hbm,
    down_hbm,
    last_gain_hbm,
    source_hbm,
    out_ref,
    attn_ref,
    proj_ref,
    hidden_ref,
    router_ref,
    routes_ref,
    gain_ref,
    last_gain_ref,
    source_ref,
    part,
    far_send,
    far_recv,
    near_send,
    near_recv,
    res,
    normed,
    gates,
    ups,
    downs,
    stage,
    ask_send,
    ask_recv,
    slot_send,
    slot_recv,
    rows_in,
    acts,
    back_send,
    back_recv,
    mix_send,
    mix_recv,
    total,
    squares,
    pick_ref,
    taken_ref,
    pack_pick,
    out_pick,
    pack_send,
    pack_recv,
    high,
    low,
    in_sem,
    own_sem,
    att_s,
    att_r,
    res_s,
    res_r,
    ask_s,
    ask_r,
    slot_s,
    slot_r,
    w_s,
    w_r,
    d_s,
    d_r,
    back_s,
    back_r,
    mix_s,
    mix_r,
    pack_s,
    pack_r,
):
    x = lax.axis_index("tensor")
    me = lax.axis_index("expert")
    rows, share = attn_hbm.shape
    width = planes * share
    slots = slot_send.shape[1]
    all_slots = peers * slots
    hidden_units = gate_hbm.shape[2]
    right = lax.rem(x + 1, planes)
    left = lax.rem(x + planes - 1, planes)
    active = x // 2
    host = lax.rem(me, 2) == active
    guest = jnp.logical_not(host)
    partner = x + 1 - 2 * lax.rem(x, 2)
    outer = planes - 1 - x
    sibling = me + 1 - 2 * lax.rem(me, 2)

    def to_plane(src, dst, send, recv, plane):
        return pltpu.make_async_remote_copy(
            src_ref=src, dst_ref=dst, send_sem=send, recv_sem=recv, device_id={"tensor": plane}
        )

    def to_device(src, dst, send, recv, plane, peer):
        return pltpu.make_async_remote_copy(
            src_ref=src,
            dst_ref=dst,
            send_sem=send,
            recv_sem=recv,
            device_id={"tensor": plane, "expert": peer},
        )

    def to_peer(src, dst, send, recv, peer):
        return pltpu.make_async_remote_copy(
            src_ref=src, dst_ref=dst, send_sem=send, recv_sem=recv, device_id={"expert": peer}
        )

    def peer_at(step):
        return lax.rem(me + step, peers)

    barrier = pltpu.get_barrier_semaphore()
    for d in range(1, planes):
        pl.semaphore_signal(barrier, inc=1, device_id={"tensor": lax.rem(x + d, planes)})
    pl.semaphore_signal(barrier, inc=1, device_id={"tensor": outer, "expert": sibling})

    @pl.loop(1, peers)
    def _(step):
        pl.semaphore_signal(barrier, inc=1, device_id={"expert": peer_at(step)})

    inputs = [
        pltpu.make_async_copy(src, dst, in_sem.at[i])
        for i, (src, dst) in enumerate(
            [
                (attn_hbm, attn_ref),
                (proj_hbm, proj_ref),
                (hidden_hbm, hidden_ref),
                (router_hbm, router_ref),
                (routes_hbm, routes_ref),
                (gain_hbm, gain_ref),
                (last_gain_hbm, last_gain_ref),
                (source_hbm, source_ref),
            ]
        )
    ]
    for copy in inputs:
        copy.start()

    piece = share // planes
    chunks = 2 * planes
    own = [
        pltpu.make_async_copy(gate_hbm.at[0], gates.at[0], own_sem.at[0]),
        pltpu.make_async_copy(up_hbm.at[0], ups.at[0], own_sem.at[1]),
    ]

    def own_down(c, buffer):
        copies = []
        for i in range(2):
            first = (c % 2 * 2 + i) * share + c // 2 * piece
            copies.append(
                pltpu.make_async_copy(
                    down_hbm.at[0, :, pl.ds(first, piece)],
                    buffer.at[c, :, pl.ds(i * piece, piece)],
                    own_sem.at[2 + 2 * c + i],
                )
            )
        return copies

    @pl.when(host)
    def _():
        for copy in own:
            copy.start()
        for c in range(chunks):
            for copy in own_down(c, downs.at[0]):
                copy.start()

    @pl.when(guest)
    def _():
        for c in range(chunks):
            for copy in own_down(c, stage):
                copy.start()

    inputs[7].wait()
    ask_send[...] = jnp.broadcast_to(source_ref[...], ask_send.shape)
    inputs[0].wait()
    inputs[1].wait()
    for j in range(planes):
        part[j] = dot(attn_ref[...], proj_ref[:, j * share : (j + 1) * share])
    top, bottom = pl.ds(0, rows // 2), pl.ds(rows // 2, rows // 2)
    wing = share // 2
    wings = [pl.ds(0, wing), pl.ds(wing, wing)]
    for h in range(2):
        far_send[h] = part[lax.rem(x + 2, planes), :, wings[h]].astype(BF)

    pl.semaphore_wait(barrier, planes - 1 + 1 + peers - 1)

    far = [
        [
            to_plane(far_send.at[h, top], far_recv.at[h, 0], att_s.at[h, 0], att_r.at[h, 0], right),
            to_plane(
                far_send.at[h, bottom], far_recv.at[h, 1], att_s.at[h, 1], att_r.at[h, 1], left
            ),
        ]
        for h in range(2)
    ]
    for copy in far[0] + far[1]:
        copy.start()

    middle = width // 4
    units_of = [(gates, gate_hbm, first) for first in range(0, width, middle)]
    units_of += [(ups, up_hbm, first) for first in range(0, width, middle)]
    unit_count = len(units_of)

    def unit_view(slot, u):
        buffer, _, first = units_of[u]
        return buffer.at[slot, pl.ds(first, middle)]

    def own_unit(u, slot, kind, plane, peer, first=0, count=middle):
        buffer, hbm, base = units_of[u]
        return to_device(
            hbm.at[0, pl.ds(base + first, count)],
            buffer.at[slot, pl.ds(base + first, count)],
            w_s.at[kind, u],
            w_r.at[slot, u],
            plane,
            peer,
        )

    def onward_unit(u, slot, there, kind, plane, peer):
        return to_device(
            unit_view(slot, u), unit_view(there, u), w_s.at[kind, u], w_r.at[there, u], plane, peer
        )

    def unit_arrived(slot, u):
        own_unit(u, slot, 0, x, me).wait_recv()

    def send_rows(phase):
        def spans(marks):
            marks = (0,) + marks + (unit_count * middle,)
            first, last = marks[phase], marks[phase + 1]
            while first < last:
                count = min(last, first // middle * middle + middle) - first
                yield first // middle, first % middle, count
                first += count

        @pl.when(host)
        def _():
            for u, first, count in spans((128, 256, 384)):
                own_unit(u, 1, 0, partner, me, first, count).start()

        @pl.when(guest)
        def _():
            for u, first, count in spans((128, 256, 384)):
                own_unit(u, 2, 0, outer, sibling, first, count).start()

    send_rows(0)

    near = []
    for h in range(2):
        for copy in far[h]:
            copy.wait_recv()
        wing_at = wings[h]
        near_send[h, 0] = part[right, :, wing_at].astype(BF)
        near_send[h, 1] = part[left, :, wing_at].astype(BF)
        near_send[h, 0, top] = (part[right, top, wing_at] + far_recv[h, 0].astype(F32)).astype(BF)
        near_send[h, 1, bottom] = (part[left, bottom, wing_at] + far_recv[h, 1].astype(F32)).astype(BF)
        near.append(
            [
                to_plane(
                    near_send.at[h, 0], near_recv.at[h, 0], att_s.at[h, 2], att_r.at[h, 2], right
                ),
                to_plane(
                    near_send.at[h, 1], near_recv.at[h, 1], att_s.at[h, 3], att_r.at[h, 3], left
                ),
            ]
        )
        for copy in near[h]:
            copy.start()
    send_rows(1)

    @pl.loop(1, peers)
    def _(step):
        to_peer(ask_send, ask_recv.at[me], ask_s, ask_r, peer_at(step)).start()

    for copy in inputs[2:7]:
        copy.wait()

    experts = peers
    named = jnp.zeros((rows, experts), jnp.bool_)
    which = iota((rows, experts), 1)
    routed = jnp.transpose(routes_ref[...].astype(F32)).astype(jnp.int32)
    for k in range(routed.shape[1]):
        named = named | (routed[:, k : k + 1] == which)
    named_f = jnp.where(named, 1.0, 0.0).astype(F32)
    before = jnp.where(iota((rows, rows), 1) < iota((rows, rows), 0), 1.0, 0.0).astype(BF)
    rank = dot(before, named_f.astype(BF))
    wide = jnp.where(
        iota((experts, all_slots), 1) // (2 * slots) * 2 + active == iota((experts, all_slots), 0),
        1.0,
        0.0,
    ).astype(BF)
    wide_rank = dot(rank.astype(BF), wide)
    wide_named = dot(named_f.astype(BF), wide)
    turn = (iota((rows, all_slots), 1) % (2 * slots) + lax.rem(x, 2) * 2 * slots).astype(F32)
    taken_f = jnp.where((wide_named > 0.5) & (wide_rank == turn), 1.0, 0.0).astype(F32)
    taken_ref[...] = taken_f.astype(BF)
    pick_ref[...] = jnp.transpose(taken_f).astype(BF)

    spread_res, res_on = [], []
    for h in range(2):
        for copy in near[h]:
            copy.wait_recv()
        mine = pl.ds(pl.multiple_of(x * share + h * wing, wing), wing)
        attention = part[x, :, wings[h]] + near_recv[h, 0].astype(F32) + near_recv[h, 1].astype(F32)
        res[x, :, wings[h]] = (hidden_ref[:, mine].astype(F32) + attention).astype(BF)
        ours = res.at[x, :, wings[h]]
        spread_res.append(
            [
                to_plane(ours, ours, res_s.at[h, 0], res_r.at[h, 0], right),
                to_plane(ours, ours, res_s.at[h, 1], res_r.at[h, 1], left),
            ]
        )
        for copy in spread_res[h]:
            copy.start()
    send_rows(2)
    for h in range(2):
        from_left, from_right = res.at[left, top, wings[h]], res.at[right, bottom, wings[h]]
        res_on.append(
            [
                to_plane(from_left, from_left, res_s.at[h, 2], res_r.at[h, 2], right),
                to_plane(from_right, from_right, res_s.at[h, 3], res_r.at[h, 3], left),
            ]
        )
        for copy, onward in zip(spread_res[h], res_on[h]):
            copy.wait_recv()
            onward.start()
    send_rows(3)

    @pl.when(host)
    def _():
        for u in range(unit_count):
            own_unit(u, 0, 1, x, sibling).start()


    for copy in res_on[0] + res_on[1]:
        copy.wait_recv()
    square = jnp.zeros((rows, 1), F32)
    for j in range(planes):
        floats = res[j].astype(F32)
        square = square + jnp.sum(floats * floats, axis=1, keepdims=True)
    inverse = lax.rsqrt(square / width + epsilon)
    for j in range(planes):
        cols = slice(j * share, (j + 1) * share)
        gain = gain_ref[cols].astype(F32).reshape(1, share)
        normed[j] = (res[j].astype(F32) * inverse * gain).astype(BF)
    pick = pick_ref[...]
    for j in range(planes):
        chosen = dot(pick, normed[j]).astype(BF)
        slot_send[:, :, j * share : (j + 1) * share] = chosen.reshape(peers, slots, share)

    side = peers // 2
    for h in range(2):

        @pl.loop(1 - h, side)
        def _(k):
            peer = peer_at(2 * k + h)
            to_peer(
                slot_send.at[peer], slot_recv.at[k + h * side], slot_s, slot_r.at[h], peer
            ).start()

    own_slot = pltpu.make_async_copy(slot_send.at[me], slot_recv.at[0], own_sem.at[2 + 2 * chunks])
    own_slot.start()

    logits = jnp.zeros((rows, experts), F32)
    for j in range(planes):
        cols = slice(j * share, (j + 1) * share)
        logits = logits + lax.dot_general(
            normed[j], router_ref[:, cols], (((1,), (1,)), ((), ())), preferred_element_type=F32
        )
    powers = jnp.where(named, jnp.exp(logits), 0.0)
    weights = powers / jnp.sum(powers, axis=1, keepdims=True)
    weights_high = weights.astype(BF)
    weights_low = (weights - weights_high.astype(F32)).astype(BF)
    taken = taken_ref[...].astype(F32) > 0.5
    high[...] = jnp.where(taken, dot(weights_high, wide), 0.0).astype(BF)
    low[...] = jnp.where(taken, dot(weights_low, wide), 0.0).astype(BF)

    def chunk_copy(c, source, slot, kind, plane, peer):
        return to_device(
            source.at[c], downs.at[slot, c], d_s.at[kind, c], d_r.at[slot, c], plane, peer
        )

    def chunk_arrived(slot, c):
        chunk_copy(c, stage, slot, 0, x, me).wait_recv()

    @pl.when(host)
    def _():
        for c in range(chunks):
            for copy in own_down(c, downs.at[0]):
                copy.wait()
            chunk_copy(c, downs.at[0], 0, 1, x, sibling).start()
        for u in range(unit_count):
            unit_arrived(1, u)
            onward_unit(u, 1, 1, 2, x, sibling).start()
        for c in range(1):
            chunk_copy(c, downs.at[0], 1, 0, partner, me).start()

    @pl.when(guest)
    def _():
        for c in range(chunks):
            for copy in own_down(c, stage):
                copy.wait()
            chunk_copy(c, stage, 2, 0, outer, sibling).start()
        for u in range(unit_count):
            unit_arrived(2, u)
            onward_unit(u, 2, 3, 1, partner, me).start()
            onward_unit(u, 2, 2, 2, x, sibling).start()
        for c in range(chunks):
            chunk_arrived(2, c)
            chunk_copy(c, downs.at[2], 3, 1, partner, me).start()
            chunk_copy(c, downs.at[2], 2, 2, x, sibling).start()
    def pass_down(c):
        @pl.when(host)
        def _():
            chunk_arrived(1, c)
            chunk_copy(c, downs.at[1], 1, 2, x, sibling).start()

        @pl.when(guest)
        def _():
            chunk_arrived(3, c)
            chunk_copy(c, downs.at[3], 3, 3, x, sibling).start()

    everyone = pl.ds(0, peers - 1)
    side_rows = side * slots

    def take_rows(h):
        count = pl.ds(0, side - 1 if h == 0 else side)
        to_peer(slot_send.at[count], slot_recv.at[count], slot_s, slot_r.at[h], me).wait_recv()
        half_side = side // 2
        for t in range(2):
            first = h * side + t * half_side
            rows_in[first * slots : (first + half_side) * slots] = slot_recv[
                first : first + half_side
            ].reshape(half_side * slots, width)

    def activate(q, h):
        there = slice(h * side_rows, (h + 1) * side_rows)
        gate_part = dot(rows_in[there], gates[q])
        up_part = dot(rows_in[there], ups[q])
        acts[q, there] = (gate_part / (1.0 + jnp.exp(-gate_part)) * up_part).astype(BF)

    own_slot.wait()
    take_rows(0)

    @pl.when(host)
    def _():
        for copy in own:
            copy.wait()

    @pl.when(guest)
    def _():
        for u in range(unit_count):
            unit_arrived(0, u)

    activate(0, 0)

    @pl.when(host)
    def _():
        for u in range(unit_count):
            unit_arrived(2, u)

    activate(2, 0)

    @pl.when(guest)
    def _():
        for u in range(unit_count):
            unit_arrived(1, u)

    activate(1, 0)

    @pl.when(host)
    def _():
        for u in range(unit_count):
            unit_arrived(3, u)
        for c in range(1, chunks):
            chunk_copy(c, downs.at[0], 1, 0, partner, me).start()

    @pl.when(guest)
    def _():
        for u in range(unit_count):
            unit_arrived(3, u)
            onward_unit(u, 3, 3, 3, x, sibling).start()

    activate(3, 0)

    groups = [[0], [1]] + [[c, c + 1] for c in range(2, chunks - 2, 2)] + [[chunks - 2], [chunks - 1]]
    group_of = {c: g for g, group in enumerate(groups) for c in group}

    def back_copy(g, here, there, peer):
        first = groups[g][0]
        if len(groups[g]) == 1:
            src, dst = back_send.at[first // 2, here, first % 2], back_recv.at[first // 2, there, first % 2]
        else:
            src, dst = back_send.at[first // 2, here], back_recv.at[first // 2, there]
        return to_peer(src, dst, back_s.at[g], back_r.at[g], peer)

    def mix_copy(c, d):
        return to_plane(
            mix_send.at[c], mix_recv.at[c, d - 1], mix_s.at[c], mix_r.at[c], lax.rem(x + d, planes)
        )

    def combine(c):
        if groups[group_of[c]][0] == c:
            back_copy(group_of[c], everyone, everyone, me).wait_recv()
        back = back_recv[c // 2, :, c % 2].reshape(all_slots, 2 * piece)
        mixed = dot(high[...], back) + dot(low[...], back)
        mix_send[c] = mixed.astype(BF)
        total[c] = mixed
        for d in range(1, planes):
            mix_copy(c, d).start()

    three = pl.ds(0, planes - 1)

    def finish(c):
        to_plane(mix_recv.at[c, three], mix_recv.at[c, three], mix_s.at[c], mix_r.at[c], x).wait_recv()
        at = slice(c // 2 * piece, (c // 2 + 1) * piece)
        first = c % 2 * 2
        whole = total[c] + jnp.concatenate([res[first, :, at], res[first + 1, :, at]], axis=1).astype(F32)
        for d in range(planes - 1):
            whole = whole + mix_recv[c, d].astype(F32)
        total[c] = whole
        added = whole[:, :piece] * whole[:, :piece] + whole[:, piece:] * whole[:, piece:]
        squares[...] = added if c == 0 else squares[...] + added

    def chunk_ready(c):
        @pl.when(host)
        def _():
            chunk_arrived(2, c)
            chunk_arrived(3, c)

        @pl.when(guest)
        def _():
            chunk_arrived(0, c)
            chunk_arrived(1, c)

    def produce(j, h):
        there = slice(h * side_rows, (h + 1) * side_rows)
        product = dot(acts[0, there], downs[0, j])
        for q in range(1, planes):
            product = product + dot(acts[q, there], downs[q, j])
        block = product.astype(BF).reshape(side, slots, 2 * piece)
        back_send[j // 2, h * side : (h + 1) * side, j % 2] = block
        if h == 0:
            back_recv[j // 2, me, j % 2] = block[0]

    def send_back(g, h):
        @pl.loop(1 - h, side)
        def _(k):
            back_copy(g, k + h * side, me, peer_at(peers - 2 * k - h)).start()

    pass_down(0)
    chunk_ready(0)
    produce(0, 0)
    send_back(0, 0)
    take_rows(1)
    for q in range(planes):
        activate(q, 1)
    produce(0, 1)
    send_back(0, 1)
    pass_down(1)
    for c in range(1, chunks):
        if c + 1 < chunks:
            pass_down(c + 1)
        chunk_ready(c)
        g = group_of[c]
        last = groups[g][-1] == c
        for h in range(2):
            produce(c, h)
            if last:
                send_back(g, h)
        if c >= 4:
            combine(c - 4)
        if c >= 5:
            finish(c - 5)

    to_peer(ask_recv.at[everyone], ask_recv.at[everyone], ask_s, ask_r, me).wait_recv()
    ask_recv[me] = ask_send[...]
    asked = ask_recv[...].reshape(peers * 8, rows)
    lanes = iota((peers * 8, rows), 1)
    ours = asked // rows == me
    first = jnp.min(jnp.where(ours, lanes, rows), axis=1, keepdims=True)
    second = jnp.max(jnp.where(ours, lanes, -1), axis=1, keepdims=True)
    line = iota((peers * 8, 1), 0) % 8
    request = jnp.where(line < 4, first, second)
    local = jnp.sum(jnp.where(lanes == request, asked % rows, 0), axis=1, keepdims=True)
    for c in range(planes):
        chooser = (lanes == local) & (line % 4 == c)
        pack_pick[c] = jnp.where(chooser, 1.0, 0.0).astype(BF)

    asks = jnp.broadcast_to(source_ref[...], (rows, rows))
    asks_down = jnp.transpose(asks.astype(F32)).astype(jnp.int32)
    same = (asks // rows == asks_down // rows) & (iota((rows, rows), 1) < iota((rows, rows), 0))
    later = jnp.max(jnp.where(same, 1, 0), axis=1, keepdims=True)
    place = (asks_down[:, 0:1] // rows) * 8 + later * 4
    at = iota((rows, peers * 8), 1)
    for c in range(planes):
        out_pick[c] = jnp.where(at == place + c, 1.0, 0.0).astype(BF)

    for c in range(chunks - 4, chunks):
        combine(c)
        finish(c - 1)
    finish(chunks - 1)
    square = jnp.sum(squares[...], axis=1, keepdims=True)
    scale = lax.rsqrt(square / width + epsilon)
    packed = jnp.zeros((peers * 8, piece), F32)
    own_half = pl.ds(pl.multiple_of(lax.rem(x, 2) * piece, piece), piece)
    for c in range(planes):
        gain = last_gain_ref[c * piece : (c + 1) * piece].astype(F32).reshape(1, piece)
        result = (total[2 * c + active, :, own_half] * scale * gain).astype(BF)
        packed = packed + dot(pack_pick[c], result)
    pack_send[...] = packed.astype(BF).reshape(peers, 8, piece)
    pack_recv[me] = pack_send[me]

    def send_pack(step):
        peer = peer_at(step)
        to_peer(pack_send.at[peer], pack_recv.at[me], pack_s, pack_r, peer).start()

    send_pack(side)

    @pl.loop(1, side)
    def _(k):
        send_pack(side - k)
        send_pack(side + k)

    att = far + near + spread_res + res_on
    for copy in sum(att, []):
        copy.wait_send()

    @pl.when(host)
    def _():
        for kind in range(3):
            for u in range(unit_count):
                own_unit(u, 0, kind, x, me).wait_send()
            for c in range(chunks):
                chunk_copy(c, stage, 0, kind, x, me).wait_send()

    @pl.when(guest)
    def _():
        for kind in range(4):
            for u in range(unit_count):
                own_unit(u, 0, kind, x, me).wait_send()
            for c in range(chunks):
                chunk_copy(c, stage, 0, kind, x, me).wait_send()

    @pl.loop(1, peers)
    def _(step):
        to_peer(ask_send, ask_recv.at[me], ask_s, ask_r, me).wait_send()

    to_peer(slot_send.at[everyone], slot_recv.at[everyone], slot_s, slot_r, me).wait_send()
    for g in range(len(groups)):
        back_copy(g, everyone, everyone, me).wait_send()
    for c in range(chunks):
        for d in range(1, planes):
            mix_copy(c, d).wait_send()
    to_peer(pack_send.at[everyone], pack_recv.at[everyone], pack_s, pack_r, me).wait_recv()
    landed = pack_recv[...].reshape(peers * 8, 128)
    for c in range(planes):
        out_ref[:, c * piece : (c + 1) * piece] = dot(out_pick[c], landed).astype(BF)

    to_peer(pack_send.at[everyone], pack_recv.at[everyone], pack_s, pack_r, me).wait_send()


def solution(mesh):
    planes, peers = mesh.shape["tensor"], mesh.shape["expert"]

    def on_device(
        attn_out,
        out_proj,
        hidden_in,
        norm_gain,
        router,
        routes,
        w_gate,
        w_up,
        w_down,
        final_gain,
        source,
    ):
        rows, width = hidden_in.shape
        share = width // planes
        top = routes.shape[1]
        slots = min(rows, 2 * rows * top // peers) // planes
        units = w_gate.shape[2]
        local = pl.BlockSpec(memory_space=pltpu.VMEM)
        remote = pl.BlockSpec(memory_space=pl.ANY)
        return pl.pallas_call(
            functools.partial(layer, planes, peers),
            out_shape=jax.ShapeDtypeStruct((rows, share), BF),
            in_specs=[remote] * 11,
            out_specs=local,
            scratch_shapes=[
                VMEM((rows, share), BF),
                VMEM((share, width), BF),
                VMEM((rows, width), BF),
                VMEM((peers, width), BF),
                VMEM((top, rows), jnp.int32),
                VMEM((width,), BF),
                VMEM((share,), BF),
                VMEM((1, rows), jnp.int32),
                VMEM((planes, rows, share), F32),
                VMEM((2, rows, share // 2), BF),
                VMEM((2, 2, rows // 2, share // 2), BF),
                VMEM((2, 2, rows, share // 2), BF),
                VMEM((2, 2, rows, share // 2), BF),
                VMEM((planes, rows, share), BF),
                VMEM((planes, rows, share), BF),
                VMEM((planes, width, units), BF),
                VMEM((planes, width, units), BF),
                VMEM((planes, 2 * planes, units, share // 2), BF),
                VMEM((2 * planes, units, share // 2), BF),
                VMEM((8, rows), jnp.int32),
                VMEM((peers, 8, rows), jnp.int32),
                VMEM((peers, slots, width), BF),
                VMEM((peers, slots, width), BF),
                VMEM((peers * slots, width), BF),
                VMEM((planes, peers * slots, units), BF),
                VMEM((planes, peers, 2, slots, share // 2), BF),
                VMEM((planes, peers, 2, slots, share // 2), BF),
                VMEM((2 * planes, rows, share // 2), BF),
                VMEM((2 * planes, planes - 1, rows, share // 2), BF),
                VMEM((2 * planes, rows, share // 2), F32),
                VMEM((rows, share // planes), F32),
                VMEM((peers * slots, rows), BF),
                VMEM((rows, peers * slots), BF),
                VMEM((planes, peers * 8, rows), BF),
                VMEM((planes, rows, peers * 8), BF),
                VMEM((peers, 8, 128), BF),
                VMEM((peers, 8, 128), BF),
                VMEM((rows, peers * slots), BF),
                VMEM((rows, peers * slots), BF),
                DMA((8,)),
                DMA((3 + 4 * planes,)),
                DMA((2, 4)),
                DMA((2, 4)),
                DMA((2, 4)),
                DMA((2, 4)),
                DMA,
                DMA,
                DMA,
                DMA((2,)),
                DMA((4, 8)),
                DMA((4, 8)),
                DMA((4, 2 * planes)),
                DMA((4, 2 * planes)),
                DMA((2 * planes,)),
                DMA((2 * planes,)),
                DMA((2 * planes,)),
                DMA((2 * planes,)),
                DMA,
                DMA,
            ],
            compiler_params=pltpu.CompilerParams(
                collective_id=0, has_side_effects=True, vmem_limit_bytes=56 * 1024 * 1024
            ),
        )(
            attn_out,
            out_proj,
            hidden_in,
            norm_gain,
            router.T,
            routes.T,
            w_gate,
            w_up,
            w_down,
            final_gain,
            source.reshape(1, rows),
        )

    placed = (
        P("expert", "tensor"),
        P("tensor", None),
        P("expert", None),
        P(),
        P(),
        P("expert", None),
        P("expert", None, "tensor"),
        P("expert", None, "tensor"),
        P("expert", "tensor", None),
        P("tensor"),
        P("expert"),
    )
    return jax.shard_map(
        on_device, mesh=mesh, in_specs=placed, out_specs=P("expert", "tensor"), check_vma=False
    )
```

```python
import functools

import jax
import jax.numpy as jnp
from jax import lax
from jax.experimental import pallas as pl
from jax.experimental.pallas import tpu as pltpu
from jax.sharding import PartitionSpec as P

epsilon = 1e-06
BF = jnp.bfloat16
F32 = jnp.float32
VMEM = pltpu.VMEM
DMA = pltpu.SemaphoreType.DMA


def dot(a, b):
    return jnp.dot(a, b, preferred_element_type=F32)


def iota(shape, dim):
    return lax.broadcasted_iota(jnp.int32, shape, dim)


def layer(
    planes,
    peers,
    attn_hbm,
    proj_hbm,
    hidden_hbm,
    gain_hbm,
    router_hbm,
    routes_hbm,
    gate_hbm,
    up_hbm,
    down_hbm,
    last_gain_hbm,
    source_hbm,
    out_ref,
    attn_ref,
    proj_ref,
    hidden_ref,
    router_ref,
    routes_ref,
    gain_ref,
    last_gain_ref,
    source_ref,
    part,
    far_send,
    far_recv,
    near_send,
    near_recv,
    res,
    normed,
    gates,
    ups,
    downs,
    stage,
    ask_send,
    ask_recv,
    slot_send,
    slot_recv,
    rows_in,
    acts,
    back_send,
    back_recv,
    mix_send,
    mix_recv,
    total,
    squares,
    pick_ref,
    taken_ref,
    pack_pick,
    out_pick,
    out_block,
    pack_send,
    pack_recv,
    high,
    low,
    in_sem,
    own_sem,
    att_s,
    att_r,
    res_s,
    res_r,
    ask_s,
    ask_r,
    slot_s,
    slot_r,
    w_s,
    w_r,
    d_s,
    d_r,
    back_s,
    back_r,
    mix_s,
    mix_r,
    pack_s,
    pack_r,
):
    x = lax.axis_index("tensor")
    me = lax.axis_index("expert")
    rows, share = attn_hbm.shape
    width = planes * share
    slots = slot_send.shape[1]
    all_slots = peers * slots
    hidden_units = gate_hbm.shape[2]
    right = lax.rem(x + 1, planes)
    left = lax.rem(x + planes - 1, planes)
    active = x // 2
    host = lax.rem(me, 2) == active
    guest = jnp.logical_not(host)
    partner = x + 1 - 2 * lax.rem(x, 2)
    outer = planes - 1 - x
    sibling = me + 1 - 2 * lax.rem(me, 2)

    def to_plane(src, dst, send, recv, plane):
        return pltpu.make_async_remote_copy(
            src_ref=src, dst_ref=dst, send_sem=send, recv_sem=recv, device_id={"tensor": plane}
        )

    def to_device(src, dst, send, recv, plane, peer):
        return pltpu.make_async_remote_copy(
            src_ref=src,
            dst_ref=dst,
            send_sem=send,
            recv_sem=recv,
            device_id={"tensor": plane, "expert": peer},
        )

    def to_peer(src, dst, send, recv, peer):
        return pltpu.make_async_remote_copy(
            src_ref=src, dst_ref=dst, send_sem=send, recv_sem=recv, device_id={"expert": peer}
        )

    def peer_at(step):
        return lax.rem(me + step, peers)

    barrier = pltpu.get_barrier_semaphore()
    for d in range(1, planes):
        pl.semaphore_signal(barrier, inc=1, device_id={"tensor": lax.rem(x + d, planes)})
    pl.semaphore_signal(barrier, inc=1, device_id={"tensor": outer, "expert": sibling})

    @pl.loop(1, peers)
    def _(step):
        pl.semaphore_signal(barrier, inc=1, device_id={"expert": peer_at(step)})

    inputs = [
        pltpu.make_async_copy(src, dst, in_sem.at[i])
        for i, (src, dst) in enumerate(
            [
                (attn_hbm, attn_ref),
                (source_hbm, source_ref),
                (hidden_hbm, hidden_ref),
                (router_hbm, router_ref),
                (routes_hbm, routes_ref),
                (gain_hbm, gain_ref),
                (last_gain_hbm, last_gain_ref),
            ]
        )
    ]
    proj_cols = [
        pl.ds(pl.multiple_of(lax.rem(x + d, planes) * share, share), share) for d in (2, 1, 3, 0)
    ]
    proj_in = [
        pltpu.make_async_copy(proj_hbm.at[:, cols], proj_ref.at[:, cols], in_sem.at[7 + i])
        for i, cols in enumerate(proj_cols)
    ]
    inputs[0].start()
    for copy in proj_in + inputs[1:]:
        copy.start()

    piece = share // planes
    chunks = 2 * planes
    own = [
        pltpu.make_async_copy(gate_hbm.at[0], gates.at[0], own_sem.at[0]),
        pltpu.make_async_copy(up_hbm.at[0], ups.at[0], own_sem.at[1]),
    ]

    def own_down(c, buffer):
        copies = []
        for i in range(2):
            first = (c % 2 * 2 + i) * share + c // 2 * piece
            copies.append(
                pltpu.make_async_copy(
                    down_hbm.at[0, :, pl.ds(first, piece)],
                    buffer.at[c, :, pl.ds(i * piece, piece)],
                    own_sem.at[2 + 2 * c + i],
                )
            )
        return copies

    @pl.when(host)
    def _():
        for copy in own:
            copy.start()
        for c in range(chunks):
            for copy in own_down(c, downs.at[0]):
                copy.start()

    @pl.when(guest)
    def _():
        for c in range(chunks):
            for copy in own_down(c, stage):
                copy.start()

    inputs[0].wait()
    proj_in[0].wait()
    far_part = dot(attn_ref[...], proj_ref[:, proj_cols[0]])
    top, bottom = pl.ds(0, rows // 2), pl.ds(rows // 2, rows // 2)
    wing = share // 2
    wings = [pl.ds(0, wing), pl.ds(wing, wing)]
    for h in range(2):
        far_send[h] = far_part[:, h * wing : (h + 1) * wing].astype(BF)

    pl.semaphore_wait(barrier, planes - 1 + 1 + peers - 1)

    far = [
        [
            to_plane(far_send.at[h, top], far_recv.at[h, 0], att_s.at[h, 0], att_r.at[h, 0], right),
            to_plane(
                far_send.at[h, bottom], far_recv.at[h, 1], att_s.at[h, 1], att_r.at[h, 1], left
            ),
        ]
        for h in range(2)
    ]
    for copy in far[0] + far[1]:
        copy.start()
    for d, copy, cols in zip((1, 3, 0), proj_in[1:], proj_cols[1:]):
        copy.wait()
        part[lax.rem(x + d, planes)] = dot(attn_ref[...], proj_ref[:, cols])
    inputs[1].wait()
    ask_send[...] = jnp.broadcast_to(source_ref[...], ask_send.shape)

    middle = width // 4
    units_of = [(gates, gate_hbm, first) for first in range(0, width, middle)]
    units_of += [(ups, up_hbm, first) for first in range(0, width, middle)]
    unit_count = len(units_of)

    def unit_view(slot, u):
        buffer, _, first = units_of[u]
        return buffer.at[slot, pl.ds(first, middle)]

    def own_unit(u, slot, kind, plane, peer, first=0, count=middle):
        buffer, hbm, base = units_of[u]
        return to_device(
            hbm.at[0, pl.ds(base + first, count)],
            buffer.at[slot, pl.ds(base + first, count)],
            w_s.at[kind, u],
            w_r.at[slot, u],
            plane,
            peer,
        )

    def onward_unit(u, slot, there, kind, plane, peer):
        return to_device(
            unit_view(slot, u), unit_view(there, u), w_s.at[kind, u], w_r.at[there, u], plane, peer
        )

    def unit_arrived(slot, u):
        own_unit(u, slot, 0, x, me).wait_recv()

    def send_rows(phase):
        def spans(marks):
            marks = (0,) + marks + (unit_count * middle,)
            first, last = marks[phase], marks[phase + 1]
            while first < last:
                count = min(last, first // middle * middle + middle) - first
                yield first // middle, first % middle, count
                first += count

        @pl.when(host)
        def _():
            for u, first, count in spans((128, 256, 384)):
                own_unit(u, 1, 0, partner, me, first, count).start()

        @pl.when(guest)
        def _():
            for u, first, count in spans((128, 256, 384)):
                own_unit(u, 2, 0, outer, sibling, first, count).start()

    send_rows(0)

    near = []
    for h in range(2):
        for copy in far[h]:
            copy.wait_recv()
        wing_at = wings[h]
        near_send[h, 0] = part[right, :, wing_at].astype(BF)
        near_send[h, 1] = part[left, :, wing_at].astype(BF)
        near_send[h, 0, top] = (part[right, top, wing_at] + far_recv[h, 0].astype(F32)).astype(BF)
        near_send[h, 1, bottom] = (part[left, bottom, wing_at] + far_recv[h, 1].astype(F32)).astype(BF)
        near.append(
            [
                to_plane(
                    near_send.at[h, 0], near_recv.at[h, 0], att_s.at[h, 2], att_r.at[h, 2], right
                ),
                to_plane(
                    near_send.at[h, 1], near_recv.at[h, 1], att_s.at[h, 3], att_r.at[h, 3], left
                ),
            ]
        )
        for copy in near[h]:
            copy.start()
    send_rows(1)

    @pl.loop(1, peers)
    def _(step):
        to_peer(ask_send, ask_recv.at[me], ask_s, ask_r, peer_at(step)).start()

    for copy in inputs[2:7]:
        copy.wait()

    experts = peers
    named = jnp.zeros((rows, experts), jnp.bool_)
    which = iota((rows, experts), 1)
    routed = jnp.transpose(routes_ref[...].astype(F32)).astype(jnp.int32)
    for k in range(routed.shape[1]):
        named = named | (routed[:, k : k + 1] == which)
    named_f = jnp.where(named, 1.0, 0.0).astype(F32)
    before = jnp.where(iota((rows, rows), 1) < iota((rows, rows), 0), 1.0, 0.0).astype(BF)
    rank = dot(before, named_f.astype(BF))
    wide = jnp.where(
        iota((experts, all_slots), 1) // (2 * slots) * 2 + active == iota((experts, all_slots), 0),
        1.0,
        0.0,
    ).astype(BF)
    wide_rank = dot(rank.astype(BF), wide)
    wide_named = dot(named_f.astype(BF), wide)
    turn = (iota((rows, all_slots), 1) % (2 * slots) + lax.rem(x, 2) * 2 * slots).astype(F32)
    taken_f = jnp.where((wide_named > 0.5) & (wide_rank == turn), 1.0, 0.0).astype(F32)
    taken_ref[...] = taken_f.astype(BF)
    pick_ref[...] = jnp.transpose(taken_f).astype(BF)

    spread_res, res_on = [], []
    for h in range(2):
        for copy in near[h]:
            copy.wait_recv()
        mine = pl.ds(pl.multiple_of(x * share + h * wing, wing), wing)
        attention = part[x, :, wings[h]] + near_recv[h, 0].astype(F32) + near_recv[h, 1].astype(F32)
        res[x, :, wings[h]] = (hidden_ref[:, mine].astype(F32) + attention).astype(BF)
        ours = res.at[x, :, wings[h]]
        spread_res.append(
            [
                to_plane(ours, ours, res_s.at[h, 0], res_r.at[h, 0], right),
                to_plane(ours, ours, res_s.at[h, 1], res_r.at[h, 1], left),
            ]
        )
        for copy in spread_res[h]:
            copy.start()
    send_rows(2)
    for h in range(2):
        from_left, from_right = res.at[left, top, wings[h]], res.at[right, bottom, wings[h]]
        res_on.append(
            [
                to_plane(from_left, from_left, res_s.at[h, 2], res_r.at[h, 2], right),
                to_plane(from_right, from_right, res_s.at[h, 3], res_r.at[h, 3], left),
            ]
        )
        for copy, onward in zip(spread_res[h], res_on[h]):
            copy.wait_recv()
            onward.start()
    send_rows(3)

    @pl.when(host)
    def _():
        for u in range(unit_count):
            own_unit(u, 0, 1, x, sibling).start()


    for copy in res_on[0] + res_on[1]:
        copy.wait_recv()
    square = jnp.zeros((rows, 1), F32)
    for j in range(planes):
        floats = res[j].astype(F32)
        square = square + jnp.sum(floats * floats, axis=1, keepdims=True)
    inverse = lax.rsqrt(square / width + epsilon)
    for j in range(planes):
        cols = slice(j * share, (j + 1) * share)
        gain = gain_ref[cols].astype(F32).reshape(1, share)
        normed[j] = (res[j].astype(F32) * inverse * gain).astype(BF)
    pick = pick_ref[...]
    for j in range(planes):
        chosen = dot(pick, normed[j]).astype(BF)
        slot_send[:, :, j * share : (j + 1) * share] = chosen.reshape(peers, slots, share)

    side = peers // 2
    for h in range(2):

        @pl.loop(1 - h, side)
        def _(k):
            peer = peer_at(2 * k + h)
            to_peer(
                slot_send.at[peer], slot_recv.at[k + h * side], slot_s, slot_r.at[h], peer
            ).start()

    own_slot = pltpu.make_async_copy(slot_send.at[me], slot_recv.at[0], own_sem.at[2 + 2 * chunks])
    own_slot.start()

    logits = jnp.zeros((rows, experts), F32)
    for j in range(planes):
        cols = slice(j * share, (j + 1) * share)
        logits = logits + lax.dot_general(
            normed[j], router_ref[:, cols], (((1,), (1,)), ((), ())), preferred_element_type=F32
        )
    powers = jnp.where(named, jnp.exp(logits), 0.0)
    weights = powers / jnp.sum(powers, axis=1, keepdims=True)
    weights_high = weights.astype(BF)
    weights_low = (weights - weights_high.astype(F32)).astype(BF)
    taken = taken_ref[...].astype(F32) > 0.5
    high[...] = jnp.where(taken, dot(weights_high, wide), 0.0).astype(BF)
    low[...] = jnp.where(taken, dot(weights_low, wide), 0.0).astype(BF)

    def chunk_copy(c, source, slot, kind, plane, peer):
        return to_device(
            source.at[c], downs.at[slot, c], d_s.at[kind, c], d_r.at[slot, c], plane, peer
        )

    def chunk_arrived(slot, c):
        chunk_copy(c, stage, slot, 0, x, me).wait_recv()

    @pl.when(host)
    def _():
        for c in range(chunks):
            for copy in own_down(c, downs.at[0]):
                copy.wait()
            chunk_copy(c, downs.at[0], 0, 1, x, sibling).start()
        for u in range(unit_count):
            unit_arrived(1, u)
            onward_unit(u, 1, 1, 2, x, sibling).start()
        for c in range(1):
            chunk_copy(c, downs.at[0], 1, 0, partner, me).start()

    @pl.when(guest)
    def _():
        for c in range(chunks):
            for copy in own_down(c, stage):
                copy.wait()
            chunk_copy(c, stage, 2, 0, outer, sibling).start()
        for u in range(unit_count):
            unit_arrived(2, u)
            onward_unit(u, 2, 3, 1, partner, me).start()
            onward_unit(u, 2, 2, 2, x, sibling).start()
        for c in range(chunks):
            chunk_arrived(2, c)
            chunk_copy(c, downs.at[2], 3, 1, partner, me).start()
            chunk_copy(c, downs.at[2], 2, 2, x, sibling).start()
    def pass_down(c):
        @pl.when(host)
        def _():
            chunk_arrived(1, c)
            chunk_copy(c, downs.at[1], 1, 2, x, sibling).start()

        @pl.when(guest)
        def _():
            chunk_arrived(3, c)
            chunk_copy(c, downs.at[3], 3, 3, x, sibling).start()

    everyone = pl.ds(0, peers - 1)
    side_rows = side * slots

    def take_rows(h):
        count = pl.ds(0, side - 1 if h == 0 else side)
        to_peer(slot_send.at[count], slot_recv.at[count], slot_s, slot_r.at[h], me).wait_recv()
        half_side = side // 2
        for t in range(2):
            first = h * side + t * half_side
            rows_in[first * slots : (first + half_side) * slots] = slot_recv[
                first : first + half_side
            ].reshape(half_side * slots, width)

    def activate(q, h):
        there = slice(h * side_rows, (h + 1) * side_rows)
        gate_part = dot(rows_in[there], gates[q])
        up_part = dot(rows_in[there], ups[q])
        acts[q, there] = (gate_part / (1.0 + jnp.exp(-gate_part)) * up_part).astype(BF)

    own_slot.wait()
    take_rows(0)

    @pl.when(host)
    def _():
        for copy in own:
            copy.wait()

    @pl.when(guest)
    def _():
        for u in range(unit_count):
            unit_arrived(0, u)

    activate(0, 0)

    @pl.when(host)
    def _():
        for u in range(unit_count):
            unit_arrived(2, u)

    activate(2, 0)

    @pl.when(guest)
    def _():
        for u in range(unit_count):
            unit_arrived(1, u)

    activate(1, 0)

    @pl.when(host)
    def _():
        for u in range(unit_count):
            unit_arrived(3, u)
        for c in range(1, chunks):
            chunk_copy(c, downs.at[0], 1, 0, partner, me).start()

    @pl.when(guest)
    def _():
        for u in range(unit_count):
            unit_arrived(3, u)
            onward_unit(u, 3, 3, 3, x, sibling).start()

    activate(3, 0)

    groups = [[0], [1]] + [[c, c + 1] for c in range(2, chunks - 2, 2)] + [[chunks - 2]]
    groups += [[chunks - 1], [chunks - 1]]
    final = len(groups) - 2
    group_of = {c: g for g, group in enumerate(groups[:-1]) for c in group}
    both = pl.ds(0, 2 * piece)

    def columns(g):
        return pl.ds((g - final) * piece, piece) if g >= final else both

    def back_copy(g, here, there, peer):
        first = groups[g][0]
        pair, at = first // 2, first % 2
        if len(groups[g]) == 1:
            src = back_send.at[pair, here, at, :, columns(g)]
            dst = back_recv.at[pair, there, at, :, columns(g)]
        else:
            src, dst = back_send.at[pair, here], back_recv.at[pair, there]
        return to_peer(src, dst, back_s.at[g], back_r.at[g], peer)

    def mix_copy(c, d, cols=both, sem=None):
        sem = c if sem is None else sem
        return to_plane(
            mix_send.at[c, :, cols],
            mix_recv.at[c, d - 1, :, cols],
            mix_s.at[sem],
            mix_r.at[sem],
            lax.rem(x + d, planes),
        )

    def combine(c):
        if groups[group_of[c]][0] == c:
            back_copy(group_of[c], everyone, everyone, me).wait_recv()
        back = back_recv[c // 2, :, c % 2].reshape(all_slots, 2 * piece)
        mixed = dot(high[...], back) + dot(low[...], back)
        mix_send[c] = mixed.astype(BF)
        total[c] = mixed
        for d in range(1, planes):
            mix_copy(c, d).start()

    def combine_half(i):
        c = chunks - 1
        back_copy(final + i, everyone, everyone, me).wait_recv()
        there = slice(i * piece, (i + 1) * piece)
        back = back_recv[c // 2, :, c % 2, :, there].reshape(all_slots, piece)
        mixed = dot(high[...], back) + dot(low[...], back)
        mix_send[c, :, there] = mixed.astype(BF)
        total[c, :, there] = mixed
        for d in range(1, planes):
            mix_copy(c, d, columns(final + i), c + i).start()

    three = pl.ds(0, planes - 1)

    def finish(c):
        to_plane(mix_recv.at[c, three], mix_recv.at[c, three], mix_s.at[c], mix_r.at[c], x).wait_recv()
        at = slice(c // 2 * piece, (c // 2 + 1) * piece)
        first = c % 2 * 2
        whole = total[c] + jnp.concatenate([res[first, :, at], res[first + 1, :, at]], axis=1).astype(F32)
        for d in range(planes - 1):
            whole = whole + mix_recv[c, d].astype(F32)
        total[c] = whole
        added = whole[:, :piece] * whole[:, :piece] + whole[:, piece:] * whole[:, piece:]
        squares[...] = added if c == 0 else squares[...] + added

    def finish_half(i):
        c = chunks - 1
        there = slice(i * piece, (i + 1) * piece)
        cols = columns(final + i)
        landing = mix_recv.at[c, three, :, cols]
        to_plane(landing, landing, mix_s.at[c + i], mix_r.at[c + i], x).wait_recv()
        whole = total[c, :, there] + res[c % 2 * 2 + i, :, c // 2 * piece : (c // 2 + 1) * piece].astype(F32)
        for d in range(planes - 1):
            whole = whole + mix_recv[c, d, :, there].astype(F32)
        total[c, :, there] = whole
        squares[...] = squares[...] + whole * whole

    def chunk_ready(c):
        @pl.when(host)
        def _():
            chunk_arrived(2, c)
            chunk_arrived(3, c)

        @pl.when(guest)
        def _():
            chunk_arrived(0, c)
            chunk_arrived(1, c)

    def produce(j, h):
        there = slice(h * side_rows, (h + 1) * side_rows)
        product = dot(acts[0, there], downs[0, j])
        for q in range(1, planes):
            product = product + dot(acts[q, there], downs[q, j])
        block = product.astype(BF).reshape(side, slots, 2 * piece)
        back_send[j // 2, h * side : (h + 1) * side, j % 2] = block
        if h == 0:
            back_recv[j // 2, me, j % 2] = block[0]

    def send_back(g, h):
        @pl.loop(1 - h, side)
        def _(k):
            back_copy(g, k + h * side, me, peer_at(peers - 2 * k - h)).start()

    pass_down(0)
    chunk_ready(0)
    produce(0, 0)
    send_back(0, 0)
    take_rows(1)
    for q in range(planes):
        activate(q, 1)
    pass_down(1)
    produce(0, 1)
    send_back(0, 1)
    for c in range(1, chunks):
        if 1 < c < chunks - 1:
            pass_down(c + 1)
        chunk_ready(c)
        g = group_of[c]
        last = groups[g][-1] == c
        for h in range(2):
            produce(c, h)
            if last:
                send_back(g, h)
        if c == chunks - 1:
            for h in range(2):
                send_back(g + 1, h)
        if c == 1:
            pass_down(2)
        if c >= 4:
            combine(c - 4)
        if c >= 5:
            finish(c - 5)

    to_peer(ask_recv.at[everyone], ask_recv.at[everyone], ask_s, ask_r, me).wait_recv()
    ask_recv[me] = ask_send[...]
    asked = ask_recv[...].reshape(peers * 8, rows)
    lanes = iota((peers * 8, rows), 1)
    ours = asked // rows == me
    first = jnp.min(jnp.where(ours, lanes, rows), axis=1, keepdims=True)
    second = jnp.max(jnp.where(ours, lanes, -1), axis=1, keepdims=True)
    line = iota((peers * 8, 1), 0) % 8
    request = jnp.where(line < 4, first, second)
    local = jnp.sum(jnp.where(lanes == request, asked % rows, 0), axis=1, keepdims=True)
    for c in range(planes):
        chooser = (lanes == local) & (line % 4 == c)
        pack_pick[c] = jnp.where(chooser, 1.0, 0.0).astype(BF)

    asks = jnp.broadcast_to(source_ref[...], (rows, rows))
    asks_down = jnp.transpose(asks.astype(F32)).astype(jnp.int32)
    same = (asks // rows == asks_down // rows) & (iota((rows, rows), 1) < iota((rows, rows), 0))
    later = jnp.max(jnp.where(same, 1, 0), axis=1, keepdims=True)
    place = (asks_down[:, 0:1] // rows) * 8 + later * 4
    at = iota((rows, peers * 8), 1)
    for c in range(planes):
        out_pick[c] = jnp.where(at == place + c, 1.0, 0.0).astype(BF)

    for c in range(chunks - 4, chunks - 1):
        combine(c)
        finish(c - 1)
    combine_half(0)
    finish(chunks - 2)
    combine_half(1)
    finish_half(0)
    finish_half(1)
    square = jnp.sum(squares[...], axis=1, keepdims=True)
    scale = lax.rsqrt(square / width + epsilon)
    packed = jnp.zeros((peers * 8, piece), F32)
    own_half = pl.ds(pl.multiple_of(lax.rem(x, 2) * piece, piece), piece)
    for c in range(planes):
        gain = last_gain_ref[c * piece : (c + 1) * piece].astype(F32).reshape(1, piece)
        result = (total[2 * c + active, :, own_half] * scale * gain).astype(BF)
        packed = packed + dot(pack_pick[c], result)
    pack_send[...] = packed.astype(BF).reshape(peers, 8, piece)
    pack_recv[me] = pack_send[me]

    def send_pack(step):
        peer = peer_at(step)
        to_peer(pack_send.at[peer], pack_recv.at[me], pack_s, pack_r, peer).start()

    send_pack(side)

    @pl.loop(1, side)
    def _(k):
        send_pack(side - k)
        send_pack(side + k)

    att = far + near + spread_res + res_on
    for copy in sum(att, []):
        copy.wait_send()

    @pl.when(host)
    def _():
        for kind in range(3):
            for u in range(unit_count):
                own_unit(u, 0, kind, x, me).wait_send()
            for c in range(chunks):
                chunk_copy(c, stage, 0, kind, x, me).wait_send()

    @pl.when(guest)
    def _():
        for kind in range(4):
            for u in range(unit_count):
                own_unit(u, 0, kind, x, me).wait_send()
            for c in range(chunks):
                chunk_copy(c, stage, 0, kind, x, me).wait_send()

    @pl.loop(1, peers)
    def _(step):
        to_peer(ask_send, ask_recv.at[me], ask_s, ask_r, me).wait_send()

    to_peer(slot_send.at[everyone], slot_recv.at[everyone], slot_s, slot_r, me).wait_send()
    for g in range(len(groups)):
        back_copy(g, everyone, everyone, me).wait_send()
    for d in range(1, planes):
        for c in range(chunks - 1):
            mix_copy(c, d).wait_send()
        for i in range(2):
            mix_copy(chunks - 1, d, columns(final + i), chunks - 1 + i).wait_send()
    to_peer(pack_send.at[everyone], pack_recv.at[everyone], pack_s, pack_r, me).wait_recv()
    landed = pack_recv[...].reshape(peers * 8, 128)
    outs = []
    for c in range(planes):
        cols = pl.ds(c * piece, piece)
        out_block[:, c * piece : (c + 1) * piece] = dot(out_pick[c], landed).astype(BF)
        outs.append(pltpu.make_async_copy(out_block.at[:, cols], out_ref.at[:, cols], in_sem.at[c]))
        outs[c].start()
    for copy in outs:
        copy.wait()

    to_peer(pack_send.at[everyone], pack_recv.at[everyone], pack_s, pack_r, me).wait_send()


def solution(mesh):
    planes, peers = mesh.shape["tensor"], mesh.shape["expert"]

    def on_device(
        attn_out,
        out_proj,
        hidden_in,
        norm_gain,
        router,
        routes,
        w_gate,
        w_up,
        w_down,
        final_gain,
        source,
    ):
        rows, width = hidden_in.shape
        share = width // planes
        top = routes.shape[1]
        slots = min(rows, 2 * rows * top // peers) // planes
        units = w_gate.shape[2]
        remote = pl.BlockSpec(memory_space=pl.ANY)
        return pl.pallas_call(
            functools.partial(layer, planes, peers),
            out_shape=jax.ShapeDtypeStruct((rows, share), BF),
            in_specs=[remote] * 11,
            out_specs=remote,
            scratch_shapes=[
                VMEM((rows, share), BF),
                VMEM((share, width), BF),
                VMEM((rows, width), BF),
                VMEM((peers, width), BF),
                VMEM((top, rows), jnp.int32),
                VMEM((width,), BF),
                VMEM((share,), BF),
                VMEM((1, rows), jnp.int32),
                VMEM((planes, rows, share), F32),
                VMEM((2, rows, share // 2), BF),
                VMEM((2, 2, rows // 2, share // 2), BF),
                VMEM((2, 2, rows, share // 2), BF),
                VMEM((2, 2, rows, share // 2), BF),
                VMEM((planes, rows, share), BF),
                VMEM((planes, rows, share), BF),
                VMEM((planes, width, units), BF),
                VMEM((planes, width, units), BF),
                VMEM((planes, 2 * planes, units, share // 2), BF),
                VMEM((2 * planes, units, share // 2), BF),
                VMEM((8, rows), jnp.int32),
                VMEM((peers, 8, rows), jnp.int32),
                VMEM((peers, slots, width), BF),
                VMEM((peers, slots, width), BF),
                VMEM((peers * slots, width), BF),
                VMEM((planes, peers * slots, units), BF),
                VMEM((planes, peers, 2, slots, share // 2), BF),
                VMEM((planes, peers, 2, slots, share // 2), BF),
                VMEM((2 * planes, rows, share // 2), BF),
                VMEM((2 * planes, planes - 1, rows, share // 2), BF),
                VMEM((2 * planes, rows, share // 2), F32),
                VMEM((rows, share // planes), F32),
                VMEM((peers * slots, rows), BF),
                VMEM((rows, peers * slots), BF),
                VMEM((planes, peers * 8, rows), BF),
                VMEM((planes, rows, peers * 8), BF),
                VMEM((rows, share), BF),
                VMEM((peers, 8, 128), BF),
                VMEM((peers, 8, 128), BF),
                VMEM((rows, peers * slots), BF),
                VMEM((rows, peers * slots), BF),
                DMA((7 + planes,)),
                DMA((3 + 4 * planes,)),
                DMA((2, 4)),
                DMA((2, 4)),
                DMA((2, 4)),
                DMA((2, 4)),
                DMA,
                DMA,
                DMA,
                DMA((2,)),
                DMA((4, 8)),
                DMA((4, 8)),
                DMA((4, 2 * planes)),
                DMA((4, 2 * planes)),
                DMA((2 * planes,)),
                DMA((2 * planes,)),
                DMA((2 * planes + 1,)),
                DMA((2 * planes + 1,)),
                DMA,
                DMA,
            ],
            compiler_params=pltpu.CompilerParams(
                collective_id=0, has_side_effects=True, vmem_limit_bytes=56 * 1024 * 1024
            ),
        )(
            attn_out,
            out_proj,
            hidden_in,
            norm_gain,
            router.T,
            routes.T,
            w_gate,
            w_up,
            w_down,
            final_gain,
            source.reshape(1, rows),
        )

    placed = (
        P("expert", "tensor"),
        P("tensor", None),
        P("expert", None),
        P(),
        P(),
        P("expert", None),
        P("expert", None, "tensor"),
        P("expert", None, "tensor"),
        P("expert", "tensor", None),
        P("tensor"),
        P("expert"),
    )
    return jax.shard_map(
        on_device, mesh=mesh, in_specs=placed, out_specs=P("expert", "tensor"), check_vma=False
    )
```

```python
import functools

import jax
import jax.numpy as jnp
from jax import lax
from jax.experimental import pallas as pl
from jax.experimental.pallas import tpu as pltpu
from jax.sharding import PartitionSpec as P

epsilon = 1e-06
BF = jnp.bfloat16
F32 = jnp.float32
VMEM = pltpu.VMEM
DMA = pltpu.SemaphoreType.DMA


def dot(a, b):
    return jnp.dot(a, b, preferred_element_type=F32)


def iota(shape, dim):
    return lax.broadcasted_iota(jnp.int32, shape, dim)


def layer(
    planes,
    peers,
    attn_hbm,
    proj_hbm,
    hidden_hbm,
    gain_hbm,
    router_hbm,
    routes_hbm,
    gate_hbm,
    up_hbm,
    down_hbm,
    last_gain_hbm,
    source_hbm,
    out_ref,
    attn_ref,
    proj_ref,
    hidden_ref,
    router_ref,
    routes_ref,
    gain_ref,
    last_gain_ref,
    source_ref,
    part,
    far_send,
    far_recv,
    near_send,
    near_recv,
    res,
    normed,
    gates,
    ups,
    downs,
    stage,
    ask_send,
    ask_recv,
    slot_send,
    slot_recv,
    rows_in,
    acts,
    back_send,
    back_recv,
    mix_send,
    mix_recv,
    total,
    squares,
    pick_ref,
    taken_ref,
    pack_pick,
    out_pick,
    out_block,
    pack_send,
    pack_recv,
    high,
    low,
    in_sem,
    own_sem,
    att_s,
    att_r,
    res_s,
    res_r,
    ask_s,
    ask_r,
    slot_s,
    slot_r,
    w_s,
    w_r,
    d_s,
    d_r,
    back_s,
    back_r,
    mix_s,
    mix_r,
    pack_s,
    pack_r,
):
    x = lax.axis_index("tensor")
    me = lax.axis_index("expert")
    rows, share = attn_hbm.shape
    width = planes * share
    slots = slot_send.shape[1]
    all_slots = peers * slots
    hidden_units = gate_hbm.shape[2]
    right = lax.rem(x + 1, planes)
    left = lax.rem(x + planes - 1, planes)
    active = x // 2
    host = lax.rem(me, 2) == active
    guest = jnp.logical_not(host)
    partner = x + 1 - 2 * lax.rem(x, 2)
    outer = planes - 1 - x
    sibling = me + 1 - 2 * lax.rem(me, 2)

    def to_plane(src, dst, send, recv, plane):
        return pltpu.make_async_remote_copy(
            src_ref=src, dst_ref=dst, send_sem=send, recv_sem=recv, device_id={"tensor": plane}
        )

    def to_device(src, dst, send, recv, plane, peer):
        return pltpu.make_async_remote_copy(
            src_ref=src,
            dst_ref=dst,
            send_sem=send,
            recv_sem=recv,
            device_id={"tensor": plane, "expert": peer},
        )

    def to_peer(src, dst, send, recv, peer):
        return pltpu.make_async_remote_copy(
            src_ref=src, dst_ref=dst, send_sem=send, recv_sem=recv, device_id={"expert": peer}
        )

    def peer_at(step):
        return lax.rem(me + step, peers)

    barrier = pltpu.get_barrier_semaphore()
    for d in range(1, planes):
        pl.semaphore_signal(barrier, inc=1, device_id={"tensor": lax.rem(x + d, planes)})
    pl.semaphore_signal(barrier, inc=1, device_id={"tensor": outer, "expert": sibling})

    @pl.loop(1, peers)
    def _(step):
        pl.semaphore_signal(barrier, inc=1, device_id={"expert": peer_at(step)})

    inputs = [
        pltpu.make_async_copy(src, dst, in_sem.at[i])
        for i, (src, dst) in enumerate(
            [
                (attn_hbm, attn_ref),
                (source_hbm, source_ref),
                (hidden_hbm, hidden_ref),
                (router_hbm, router_ref),
                (routes_hbm, routes_ref),
                (gain_hbm, gain_ref),
                (last_gain_hbm, last_gain_ref),
            ]
        )
    ]
    proj_cols = [
        pl.ds(pl.multiple_of(lax.rem(x + d, planes) * share, share), share) for d in (2, 1, 3, 0)
    ]
    proj_in = [
        pltpu.make_async_copy(proj_hbm.at[:, cols], proj_ref.at[:, cols], in_sem.at[7 + i])
        for i, cols in enumerate(proj_cols)
    ]
    inputs[0].start()
    for copy in proj_in + inputs[1:]:
        copy.start()

    piece = share // planes
    chunks = 2 * planes
    own = [
        pltpu.make_async_copy(gate_hbm.at[0], gates.at[0], own_sem.at[0]),
        pltpu.make_async_copy(up_hbm.at[0], ups.at[0], own_sem.at[1]),
    ]

    def own_down(c, buffer):
        copies = []
        for i in range(2):
            first = (c % 2 * 2 + i) * share + c // 2 * piece
            copies.append(
                pltpu.make_async_copy(
                    down_hbm.at[0, :, pl.ds(first, piece)],
                    buffer.at[c, :, pl.ds(i * piece, piece)],
                    own_sem.at[2 + 2 * c + i],
                )
            )
        return copies

    @pl.when(host)
    def _():
        for copy in own:
            copy.start()
        for c in range(chunks):
            for copy in own_down(c, downs.at[0]):
                copy.start()

    @pl.when(guest)
    def _():
        for c in range(chunks):
            for copy in own_down(c, stage):
                copy.start()

    inputs[0].wait()
    proj_in[0].wait()
    far_part = dot(attn_ref[...], proj_ref[:, proj_cols[0]])
    top, bottom = pl.ds(0, rows // 2), pl.ds(rows // 2, rows // 2)
    wing = share // 2
    wings = [pl.ds(0, wing), pl.ds(wing, wing)]
    for h in range(2):
        far_send[h] = far_part[:, h * wing : (h + 1) * wing].astype(BF)

    pl.semaphore_wait(barrier, planes - 1 + 1 + peers - 1)

    far = [
        [
            to_plane(far_send.at[h, top], far_recv.at[h, 0], att_s.at[h, 0], att_r.at[h, 0], right),
            to_plane(
                far_send.at[h, bottom], far_recv.at[h, 1], att_s.at[h, 1], att_r.at[h, 1], left
            ),
        ]
        for h in range(2)
    ]
    for copy in far[0] + far[1]:
        copy.start()
    for d, copy, cols in zip((1, 3, 0), proj_in[1:], proj_cols[1:]):
        copy.wait()
        part[lax.rem(x + d, planes)] = dot(attn_ref[...], proj_ref[:, cols])
    inputs[1].wait()
    ask_send[...] = jnp.broadcast_to(source_ref[...], ask_send.shape)

    middle = width // 4
    units_of = [(gates, gate_hbm, first) for first in range(0, width, middle)]
    units_of += [(ups, up_hbm, first) for first in range(0, width, middle)]
    unit_count = len(units_of)

    def unit_view(slot, u):
        buffer, _, first = units_of[u]
        return buffer.at[slot, pl.ds(first, middle)]

    def own_unit(u, slot, kind, plane, peer, first=0, count=middle):
        buffer, hbm, base = units_of[u]
        return to_device(
            hbm.at[0, pl.ds(base + first, count)],
            buffer.at[slot, pl.ds(base + first, count)],
            w_s,
            w_r.at[slot, u],
            plane,
            peer,
        )

    def onward_unit(u, slot, there, kind, plane, peer):
        return to_device(
            unit_view(slot, u), unit_view(there, u), w_s, w_r.at[there, u], plane, peer
        )

    def unit_arrived(slot, u):
        own_unit(u, slot, 0, x, me).wait_recv()

    def send_rows(phase):
        def spans(marks):
            marks = (0,) + marks + (unit_count * middle,)
            first, last = marks[phase], marks[phase + 1]
            while first < last:
                count = min(last, first // middle * middle + middle) - first
                yield first // middle, first % middle, count
                first += count

        @pl.when(host)
        def _():
            for u, first, count in spans((128, 256, 384)):
                own_unit(u, 1, 0, partner, me, first, count).start()

        @pl.when(guest)
        def _():
            for u, first, count in spans((128, 256, 384)):
                own_unit(u, 2, 0, outer, sibling, first, count).start()

    send_rows(0)

    near = []
    for h in range(2):
        for copy in far[h]:
            copy.wait_recv()
        wing_at = wings[h]
        near_send[h, 0] = part[right, :, wing_at].astype(BF)
        near_send[h, 1] = part[left, :, wing_at].astype(BF)
        near_send[h, 0, top] = (part[right, top, wing_at] + far_recv[h, 0].astype(F32)).astype(BF)
        near_send[h, 1, bottom] = (part[left, bottom, wing_at] + far_recv[h, 1].astype(F32)).astype(BF)
        near.append(
            [
                to_plane(
                    near_send.at[h, 0], near_recv.at[h, 0], att_s.at[h, 2], att_r.at[h, 2], right
                ),
                to_plane(
                    near_send.at[h, 1], near_recv.at[h, 1], att_s.at[h, 3], att_r.at[h, 3], left
                ),
            ]
        )
        for copy in near[h]:
            copy.start()
    send_rows(1)

    @pl.loop(1, peers)
    def _(step):
        to_peer(ask_send, ask_recv.at[me], ask_s, ask_r, peer_at(step)).start()

    for copy in inputs[2:7]:
        copy.wait()

    experts = peers
    named = jnp.zeros((rows, experts), jnp.bool_)
    which = iota((rows, experts), 1)
    routed = jnp.transpose(routes_ref[...].astype(F32)).astype(jnp.int32)
    for k in range(routed.shape[1]):
        named = named | (routed[:, k : k + 1] == which)
    named_f = jnp.where(named, 1.0, 0.0).astype(F32)
    before = jnp.where(iota((rows, rows), 1) < iota((rows, rows), 0), 1.0, 0.0).astype(BF)
    rank = dot(before, named_f.astype(BF))
    wide = jnp.where(
        iota((experts, all_slots), 1) // (2 * slots) * 2 + active == iota((experts, all_slots), 0),
        1.0,
        0.0,
    ).astype(BF)
    wide_rank = dot(rank.astype(BF), wide)
    wide_named = dot(named_f.astype(BF), wide)
    turn = (iota((rows, all_slots), 1) % (2 * slots) + lax.rem(x, 2) * 2 * slots).astype(F32)
    taken_f = jnp.where((wide_named > 0.5) & (wide_rank == turn), 1.0, 0.0).astype(F32)
    taken_ref[...] = taken_f.astype(BF)
    pick_ref[...] = jnp.transpose(taken_f).astype(BF)

    spread_res, res_on = [], []
    for h in range(2):
        for copy in near[h]:
            copy.wait_recv()
        mine = pl.ds(pl.multiple_of(x * share + h * wing, wing), wing)
        attention = part[x, :, wings[h]] + near_recv[h, 0].astype(F32) + near_recv[h, 1].astype(F32)
        res[x, :, wings[h]] = (hidden_ref[:, mine].astype(F32) + attention).astype(BF)
        ours = res.at[x, :, wings[h]]
        spread_res.append(
            [
                to_plane(ours, ours, res_s.at[h, 0], res_r.at[h, 0], right),
                to_plane(ours, ours, res_s.at[h, 1], res_r.at[h, 1], left),
            ]
        )
        for copy in spread_res[h]:
            copy.start()
    send_rows(2)
    for h in range(2):
        from_left, from_right = res.at[left, top, wings[h]], res.at[right, bottom, wings[h]]
        res_on.append(
            [
                to_plane(from_left, from_left, res_s.at[h, 2], res_r.at[h, 2], right),
                to_plane(from_right, from_right, res_s.at[h, 3], res_r.at[h, 3], left),
            ]
        )
        for copy, onward in zip(spread_res[h], res_on[h]):
            copy.wait_recv()
            onward.start()
    send_rows(3)

    @pl.when(host)
    def _():
        for u in range(unit_count):
            own_unit(u, 0, 1, x, sibling).start()


    for copy in res_on[0] + res_on[1]:
        copy.wait_recv()
    square = jnp.zeros((rows, 1), F32)
    for j in range(planes):
        floats = res[j].astype(F32)
        square = square + jnp.sum(floats * floats, axis=1, keepdims=True)
    inverse = lax.rsqrt(square / width + epsilon)
    for j in range(planes):
        cols = slice(j * share, (j + 1) * share)
        gain = gain_ref[cols].astype(F32).reshape(1, share)
        normed[j] = (res[j].astype(F32) * inverse * gain).astype(BF)
    pick = pick_ref[...]
    for j in range(planes):
        chosen = dot(pick, normed[j]).astype(BF)
        slot_send[:, :, j * share : (j + 1) * share] = chosen.reshape(peers, slots, share)

    side = peers // 2
    for h in range(2):

        @pl.loop(1 - h, side)
        def _(k):
            peer = peer_at(2 * k + h)
            to_peer(
                slot_send.at[peer], slot_recv.at[k + h * side], slot_s, slot_r.at[h], peer
            ).start()

    own_slot = pltpu.make_async_copy(slot_send.at[me], slot_recv.at[0], own_sem.at[2 + 2 * chunks])
    own_slot.start()

    logits = jnp.zeros((rows, experts), F32)
    for j in range(planes):
        cols = slice(j * share, (j + 1) * share)
        logits = logits + lax.dot_general(
            normed[j], router_ref[:, cols], (((1,), (1,)), ((), ())), preferred_element_type=F32
        )
    powers = jnp.where(named, jnp.exp(logits), 0.0)
    weights = powers / jnp.sum(powers, axis=1, keepdims=True)
    weights_high = weights.astype(BF)
    weights_low = (weights - weights_high.astype(F32)).astype(BF)
    taken = taken_ref[...].astype(F32) > 0.5
    high[...] = jnp.where(taken, dot(weights_high, wide), 0.0).astype(BF)
    low[...] = jnp.where(taken, dot(weights_low, wide), 0.0).astype(BF)

    def chunk_copy(c, source, slot, kind, plane, peer):
        return to_device(
            source.at[c], downs.at[slot, c], d_s, d_r.at[slot, c], plane, peer
        )

    def chunk_arrived(slot, c):
        chunk_copy(c, stage, slot, 0, x, me).wait_recv()

    @pl.when(host)
    def _():
        for c in range(chunks):
            for copy in own_down(c, downs.at[0]):
                copy.wait()
            chunk_copy(c, downs.at[0], 0, 1, x, sibling).start()
        for u in range(unit_count):
            unit_arrived(1, u)
            onward_unit(u, 1, 1, 2, x, sibling).start()
        for c in range(1):
            chunk_copy(c, downs.at[0], 1, 0, partner, me).start()

    @pl.when(guest)
    def _():
        for c in range(chunks):
            for copy in own_down(c, stage):
                copy.wait()
            chunk_copy(c, stage, 2, 0, outer, sibling).start()
        for u in range(unit_count):
            unit_arrived(2, u)
            onward_unit(u, 2, 3, 1, partner, me).start()
            onward_unit(u, 2, 2, 2, x, sibling).start()
        for c in range(chunks):
            chunk_arrived(2, c)
            chunk_copy(c, downs.at[2], 3, 1, partner, me).start()
            chunk_copy(c, downs.at[2], 2, 2, x, sibling).start()
    def pass_down(c):
        @pl.when(host)
        def _():
            chunk_arrived(1, c)
            chunk_copy(c, downs.at[1], 1, 2, x, sibling).start()

        @pl.when(guest)
        def _():
            chunk_arrived(3, c)
            chunk_copy(c, downs.at[3], 3, 3, x, sibling).start()

    everyone = pl.ds(0, peers - 1)
    side_rows = side * slots

    def take_rows(h):
        count = pl.ds(0, side - 1 if h == 0 else side)
        to_peer(slot_send.at[count], slot_recv.at[count], slot_s, slot_r.at[h], me).wait_recv()
        half_side = side // 2
        for t in range(2):
            first = h * side + t * half_side
            rows_in[first * slots : (first + half_side) * slots] = slot_recv[
                first : first + half_side
            ].reshape(half_side * slots, width)

    def activate(q, h):
        there = slice(h * side_rows, (h + 1) * side_rows)
        gate_part = dot(rows_in[there], gates[q])
        up_part = dot(rows_in[there], ups[q])
        acts[q, there] = (gate_part / (1.0 + jnp.exp(-gate_part)) * up_part).astype(BF)

    own_slot.wait()
    take_rows(0)

    @pl.when(host)
    def _():
        for copy in own:
            copy.wait()

    @pl.when(guest)
    def _():
        for u in range(unit_count):
            unit_arrived(0, u)

    activate(0, 0)

    @pl.when(host)
    def _():
        for u in range(unit_count):
            unit_arrived(2, u)

    activate(2, 0)

    @pl.when(guest)
    def _():
        for u in range(unit_count):
            unit_arrived(1, u)

    activate(1, 0)

    @pl.when(host)
    def _():
        for u in range(unit_count):
            unit_arrived(3, u)
        for c in range(1, chunks):
            chunk_copy(c, downs.at[0], 1, 0, partner, me).start()

    @pl.when(guest)
    def _():
        for u in range(unit_count):
            unit_arrived(3, u)
            onward_unit(u, 3, 3, 3, x, sibling).start()

    activate(3, 0)

    groups = [[0], [1]] + [[c, c + 1] for c in range(2, chunks - 2, 2)] + [[chunks - 2]]
    groups += [[chunks - 1], [chunks - 1]]
    final = len(groups) - 2
    group_of = {c: g for g, group in enumerate(groups[:-1]) for c in group}
    both = pl.ds(0, 2 * piece)

    def columns(g):
        return pl.ds((g - final) * piece, piece) if g >= final else both

    def back_copy(g, here, there, peer):
        first = groups[g][0]
        pair, at = first // 2, first % 2
        if len(groups[g]) == 1:
            src = back_send.at[pair, here, at, :, columns(g)]
            dst = back_recv.at[pair, there, at, :, columns(g)]
        else:
            src, dst = back_send.at[pair, here], back_recv.at[pair, there]
        return to_peer(src, dst, back_s.at[g], back_r.at[g], peer)

    def mix_copy(c, d, cols=both, sem=None):
        sem = c if sem is None else sem
        return to_plane(
            mix_send.at[c, :, cols],
            mix_recv.at[c, d - 1, :, cols],
            mix_s,
            mix_r.at[sem],
            lax.rem(x + d, planes),
        )

    def combine(c):
        if groups[group_of[c]][0] == c:
            back_copy(group_of[c], everyone, everyone, me).wait_recv()
        back = back_recv[c // 2, :, c % 2].reshape(all_slots, 2 * piece)
        mixed = dot(high[...], back) + dot(low[...], back)
        mix_send[c] = mixed.astype(BF)
        total[c] = mixed
        for d in range(1, planes):
            mix_copy(c, d).start()

    def combine_half(i):
        c = chunks - 1
        back_copy(final + i, everyone, everyone, me).wait_recv()
        there = slice(i * piece, (i + 1) * piece)
        back = back_recv[c // 2, :, c % 2, :, there].reshape(all_slots, piece)
        mixed = dot(high[...], back) + dot(low[...], back)
        mix_send[c, :, there] = mixed.astype(BF)
        total[c, :, there] = mixed
        for d in range(1, planes):
            mix_copy(c, d, columns(final + i), c + i).start()

    three = pl.ds(0, planes - 1)

    def finish(c):
        to_plane(mix_recv.at[c, three], mix_recv.at[c, three], mix_s, mix_r.at[c], x).wait_recv()
        at = slice(c // 2 * piece, (c // 2 + 1) * piece)
        first = c % 2 * 2
        whole = total[c] + jnp.concatenate([res[first, :, at], res[first + 1, :, at]], axis=1).astype(F32)
        for d in range(planes - 1):
            whole = whole + mix_recv[c, d].astype(F32)
        total[c] = whole
        added = whole[:, :piece] * whole[:, :piece] + whole[:, piece:] * whole[:, piece:]
        squares[...] = added if c == 0 else squares[...] + added

    def finish_half(i):
        c = chunks - 1
        there = slice(i * piece, (i + 1) * piece)
        cols = columns(final + i)
        landing = mix_recv.at[c, three, :, cols]
        to_plane(landing, landing, mix_s, mix_r.at[c + i], x).wait_recv()
        whole = total[c, :, there] + res[c % 2 * 2 + i, :, c // 2 * piece : (c // 2 + 1) * piece].astype(F32)
        for d in range(planes - 1):
            whole = whole + mix_recv[c, d, :, there].astype(F32)
        total[c, :, there] = whole
        squares[...] = squares[...] + whole * whole

    def chunk_ready(c):
        @pl.when(host)
        def _():
            chunk_arrived(2, c)
            chunk_arrived(3, c)

        @pl.when(guest)
        def _():
            chunk_arrived(0, c)
            chunk_arrived(1, c)

    def produce(j, h):
        there = slice(h * side_rows, (h + 1) * side_rows)
        product = dot(acts[0, there], downs[0, j])
        for q in range(1, planes):
            product = product + dot(acts[q, there], downs[q, j])
        block = product.astype(BF).reshape(side, slots, 2 * piece)
        back_send[j // 2, h * side : (h + 1) * side, j % 2] = block
        if h == 0:
            back_recv[j // 2, me, j % 2] = block[0]

    def send_back(g, h):
        @pl.loop(1 - h, side)
        def _(k):
            back_copy(g, k + h * side, me, peer_at(peers - 2 * k - h)).start()

    pass_down(0)
    chunk_ready(0)
    produce(0, 0)
    send_back(0, 0)
    take_rows(1)
    for q in range(planes):
        activate(q, 1)
    pass_down(1)
    produce(0, 1)
    send_back(0, 1)
    for c in range(1, chunks):
        if 1 < c < chunks - 1:
            pass_down(c + 1)
        chunk_ready(c)
        g = group_of[c]
        last = groups[g][-1] == c
        for h in range(2):
            produce(c, h)
            if last:
                send_back(g, h)
        if c == chunks - 1:
            for h in range(2):
                send_back(g + 1, h)
        if c == 1:
            pass_down(2)
        if c >= 4:
            combine(c - 4)
        if c >= 5:
            finish(c - 5)

    to_peer(ask_recv.at[everyone], ask_recv.at[everyone], ask_s, ask_r, me).wait_recv()
    ask_recv[me] = ask_send[...]
    asked = ask_recv[...].reshape(peers * 8, rows)
    lanes = iota((peers * 8, rows), 1)
    ours = asked // rows == me
    first = jnp.min(jnp.where(ours, lanes, rows), axis=1, keepdims=True)
    second = jnp.max(jnp.where(ours, lanes, -1), axis=1, keepdims=True)
    line = iota((peers * 8, 1), 0) % 8
    request = jnp.where(line < 4, first, second)
    local = jnp.sum(jnp.where(lanes == request, asked % rows, 0), axis=1, keepdims=True)
    for c in range(planes):
        chooser = (lanes == local) & (line % 4 == c)
        pack_pick[c] = jnp.where(chooser, 1.0, 0.0).astype(BF)

    asks = jnp.broadcast_to(source_ref[...], (rows, rows))
    asks_down = jnp.transpose(asks.astype(F32)).astype(jnp.int32)
    same = (asks // rows == asks_down // rows) & (iota((rows, rows), 1) < iota((rows, rows), 0))
    later = jnp.max(jnp.where(same, 1, 0), axis=1, keepdims=True)
    place = (asks_down[:, 0:1] // rows) * 8 + later * 4
    at = iota((rows, peers * 8), 1)
    for c in range(planes):
        out_pick[c] = jnp.where(at == place + c, 1.0, 0.0).astype(BF)

    for c in range(chunks - 4, chunks - 1):
        combine(c)
        finish(c - 1)
    combine_half(0)
    finish(chunks - 2)
    combine_half(1)
    finish_half(0)
    finish_half(1)
    square = jnp.sum(squares[...], axis=1, keepdims=True)
    scale = lax.rsqrt(square / width + epsilon)
    packed = jnp.zeros((peers * 8, piece), F32)
    own_half = pl.ds(pl.multiple_of(lax.rem(x, 2) * piece, piece), piece)
    for c in range(planes):
        gain = last_gain_ref[c * piece : (c + 1) * piece].astype(F32).reshape(1, piece)
        result = (total[2 * c + active, :, own_half] * scale * gain).astype(BF)
        packed = packed + dot(pack_pick[c], result)
    pack_send[...] = packed.astype(BF).reshape(peers, 8, piece)
    pack_recv[me] = pack_send[me]

    def send_pack(step):
        peer = peer_at(step)
        to_peer(pack_send.at[peer], pack_recv.at[me], pack_s, pack_r, peer).start()

    send_pack(side)

    @pl.loop(1, side)
    def _(k):
        send_pack(side - k)
        send_pack(side + k)

    att = far + near + spread_res + res_on
    for copy in sum(att, []):
        copy.wait_send()

    @pl.when(host)
    def _():
        for kind in range(3):
            for u in range(unit_count):
                own_unit(u, 0, kind, x, me).wait_send()
            for c in range(chunks):
                chunk_copy(c, stage, 0, kind, x, me).wait_send()

    @pl.when(guest)
    def _():
        for kind in range(4):
            for u in range(unit_count):
                own_unit(u, 0, kind, x, me).wait_send()
            for c in range(chunks):
                chunk_copy(c, stage, 0, kind, x, me).wait_send()

    @pl.loop(1, peers)
    def _(step):
        to_peer(ask_send, ask_recv.at[me], ask_s, ask_r, me).wait_send()

    to_peer(slot_send.at[everyone], slot_recv.at[everyone], slot_s, slot_r, me).wait_send()
    for g in range(len(groups)):
        back_copy(g, everyone, everyone, me).wait_send()
    for d in range(1, planes):
        for c in range(chunks - 1):
            mix_copy(c, d).wait_send()
        for i in range(2):
            mix_copy(chunks - 1, d, columns(final + i), chunks - 1 + i).wait_send()
    to_peer(pack_send.at[everyone], pack_recv.at[everyone], pack_s, pack_r, me).wait_recv()
    landed = pack_recv[...].reshape(peers * 8, 128)
    outs = []
    for c in range(planes):
        cols = pl.ds(c * piece, piece)
        out_block[:, c * piece : (c + 1) * piece] = dot(out_pick[c], landed).astype(BF)
        outs.append(pltpu.make_async_copy(out_block.at[:, cols], out_ref.at[:, cols], in_sem.at[c]))
        outs[c].start()
    for copy in outs:
        copy.wait()

    to_peer(pack_send.at[everyone], pack_recv.at[everyone], pack_s, pack_r, me).wait_send()


def solution(mesh):
    planes, peers = mesh.shape["tensor"], mesh.shape["expert"]

    def on_device(
        attn_out,
        out_proj,
        hidden_in,
        norm_gain,
        router,
        routes,
        w_gate,
        w_up,
        w_down,
        final_gain,
        source,
    ):
        rows, width = hidden_in.shape
        share = width // planes
        top = routes.shape[1]
        slots = min(rows, 2 * rows * top // peers) // planes
        units = w_gate.shape[2]
        remote = pl.BlockSpec(memory_space=pl.ANY)
        return pl.pallas_call(
            functools.partial(layer, planes, peers),
            out_shape=jax.ShapeDtypeStruct((rows, share), BF),
            in_specs=[remote] * 11,
            out_specs=remote,
            scratch_shapes=[
                VMEM((rows, share), BF),
                VMEM((share, width), BF),
                VMEM((rows, width), BF),
                VMEM((peers, width), BF),
                VMEM((top, rows), jnp.int32),
                VMEM((width,), BF),
                VMEM((share,), BF),
                VMEM((1, rows), jnp.int32),
                VMEM((planes, rows, share), F32),
                VMEM((2, rows, share // 2), BF),
                VMEM((2, 2, rows // 2, share // 2), BF),
                VMEM((2, 2, rows, share // 2), BF),
                VMEM((2, 2, rows, share // 2), BF),
                VMEM((planes, rows, share), BF),
                VMEM((planes, rows, share), BF),
                VMEM((planes, width, units), BF),
                VMEM((planes, width, units), BF),
                VMEM((planes, 2 * planes, units, share // 2), BF),
                VMEM((2 * planes, units, share // 2), BF),
                VMEM((8, rows), jnp.int32),
                VMEM((peers, 8, rows), jnp.int32),
                VMEM((peers, slots, width), BF),
                VMEM((peers, slots, width), BF),
                VMEM((peers * slots, width), BF),
                VMEM((planes, peers * slots, units), BF),
                VMEM((planes, peers, 2, slots, share // 2), BF),
                VMEM((planes, peers, 2, slots, share // 2), BF),
                VMEM((2 * planes, rows, share // 2), BF),
                VMEM((2 * planes, planes - 1, rows, share // 2), BF),
                VMEM((2 * planes, rows, share // 2), F32),
                VMEM((rows, share // planes), F32),
                VMEM((peers * slots, rows), BF),
                VMEM((rows, peers * slots), BF),
                VMEM((planes, peers * 8, rows), BF),
                VMEM((planes, rows, peers * 8), BF),
                VMEM((rows, share), BF),
                VMEM((peers, 8, 128), BF),
                VMEM((peers, 8, 128), BF),
                VMEM((rows, peers * slots), BF),
                VMEM((rows, peers * slots), BF),
                DMA((7 + planes,)),
                DMA((3 + 4 * planes,)),
                DMA((2, 4)),
                DMA((2, 4)),
                DMA((2, 4)),
                DMA((2, 4)),
                DMA,
                DMA,
                DMA,
                DMA((2,)),
                DMA,
                DMA((4, 8)),
                DMA,
                DMA((4, 2 * planes)),
                DMA((2 * planes,)),
                DMA((2 * planes,)),
                DMA,
                DMA((2 * planes + 1,)),
                DMA,
                DMA,
            ],
            compiler_params=pltpu.CompilerParams(
                collective_id=0, has_side_effects=True, vmem_limit_bytes=56 * 1024 * 1024
            ),
        )(
            attn_out,
            out_proj,
            hidden_in,
            norm_gain,
            router.T,
            routes.T,
            w_gate,
            w_up,
            w_down,
            final_gain,
            source.reshape(1, rows),
        )

    placed = (
        P("expert", "tensor"),
        P("tensor", None),
        P("expert", None),
        P(),
        P(),
        P("expert", None),
        P("expert", None, "tensor"),
        P("expert", None, "tensor"),
        P("expert", "tensor", None),
        P("tensor"),
        P("expert"),
    )
    return jax.shard_map(
        on_device, mesh=mesh, in_specs=placed, out_specs=P("expert", "tensor"), check_vma=False
    )
```

```python
import functools

import jax
import jax.numpy as jnp
from jax import lax
from jax.experimental import pallas as pl
from jax.experimental.pallas import tpu as pltpu
from jax.sharding import PartitionSpec as P

epsilon = 1e-06
BF = jnp.bfloat16
F32 = jnp.float32
VMEM = pltpu.VMEM
DMA = pltpu.SemaphoreType.DMA


def dot(a, b):
    return jnp.dot(a, b, preferred_element_type=F32)


def iota(shape, dim):
    return lax.broadcasted_iota(jnp.int32, shape, dim)


def layer(
    planes,
    peers,
    attn_hbm,
    proj_hbm,
    hidden_hbm,
    gain_hbm,
    router_hbm,
    routes_hbm,
    gate_hbm,
    up_hbm,
    down_hbm,
    last_gain_hbm,
    source_hbm,
    out_ref,
    attn_ref,
    proj_ref,
    hidden_ref,
    router_ref,
    routes_ref,
    gain_ref,
    last_gain_ref,
    source_ref,
    part,
    far_send,
    far_recv,
    near_send,
    near_recv,
    res,
    normed,
    gates,
    ups,
    downs,
    stage,
    ask_send,
    ask_recv,
    slot_send,
    slot_recv,
    rows_in,
    acts,
    back_send,
    back_recv,
    mix_send,
    mix_recv,
    total,
    squares,
    pick_ref,
    taken_ref,
    pack_pick,
    out_pick,
    out_block,
    pack_send,
    pack_recv,
    high,
    low,
    in_sem,
    own_sem,
    att_s,
    att_r,
    res_s,
    res_r,
    ask_s,
    ask_r,
    slot_s,
    slot_r,
    w_s,
    w_r,
    d_s,
    d_r,
    back_s,
    back_r,
    mix_s,
    mix_r,
    pack_s,
    pack_r,
):
    x = lax.axis_index("tensor")
    me = lax.axis_index("expert")
    rows, share = attn_hbm.shape
    width = planes * share
    slots = slot_send.shape[1]
    all_slots = peers * slots
    hidden_units = gate_hbm.shape[2]
    right = lax.rem(x + 1, planes)
    left = lax.rem(x + planes - 1, planes)
    active = x // 2
    host = lax.rem(me, 2) == active
    guest = jnp.logical_not(host)
    partner = x + 1 - 2 * lax.rem(x, 2)
    outer = planes - 1 - x
    sibling = me + 1 - 2 * lax.rem(me, 2)

    def to_plane(src, dst, send, recv, plane):
        return pltpu.make_async_remote_copy(
            src_ref=src, dst_ref=dst, send_sem=send, recv_sem=recv, device_id={"tensor": plane}
        )

    def to_device(src, dst, send, recv, plane, peer):
        return pltpu.make_async_remote_copy(
            src_ref=src,
            dst_ref=dst,
            send_sem=send,
            recv_sem=recv,
            device_id={"tensor": plane, "expert": peer},
        )

    def to_peer(src, dst, send, recv, peer):
        return pltpu.make_async_remote_copy(
            src_ref=src, dst_ref=dst, send_sem=send, recv_sem=recv, device_id={"expert": peer}
        )

    def peer_at(step):
        return lax.rem(me + step, peers)

    barrier = pltpu.get_barrier_semaphore()
    for d in range(1, planes):
        pl.semaphore_signal(barrier, inc=1, device_id={"tensor": lax.rem(x + d, planes)})
    pl.semaphore_signal(barrier, inc=1, device_id={"tensor": outer, "expert": sibling})

    @pl.loop(1, peers)
    def _(step):
        pl.semaphore_signal(barrier, inc=1, device_id={"expert": peer_at(step)})

    inputs = [
        pltpu.make_async_copy(src, dst, in_sem.at[i])
        for i, (src, dst) in enumerate(
            [
                (attn_hbm, attn_ref),
                (source_hbm, source_ref),
                (hidden_hbm, hidden_ref),
                (router_hbm, router_ref),
                (routes_hbm, routes_ref),
                (gain_hbm, gain_ref),
                (last_gain_hbm, last_gain_ref),
            ]
        )
    ]
    proj_cols = [
        pl.ds(pl.multiple_of(lax.rem(x + d, planes) * share, share), share) for d in (2, 1, 3, 0)
    ]
    proj_in = [
        pltpu.make_async_copy(proj_hbm.at[:, cols], proj_ref.at[:, cols], in_sem.at[7 + i])
        for i, cols in enumerate(proj_cols)
    ]
    inputs[0].start()
    for copy in proj_in + inputs[1:]:
        copy.start()

    piece = share // planes
    chunks = 2 * planes
    own = [
        pltpu.make_async_copy(gate_hbm.at[0], gates.at[0], own_sem.at[0]),
        pltpu.make_async_copy(up_hbm.at[0], ups.at[0], own_sem.at[1]),
    ]

    def own_down(c, buffer):
        copies = []
        for i in range(2):
            first = (c % 2 * 2 + i) * share + c // 2 * piece
            copies.append(
                pltpu.make_async_copy(
                    down_hbm.at[0, :, pl.ds(first, piece)],
                    buffer.at[c, :, pl.ds(i * piece, piece)],
                    own_sem.at[2 + 2 * c + i],
                )
            )
        return copies

    @pl.when(host)
    def _():
        for copy in own:
            copy.start()
        for c in range(chunks):
            for copy in own_down(c, downs.at[0]):
                copy.start()

    @pl.when(guest)
    def _():
        for c in range(chunks):
            for copy in own_down(c, stage):
                copy.start()

    inputs[0].wait()
    proj_in[0].wait()
    far_part = dot(attn_ref[...], proj_ref[:, proj_cols[0]])
    top, bottom = pl.ds(0, rows // 2), pl.ds(rows // 2, rows // 2)
    wing = share // 2
    wings = [pl.ds(0, wing), pl.ds(wing, wing)]
    for h in range(2):
        far_send[h] = far_part[:, h * wing : (h + 1) * wing].astype(BF)

    pl.semaphore_wait(barrier, planes - 1 + 1 + peers - 1)

    far = [
        [
            to_plane(far_send.at[h, top], far_recv.at[h, 0], att_s.at[h, 0], att_r.at[h, 0], right),
            to_plane(
                far_send.at[h, bottom], far_recv.at[h, 1], att_s.at[h, 1], att_r.at[h, 1], left
            ),
        ]
        for h in range(2)
    ]
    for copy in far[0] + far[1]:
        copy.start()
    for d, copy, cols in zip((1, 3, 0), proj_in[1:], proj_cols[1:]):
        copy.wait()
        part[lax.rem(x + d, planes)] = dot(attn_ref[...], proj_ref[:, cols])
    inputs[1].wait()
    ask_send[...] = jnp.broadcast_to(source_ref[...], ask_send.shape)

    middle = width // 4
    units_of = [(gates, gate_hbm, first) for first in range(0, width, middle)]
    units_of += [(ups, up_hbm, first) for first in range(0, width, middle)]
    unit_count = len(units_of)

    def unit_view(slot, u):
        buffer, _, first = units_of[u]
        return buffer.at[slot, pl.ds(first, middle)]

    def own_unit(u, slot, kind, plane, peer, first=0, count=middle):
        buffer, hbm, base = units_of[u]
        return to_device(
            hbm.at[0, pl.ds(base + first, count)],
            buffer.at[slot, pl.ds(base + first, count)],
            w_s,
            w_r.at[slot, u],
            plane,
            peer,
        )

    def onward_unit(u, slot, there, kind, plane, peer):
        return to_device(
            unit_view(slot, u), unit_view(there, u), w_s, w_r.at[there, u], plane, peer
        )

    def unit_arrived(slot, u):
        own_unit(u, slot, 0, x, me).wait_recv()

    def send_rows(phase):
        def spans(marks):
            marks = (0,) + marks + (unit_count * middle,)
            first, last = marks[phase], marks[phase + 1]
            while first < last:
                count = min(last, first // middle * middle + middle) - first
                yield first // middle, first % middle, count
                first += count

        @pl.when(host)
        def _():
            for u, first, count in spans((256, 512, 768)):
                own_unit(u, 1, 0, partner, me, first, count).start()

        @pl.when(guest)
        def _():
            for u, first, count in spans((256, 512, 768)):
                own_unit(u, 2, 0, outer, sibling, first, count).start()

    send_rows(0)

    near = []
    for h in range(2):
        for copy in far[h]:
            copy.wait_recv()
        wing_at = wings[h]
        near_send[h, 0] = part[right, :, wing_at].astype(BF)
        near_send[h, 1] = part[left, :, wing_at].astype(BF)
        near_send[h, 0, top] = (part[right, top, wing_at] + far_recv[h, 0].astype(F32)).astype(BF)
        near_send[h, 1, bottom] = (part[left, bottom, wing_at] + far_recv[h, 1].astype(F32)).astype(BF)
        near.append(
            [
                to_plane(
                    near_send.at[h, 0], near_recv.at[h, 0], att_s.at[h, 2], att_r.at[h, 2], right
                ),
                to_plane(
                    near_send.at[h, 1], near_recv.at[h, 1], att_s.at[h, 3], att_r.at[h, 3], left
                ),
            ]
        )
        for copy in near[h]:
            copy.start()
    send_rows(1)

    @pl.loop(1, peers)
    def _(step):
        to_peer(ask_send, ask_recv.at[me], ask_s, ask_r, peer_at(step)).start()

    for copy in inputs[2:7]:
        copy.wait()

    experts = peers
    named = jnp.zeros((rows, experts), jnp.bool_)
    which = iota((rows, experts), 1)
    routed = jnp.transpose(routes_ref[...].astype(F32)).astype(jnp.int32)
    for k in range(routed.shape[1]):
        named = named | (routed[:, k : k + 1] == which)
    named_f = jnp.where(named, 1.0, 0.0).astype(F32)
    before = jnp.where(iota((rows, rows), 1) < iota((rows, rows), 0), 1.0, 0.0).astype(BF)
    rank = dot(before, named_f.astype(BF))
    wide = jnp.where(
        iota((experts, all_slots), 1) // (2 * slots) * 2 + active == iota((experts, all_slots), 0),
        1.0,
        0.0,
    ).astype(BF)
    wide_rank = dot(rank.astype(BF), wide)
    wide_named = dot(named_f.astype(BF), wide)
    turn = (iota((rows, all_slots), 1) % (2 * slots) + lax.rem(x, 2) * 2 * slots).astype(F32)
    taken_f = jnp.where((wide_named > 0.5) & (wide_rank == turn), 1.0, 0.0).astype(F32)
    taken_ref[...] = taken_f.astype(BF)
    pick_ref[...] = jnp.transpose(taken_f).astype(BF)

    spread_res, res_on = [], []
    for h in range(2):
        for copy in near[h]:
            copy.wait_recv()
        mine = pl.ds(pl.multiple_of(x * share + h * wing, wing), wing)
        attention = part[x, :, wings[h]] + near_recv[h, 0].astype(F32) + near_recv[h, 1].astype(F32)
        res[x, :, wings[h]] = (hidden_ref[:, mine].astype(F32) + attention).astype(BF)
        ours = res.at[x, :, wings[h]]
        spread_res.append(
            [
                to_plane(ours, ours, res_s.at[h, 0], res_r.at[h, 0], right),
                to_plane(ours, ours, res_s.at[h, 1], res_r.at[h, 1], left),
            ]
        )
        for copy in spread_res[h]:
            copy.start()
    send_rows(2)
    for h in range(2):
        from_left, from_right = res.at[left, top, wings[h]], res.at[right, bottom, wings[h]]
        res_on.append(
            [
                to_plane(from_left, from_left, res_s.at[h, 2], res_r.at[h, 2], right),
                to_plane(from_right, from_right, res_s.at[h, 3], res_r.at[h, 3], left),
            ]
        )
        for copy, onward in zip(spread_res[h], res_on[h]):
            copy.wait_recv()
            onward.start()
    send_rows(3)

    @pl.when(host)
    def _():
        for u in range(unit_count):
            own_unit(u, 0, 1, x, sibling).start()


    for copy in res_on[0] + res_on[1]:
        copy.wait_recv()
    square = jnp.zeros((rows, 1), F32)
    for j in range(planes):
        floats = res[j].astype(F32)
        square = square + jnp.sum(floats * floats, axis=1, keepdims=True)
    inverse = lax.rsqrt(square / width + epsilon)
    for j in range(planes):
        cols = slice(j * share, (j + 1) * share)
        gain = gain_ref[cols].astype(F32).reshape(1, share)
        normed[j] = (res[j].astype(F32) * inverse * gain).astype(BF)
    pick = pick_ref[...]
    for j in range(planes):
        chosen = dot(pick, normed[j]).astype(BF)
        slot_send[:, :, j * share : (j + 1) * share] = chosen.reshape(peers, slots, share)

    side = peers // 2
    for h in range(2):

        @pl.loop(1 - h, side)
        def _(k):
            peer = peer_at(2 * k + h)
            to_peer(
                slot_send.at[peer], slot_recv.at[k + h * side], slot_s, slot_r.at[h], peer
            ).start()

    own_slot = pltpu.make_async_copy(slot_send.at[me], slot_recv.at[0], own_sem.at[2 + 2 * chunks])
    own_slot.start()

    logits = jnp.zeros((rows, experts), F32)
    for j in range(planes):
        cols = slice(j * share, (j + 1) * share)
        logits = logits + lax.dot_general(
            normed[j], router_ref[:, cols], (((1,), (1,)), ((), ())), preferred_element_type=F32
        )
    powers = jnp.where(named, jnp.exp(logits), 0.0)
    weights = powers / jnp.sum(powers, axis=1, keepdims=True)
    weights_high = weights.astype(BF)
    weights_low = (weights - weights_high.astype(F32)).astype(BF)
    taken = taken_ref[...].astype(F32) > 0.5
    high[...] = jnp.where(taken, dot(weights_high, wide), 0.0).astype(BF)
    low[...] = jnp.where(taken, dot(weights_low, wide), 0.0).astype(BF)

    def chunk_copy(c, source, slot, kind, plane, peer):
        return to_device(
            source.at[c], downs.at[slot, c], d_s, d_r.at[slot, c], plane, peer
        )

    def chunk_arrived(slot, c):
        chunk_copy(c, stage, slot, 0, x, me).wait_recv()

    @pl.when(host)
    def _():
        for c in range(chunks):
            for copy in own_down(c, downs.at[0]):
                copy.wait()
            chunk_copy(c, downs.at[0], 0, 1, x, sibling).start()
        for u in range(unit_count):
            unit_arrived(1, u)
            onward_unit(u, 1, 1, 2, x, sibling).start()
        for c in range(1):
            chunk_copy(c, downs.at[0], 1, 0, partner, me).start()

    @pl.when(guest)
    def _():
        for c in range(chunks):
            for copy in own_down(c, stage):
                copy.wait()
            chunk_copy(c, stage, 2, 0, outer, sibling).start()
        for u in range(unit_count):
            unit_arrived(2, u)
            onward_unit(u, 2, 3, 1, partner, me).start()
            onward_unit(u, 2, 2, 2, x, sibling).start()
        for c in range(chunks):
            chunk_arrived(2, c)
            chunk_copy(c, downs.at[2], 3, 1, partner, me).start()
            chunk_copy(c, downs.at[2], 2, 2, x, sibling).start()
    def pass_down(c):
        @pl.when(host)
        def _():
            chunk_arrived(1, c)
            chunk_copy(c, downs.at[1], 1, 2, x, sibling).start()

        @pl.when(guest)
        def _():
            chunk_arrived(3, c)
            chunk_copy(c, downs.at[3], 3, 3, x, sibling).start()

    everyone = pl.ds(0, peers - 1)
    side_rows = side * slots

    def take_rows(h):
        count = pl.ds(0, side - 1 if h == 0 else side)
        to_peer(slot_send.at[count], slot_recv.at[count], slot_s, slot_r.at[h], me).wait_recv()
        half_side = side // 2
        for t in range(2):
            first = h * side + t * half_side
            rows_in[first * slots : (first + half_side) * slots] = slot_recv[
                first : first + half_side
            ].reshape(half_side * slots, width)

    def activate(q, h):
        there = slice(h * side_rows, (h + 1) * side_rows)
        gate_part = dot(rows_in[there], gates[q])
        up_part = dot(rows_in[there], ups[q])
        acts[q, there] = (gate_part / (1.0 + jnp.exp(-gate_part)) * up_part).astype(BF)

    own_slot.wait()
    take_rows(0)

    @pl.when(host)
    def _():
        for copy in own:
            copy.wait()

    @pl.when(guest)
    def _():
        for u in range(unit_count):
            unit_arrived(0, u)

    activate(0, 0)

    @pl.when(host)
    def _():
        for u in range(unit_count):
            unit_arrived(2, u)

    activate(2, 0)

    @pl.when(guest)
    def _():
        for u in range(unit_count):
            unit_arrived(1, u)

    activate(1, 0)

    @pl.when(host)
    def _():
        for u in range(unit_count):
            unit_arrived(3, u)
        for c in range(1, chunks):
            chunk_copy(c, downs.at[0], 1, 0, partner, me).start()

    @pl.when(guest)
    def _():
        for u in range(unit_count):
            unit_arrived(3, u)
            onward_unit(u, 3, 3, 3, x, sibling).start()

    activate(3, 0)

    groups = [[0], [1]] + [[c, c + 1] for c in range(2, chunks - 2, 2)] + [[chunks - 2]]
    groups += [[chunks - 1], [chunks - 1]]
    final = len(groups) - 2
    group_of = {c: g for g, group in enumerate(groups[:-1]) for c in group}
    both = pl.ds(0, 2 * piece)

    def columns(g):
        return pl.ds((g - final) * piece, piece) if g >= final else both

    def back_copy(g, here, there, peer):
        first = groups[g][0]
        pair, at = first // 2, first % 2
        if len(groups[g]) == 1:
            src = back_send.at[pair, here, at, :, columns(g)]
            dst = back_recv.at[pair, there, at, :, columns(g)]
        else:
            src, dst = back_send.at[pair, here], back_recv.at[pair, there]
        return to_peer(src, dst, back_s.at[g], back_r.at[g], peer)

    def mix_copy(c, d, cols=both, sem=None):
        sem = c if sem is None else sem
        return to_plane(
            mix_send.at[c, :, cols],
            mix_recv.at[c, d - 1, :, cols],
            mix_s,
            mix_r.at[sem],
            lax.rem(x + d, planes),
        )

    def combine(c):
        if groups[group_of[c]][0] == c:
            back_copy(group_of[c], everyone, everyone, me).wait_recv()
        back = back_recv[c // 2, :, c % 2].reshape(all_slots, 2 * piece)
        mixed = dot(high[...], back) + dot(low[...], back)
        mix_send[c] = mixed.astype(BF)
        total[c] = mixed
        for d in range(1, planes):
            mix_copy(c, d).start()

    def combine_half(i):
        c = chunks - 1
        back_copy(final + i, everyone, everyone, me).wait_recv()
        there = slice(i * piece, (i + 1) * piece)
        back = back_recv[c // 2, :, c % 2, :, there].reshape(all_slots, piece)
        mixed = dot(high[...], back) + dot(low[...], back)
        mix_send[c, :, there] = mixed.astype(BF)
        total[c, :, there] = mixed
        for d in range(1, planes):
            mix_copy(c, d, columns(final + i), c + i).start()

    three = pl.ds(0, planes - 1)

    def finish(c):
        to_plane(mix_recv.at[c, three], mix_recv.at[c, three], mix_s, mix_r.at[c], x).wait_recv()
        at = slice(c // 2 * piece, (c // 2 + 1) * piece)
        first = c % 2 * 2
        whole = total[c] + jnp.concatenate([res[first, :, at], res[first + 1, :, at]], axis=1).astype(F32)
        for d in range(planes - 1):
            whole = whole + mix_recv[c, d].astype(F32)
        total[c] = whole
        added = whole[:, :piece] * whole[:, :piece] + whole[:, piece:] * whole[:, piece:]
        squares[...] = added if c == 0 else squares[...] + added

    def finish_half(i):
        c = chunks - 1
        there = slice(i * piece, (i + 1) * piece)
        cols = columns(final + i)
        landing = mix_recv.at[c, three, :, cols]
        to_plane(landing, landing, mix_s, mix_r.at[c + i], x).wait_recv()
        whole = total[c, :, there] + res[c % 2 * 2 + i, :, c // 2 * piece : (c // 2 + 1) * piece].astype(F32)
        for d in range(planes - 1):
            whole = whole + mix_recv[c, d, :, there].astype(F32)
        total[c, :, there] = whole
        squares[...] = squares[...] + whole * whole

    def chunk_ready(c):
        @pl.when(host)
        def _():
            chunk_arrived(2, c)
            chunk_arrived(3, c)

        @pl.when(guest)
        def _():
            chunk_arrived(0, c)
            chunk_arrived(1, c)

    def produce(j, h):
        there = slice(h * side_rows, (h + 1) * side_rows)
        product = dot(acts[0, there], downs[0, j])
        for q in range(1, planes):
            product = product + dot(acts[q, there], downs[q, j])
        block = product.astype(BF).reshape(side, slots, 2 * piece)
        back_send[j // 2, h * side : (h + 1) * side, j % 2] = block
        if h == 0:
            back_recv[j // 2, me, j % 2] = block[0]

    def send_back(g, h):
        @pl.loop(1 - h, side)
        def _(k):
            back_copy(g, k + h * side, me, peer_at(peers - 2 * k - h)).start()

    pass_down(0)
    chunk_ready(0)
    produce(0, 0)
    send_back(0, 0)
    take_rows(1)
    for q in range(planes):
        activate(q, 1)
    pass_down(1)
    produce(0, 1)
    send_back(0, 1)
    for c in range(1, chunks):
        if 1 < c < chunks - 1:
            pass_down(c + 1)
        chunk_ready(c)
        g = group_of[c]
        last = groups[g][-1] == c
        for h in range(2):
            produce(c, h)
            if last:
                send_back(g, h)
        if c == chunks - 1:
            for h in range(2):
                send_back(g + 1, h)
        if c == 1:
            pass_down(2)
        if c >= 4:
            combine(c - 4)
        if c >= 5:
            finish(c - 5)

    to_peer(ask_recv.at[everyone], ask_recv.at[everyone], ask_s, ask_r, me).wait_recv()
    ask_recv[me] = ask_send[...]
    asked = ask_recv[...].reshape(peers * 8, rows)
    lanes = iota((peers * 8, rows), 1)
    ours = asked // rows == me
    first = jnp.min(jnp.where(ours, lanes, rows), axis=1, keepdims=True)
    second = jnp.max(jnp.where(ours, lanes, -1), axis=1, keepdims=True)
    line = iota((peers * 8, 1), 0) % 8
    request = jnp.where(line < 4, first, second)
    local = jnp.sum(jnp.where(lanes == request, asked % rows, 0), axis=1, keepdims=True)
    for c in range(planes):
        chooser = (lanes == local) & (line % 4 == c)
        pack_pick[c] = jnp.where(chooser, 1.0, 0.0).astype(BF)

    asks = jnp.broadcast_to(source_ref[...], (rows, rows))
    asks_down = jnp.transpose(asks.astype(F32)).astype(jnp.int32)
    same = (asks // rows == asks_down // rows) & (iota((rows, rows), 1) < iota((rows, rows), 0))
    later = jnp.max(jnp.where(same, 1, 0), axis=1, keepdims=True)
    place = (asks_down[:, 0:1] // rows) * 8 + later * 4
    at = iota((rows, peers * 8), 1)
    for c in range(planes):
        out_pick[c] = jnp.where(at == place + c, 1.0, 0.0).astype(BF)

    for c in range(chunks - 4, chunks - 1):
        combine(c)
        finish(c - 1)
    combine_half(0)
    finish(chunks - 2)
    combine_half(1)
    finish_half(0)
    finish_half(1)
    square = jnp.sum(squares[...], axis=1, keepdims=True)
    scale = lax.rsqrt(square / width + epsilon)
    packed = jnp.zeros((peers * 8, piece), F32)
    own_half = pl.ds(pl.multiple_of(lax.rem(x, 2) * piece, piece), piece)
    for c in range(planes):
        gain = last_gain_ref[c * piece : (c + 1) * piece].astype(F32).reshape(1, piece)
        result = (total[2 * c + active, :, own_half] * scale * gain).astype(BF)
        packed = packed + dot(pack_pick[c], result)
    pack_send[...] = packed.astype(BF).reshape(peers, 8, piece)
    pack_recv[me] = pack_send[me]

    def send_pack(step):
        peer = peer_at(step)
        to_peer(pack_send.at[peer], pack_recv.at[me], pack_s, pack_r, peer).start()

    send_pack(side)

    @pl.loop(1, side)
    def _(k):
        send_pack(side - k)
        send_pack(side + k)

    att = far + near + spread_res + res_on
    for copy in sum(att, []):
        copy.wait_send()

    @pl.when(host)
    def _():
        for kind in range(3):
            for u in range(unit_count):
                own_unit(u, 0, kind, x, me).wait_send()
            for c in range(chunks):
                chunk_copy(c, stage, 0, kind, x, me).wait_send()

    @pl.when(guest)
    def _():
        for kind in range(4):
            for u in range(unit_count):
                own_unit(u, 0, kind, x, me).wait_send()
            for c in range(chunks):
                chunk_copy(c, stage, 0, kind, x, me).wait_send()

    @pl.loop(1, peers)
    def _(step):
        to_peer(ask_send, ask_recv.at[me], ask_s, ask_r, me).wait_send()

    to_peer(slot_send.at[everyone], slot_recv.at[everyone], slot_s, slot_r, me).wait_send()
    for g in range(len(groups)):
        back_copy(g, everyone, everyone, me).wait_send()
    for d in range(1, planes):
        for c in range(chunks - 1):
            mix_copy(c, d).wait_send()
        for i in range(2):
            mix_copy(chunks - 1, d, columns(final + i), chunks - 1 + i).wait_send()
    to_peer(pack_send.at[everyone], pack_recv.at[everyone], pack_s, pack_r, me).wait_recv()
    landed = pack_recv[...].reshape(peers * 8, 128)
    outs = []
    for c in range(planes):
        cols = pl.ds(c * piece, piece)
        out_block[:, c * piece : (c + 1) * piece] = dot(out_pick[c], landed).astype(BF)
        outs.append(pltpu.make_async_copy(out_block.at[:, cols], out_ref.at[:, cols], in_sem.at[c]))
        outs[c].start()
    for copy in outs:
        copy.wait()

    to_peer(pack_send.at[everyone], pack_recv.at[everyone], pack_s, pack_r, me).wait_send()


def solution(mesh):
    planes, peers = mesh.shape["tensor"], mesh.shape["expert"]

    def on_device(
        attn_out,
        out_proj,
        hidden_in,
        norm_gain,
        router,
        routes,
        w_gate,
        w_up,
        w_down,
        final_gain,
        source,
    ):
        rows, width = hidden_in.shape
        share = width // planes
        top = routes.shape[1]
        slots = min(rows, 2 * rows * top // peers) // planes
        units = w_gate.shape[2]
        remote = pl.BlockSpec(memory_space=pl.ANY)
        return pl.pallas_call(
            functools.partial(layer, planes, peers),
            out_shape=jax.ShapeDtypeStruct((rows, share), BF),
            in_specs=[remote] * 11,
            out_specs=remote,
            scratch_shapes=[
                VMEM((rows, share), BF),
                VMEM((share, width), BF),
                VMEM((rows, width), BF),
                VMEM((peers, width), BF),
                VMEM((top, rows), jnp.int32),
                VMEM((width,), BF),
                VMEM((share,), BF),
                VMEM((1, rows), jnp.int32),
                VMEM((planes, rows, share), F32),
                VMEM((2, rows, share // 2), BF),
                VMEM((2, 2, rows // 2, share // 2), BF),
                VMEM((2, 2, rows, share // 2), BF),
                VMEM((2, 2, rows, share // 2), BF),
                VMEM((planes, rows, share), BF),
                VMEM((planes, rows, share), BF),
                VMEM((planes, width, units), BF),
                VMEM((planes, width, units), BF),
                VMEM((planes, 2 * planes, units, share // 2), BF),
                VMEM((2 * planes, units, share // 2), BF),
                VMEM((8, rows), jnp.int32),
                VMEM((peers, 8, rows), jnp.int32),
                VMEM((peers, slots, width), BF),
                VMEM((peers, slots, width), BF),
                VMEM((peers * slots, width), BF),
                VMEM((planes, peers * slots, units), BF),
                VMEM((planes, peers, 2, slots, share // 2), BF),
                VMEM((planes, peers, 2, slots, share // 2), BF),
                VMEM((2 * planes, rows, share // 2), BF),
                VMEM((2 * planes, planes - 1, rows, share // 2), BF),
                VMEM((2 * planes, rows, share // 2), F32),
                VMEM((rows, share // planes), F32),
                VMEM((peers * slots, rows), BF),
                VMEM((rows, peers * slots), BF),
                VMEM((planes, peers * 8, rows), BF),
                VMEM((planes, rows, peers * 8), BF),
                VMEM((rows, share), BF),
                VMEM((peers, 8, 128), BF),
                VMEM((peers, 8, 128), BF),
                VMEM((rows, peers * slots), BF),
                VMEM((rows, peers * slots), BF),
                DMA((7 + planes,)),
                DMA((3 + 4 * planes,)),
                DMA((2, 4)),
                DMA((2, 4)),
                DMA((2, 4)),
                DMA((2, 4)),
                DMA,
                DMA,
                DMA,
                DMA((2,)),
                DMA,
                DMA((4, 8)),
                DMA,
                DMA((4, 2 * planes)),
                DMA((2 * planes,)),
                DMA((2 * planes,)),
                DMA,
                DMA((2 * planes + 1,)),
                DMA,
                DMA,
            ],
            compiler_params=pltpu.CompilerParams(
                collective_id=0, has_side_effects=True, vmem_limit_bytes=56 * 1024 * 1024
            ),
        )(
            attn_out,
            out_proj,
            hidden_in,
            norm_gain,
            router.T,
            routes.T,
            w_gate,
            w_up,
            w_down,
            final_gain,
            source.reshape(1, rows),
        )

    placed = (
        P("expert", "tensor"),
        P("tensor", None),
        P("expert", None),
        P(),
        P(),
        P("expert", None),
        P("expert", None, "tensor"),
        P("expert", None, "tensor"),
        P("expert", "tensor", None),
        P("tensor"),
        P("expert"),
    )
    return jax.shard_map(
        on_device, mesh=mesh, in_specs=placed, out_specs=P("expert", "tensor"), check_vma=False
    )
```
